32 devices in a mesh: page: 8 (over z, x), head: 4 (over y, core).
Axes of the slice: x: 2, y: 2, z: 4, core: 2. Of those that a mesh axis runs over, the one named last changes fastest.
Arguments:
- tokens: bfloat16 [2, 2, 4096, 768], P(None, None, ('page', 'head')), may hold values from -6 to 6
- spatial: bfloat16 [2, 2, 4096, 768], P(None, None, ('page', 'head')), may hold values from -6 to 6
- box_coords: int32 [2, 2, 2, 4096], P(None, None, None, 'page'), may hold values from 0 to 1023
- reading_order: int32 [2, 2, 4096], P(None, None, 'page'), may hold values from 0 to 127
- page_len: int32 [2, 8], P(None, 'page'), may hold values from 256 to 512, as said below
- w_attn: bfloat16 [2, 5, 768, 768], P(None, None, 'page', 'head'), may hold values from -0.21875 to 0.21875
- tables: bfloat16 [2, 3, 12, 128, 128], P(None, None, 'head', 'page'), may hold values from -3 to 3
- w_out: bfloat16 [2, 768, 768], P(None, 'head', 'page'), may hold values from -0.875 to 0.875
- ln_gain: bfloat16 [2, 768], P(None, ('page', 'head')), may hold values from 0.5 to 1.5
- ln_shift: bfloat16 [2, 768], P(None, ('page', 'head')), may hold values from -1.796875 to 1.796875
- w_up: bfloat16 [768, 3072], P(None, ('page', 'head')), may hold values from -0.21875 to 0.21875
- w_down: bfloat16 [3072, 768], P(('page', 'head')), may hold values from -0.109375 to 0.109375
- grad_out: bfloat16 [2, 4096, 768], P(None, ('page', 'head')), may hold values from -6 to 6
Outputs:
- out: bfloat16 [2, 4096, 768], P(None, ('page', 'head'))
- grad_tokens: bfloat16 [2, 2, 4096, 768], P(None, None, ('page', 'head'))
- grad_w_attn: float32 [2, 5, 768, 768], P(None, None, 'page', 'head')
- grad_tables: float32 [2, 3, 12, 128, 128], P(None, None, 'head', 'page')
- grad_w_out: float32 [2, 768, 768], P(None, 'head', 'page')
- grad_ln_gain: float32 [2, 768], P(None, ('page', 'head'))
- grad_ln_shift: float32 [2, 768], P(None, ('page', 'head'))
- grad_w_up: float32 [768, 3072], P(None, ('page', 'head'))
- grad_w_down: float32 [3072, 768], P(('page', 'head'))
The draws below stay inside these ranges and needn't reach their ends.
Inputs may be any that keep to these rules, and one draw needn't show every extreme that they name: `page_len`: each entry is 512 (a slot with one page) or 512 / 2 (a slot with two pages); both values occur in every draw.
All inputs are finite; a program needn't handle non-finite values.
Results may differ from the reference program's by a relative error of at most 0.02.
Values may be sent and summed in bfloat16 or wider, within the bound.
No kernel may reach another device: no remote copies, remote signals or barrier semaphores. Data moves between devices by JAX's collectives and lax.ppermute only.
A program may use at most 192 MiB of HBM per device.

```python
import math
import jax
import jax.numpy as jnp
from jax import lax

D = 768
FF = 3072
NHEAD = 12
HDIM = 64
NB = 128
COORD = 1024
SLOT = 512
MB = 2
SLOTS_ALL = 8
TOK_MB = 4096


def draw_page_len(key, part):
    chosen = jax.random.randint(key, (MB, SLOTS_ALL), 0, 2)
    lengths = (chosen + 1) * (SLOT // 2)
    lengths = lengths.at[0, 0].set(SLOT)
    lengths = lengths.at[0, 1].set(SLOT // 2)
    return lengths.astype(jnp.int32)


def set_ends(entries, own_key, smallest, high):
    shape = entries.shape
    spot = [jax.random.randint(jax.random.fold_in(own_key, axis), (), 0, shape[axis]) for axis in range(len(shape))]
    entries = entries.at[tuple(spot)].set(smallest)
    longest = shape.index(max(shape))
    spot[longest] = (spot[longest] + 1) % shape[longest]
    return entries.at[tuple(spot)].set(high)


def block_scale(stream_key, extent, shards, low, high):
    factor_of, own = 1.0, jax.random.fold_in(stream_key, 6)
    for dim, blocks in shards:
        draws = jnp.exp(jax.random.uniform(jax.random.fold_in(own, dim), (blocks,), jnp.float32, low / len(shards), high / len(shards)))
        factor_of = factor_of * jnp.repeat(draws, extent[dim] // blocks).reshape([-1 if axis == dim else 1 for axis in range(len(extent))])
    return factor_of


def noise(stream_key, dims, scale, limit, cuts=(), kind=jnp.bfloat16):
    entries = scale * jax.random.normal(stream_key, dims, jnp.float32)
    if cuts:
        entries = entries * block_scale(stream_key, dims, cuts, -0.22, 0.18)
    return jnp.clip(entries, -limit, limit).astype(kind)


def setup_inputs(seed: int = 0) -> dict:
    arg_keys = jax.random.split(jax.random.key(seed), 14)
    tokens = noise(arg_keys[0], (2, MB, TOK_MB, D), 1.0, 6.0, ((2, 32),))
    spatial = noise(arg_keys[1], (2, MB, TOK_MB, D), 1.0, 6.0, ((2, 32),))
    box_coords = set_ends(jax.random.randint(arg_keys[2], (2, 2, MB, TOK_MB), 0, COORD), jax.random.fold_in(arg_keys[2], 1), 0, COORD - 1).astype(jnp.int32)
    reading_order = set_ends(jax.random.randint(arg_keys[3], (2, MB, TOK_MB), 0, NB), jax.random.fold_in(arg_keys[3], 1), 0, NB - 1).astype(jnp.int32)
    page_len = draw_page_len(jax.random.fold_in(arg_keys[13], 71), 0)
    w_attn = noise(arg_keys[5], (2, 5, D, D), D ** -0.5, 0.21875, ((2, 8), (3, 4)))
    tables = noise(arg_keys[6], (2, 3, NHEAD, NB, NB), 0.5, 3.0, ((2, 4), (3, 8)))
    w_out = noise(arg_keys[7], (2, D, D), (2 * D // 32) ** -0.5, 0.875, ((1, 4), (2, 8)))
    ln_gain = jnp.clip(1.0 + 0.1 * jax.random.normal(arg_keys[8], (2, D), jnp.float32), 0.5, 1.5).astype(jnp.bfloat16)
    ln_shift = noise(arg_keys[9], (2, D), 0.3, 1.796875, ((1, 32),))
    w_up = noise(arg_keys[10], (D, FF), D ** -0.5, 0.21875, ((1, 32),))
    w_down = noise(arg_keys[11], (FF, D), FF ** -0.5, 0.109375, ((0, 32),))
    grad_out = noise(arg_keys[12], (MB, TOK_MB, D), 1.0, 6.0, ((1, 32),))
    return {"tokens": tokens, "spatial": spatial, "box_coords": box_coords, "reading_order": reading_order, "page_len": page_len, "w_attn": w_attn, "tables": tables, "w_out": w_out, "ln_gain": ln_gain, "ln_shift": ln_shift, "w_up": w_up, "w_down": w_down, "grad_out": grad_out}


highest = lax.Precision.HIGHEST

@jax.custom_vjp
def low(v):
    return lax.optimization_barrier(v.astype(jnp.bfloat16)).astype(jnp.float32)

@jax.custom_vjp
def low_back(v):
    return v

def low_keep(v):
    return (low(v), None)

def low_pass(kept, grad):
    return (grad,)

def back_keep(v):
    return (v, None)

def back_low(kept, grad):
    return (low(grad),)
low.defvjp(low_keep, low_pass)
low_back.defvjp(back_keep, back_low)

def layer_norm(value, gain, shift):
    center = lax.optimization_barrier(jnp.mean(value, axis=-1, keepdims=True))
    centred = value - center
    variance = lax.optimization_barrier(jnp.mean(centred * centred, axis=-1, keepdims=True))
    return centred * lax.rsqrt(variance + 1e-05) * gain + shift

def one_hot(index, count):
    return (index[..., None] == jnp.arange(count, dtype=jnp.int32)).astype(jnp.float32)

def slot_block(params, token_rows, space_rows, box_rows, order_rows, length_rows):
    w_attn, tables, w_out, ln_gain, ln_shift, w_up, w_down = params
    position = jnp.arange(SLOT, dtype=jnp.int32)
    page_id = position[None, :] // length_rows[:, None]
    same_page = (page_id[:, :, None] == page_id[:, None, :])[:, None]
    coarse = COORD // NB
    head_rows = []
    for modality in range(2):
        sources = (token_rows[modality], token_rows[modality], token_rows[modality], space_rows[modality], space_rows[modality])
        projected = []
        for which in range(5):
            made = jnp.einsum('bid,de->bie', sources[which], w_attn[modality, which], precision=highest)
            projected.append(low_back(low(made)).reshape(made.shape[0], SLOT, NHEAD, HDIM))
        queries, key_rows, value_rows, space_query, space_key = projected
        bucket_hot = (one_hot(order_rows[modality], NB), one_hot(box_rows[modality, 0] // coarse, NB), one_hot(box_rows[modality, 1] // coarse, NB))
        pair_bias = jnp.zeros((queries.shape[0], NHEAD, SLOT, SLOT), jnp.float32)
        for which in range(3):
            tabled = jnp.einsum('bia,hac->bhic', bucket_hot[which], tables[modality, which], precision=highest)
            pair_bias = pair_bias + jnp.einsum('bhic,bjc->bhij', tabled, bucket_hot[which], precision=highest)
        score = jnp.einsum('bihd,bjhd->bhij', queries, key_rows, precision=highest)
        score = score + jnp.einsum('bihd,bjhd->bhij', space_query, space_key, precision=highest)
        score = low_back(score * 0.125 + pair_bias)
        attn_prob = jax.nn.softmax(jnp.where(same_page, score, -1e+30), axis=-1)
        attended = jnp.einsum('bhij,bjhd->bihd', low(attn_prob), value_rows, precision=highest)
        head_rows.append(low_back(low(attended)).reshape(attended.shape[0], SLOT, D))
    attn_sum = low_back(jnp.einsum('sbid,sde->bie', jnp.stack(head_rows), w_out, precision=highest))
    residual = token_rows[0] + token_rows[1] + attn_sum
    hidden = layer_norm(residual, ln_gain[0], ln_shift[0])
    pre_act = low_back(jnp.einsum('bid,df->bif', low(hidden), w_up, precision=highest))
    activated = low(jax.nn.gelu(pre_act, approximate=False))
    branch = low_back(jnp.einsum('bif,fd->bid', activated, w_down, precision=highest))
    return layer_norm(hidden + branch, ln_gain[1], ln_shift[1])

def reference(tokens, spatial, box_coords, reading_order, page_len, w_attn, tables, w_out, ln_gain, ln_shift, w_up, w_down, grad_out):
    slot_total = MB * SLOTS_ALL
    group = math.gcd(slot_total, 8)
    blocks = slot_total // group
    token_blocks = tokens.astype(jnp.float32).reshape(2, blocks, group, SLOT, D).swapaxes(0, 1)
    space_blocks = spatial.astype(jnp.float32).reshape(2, blocks, group, SLOT, D).swapaxes(0, 1)
    box_blocks = box_coords.reshape(2, 2, blocks, group, SLOT).transpose(2, 0, 1, 3, 4)
    order_blocks = reading_order.reshape(2, blocks, group, SLOT).swapaxes(0, 1)
    length_blocks = page_len.reshape(blocks, group)
    cotangent = grad_out.astype(jnp.float32).reshape(blocks, group, SLOT, D)
    params = tuple((weight.astype(jnp.float32) for weight in (w_attn, tables, w_out, ln_gain, ln_shift, w_up, w_down)))
    checked = jax.checkpoint(slot_block)

    def forward(weights, token_input):

        def one_block(pieces):
            return checked(weights, pieces[0], pieces[1], pieces[2], pieces[3], pieces[4])
        return lax.map(one_block, (token_input, space_blocks, box_blocks, order_blocks, length_blocks))
    result, pullback = jax.vjp(forward, params, token_blocks)
    grad_params, grad_token_blocks = pullback(cotangent)
    out = result.reshape(MB, TOK_MB, D).astype(jnp.bfloat16)
    grad_tokens = grad_token_blocks.swapaxes(0, 1).reshape(2, MB, TOK_MB, D).astype(jnp.bfloat16)
    return (out, grad_tokens, grad_params[0], grad_params[1], grad_params[2], grad_params[3], grad_params[4], grad_params[5], grad_params[6])
```

```python
import functools

import jax
import jax.numpy as jnp
from jax import lax
from jax.experimental import pallas as pl
from jax.experimental.pallas import tpu as pltpu
from jax.sharding import PartitionSpec as P

COORD = 1024
f32 = jnp.float32
bf16 = jnp.bfloat16


def layer_norm(value, gain, shift):
    center = jnp.mean(value, axis=-1, keepdims=True)
    centred = value - center
    variance = jnp.mean(centred * centred, axis=-1, keepdims=True)
    return centred * lax.rsqrt(variance + 1e-05) * gain + shift


def swap(value, axis, mask):
    count = lax.axis_size(axis)
    return lax.ppermute(value, axis, [(place, place ^ mask) for place in range(count)])


def gather_rows(own):
    two = jnp.stack([own, swap(own, "head", 2)])
    four = jnp.concatenate([two, swap(two, "head", 1)])
    return four.reshape((4 * own.shape[0],) + own.shape[1:])


def scatter_rows(part):
    blocks = part.reshape((4, part.shape[0] // 4) + part.shape[1:])
    half = blocks[:2].astype(f32) + swap(blocks[2:].astype(bf16), "head", 1).astype(f32)
    return half[0] + swap(half[1].astype(bf16), "head", 2).astype(f32)


def page_bits():
    count = lax.axis_size("page")
    return [1 << bit for bit in reversed(range(count.bit_length() - 1))]


def gather_pages(own):
    full = own
    for depth, mask in enumerate(page_bits()):
        full = jnp.stack([full, swap(full, "page", mask)], axis=depth)
    return full.reshape((lax.axis_size("page"),) + own.shape)


def scatter_pages(blocks):
    masks = page_bits()
    part = blocks.reshape((2,) * len(masks) + blocks.shape[1:])
    for depth in reversed(range(len(masks))):
        keep = lax.index_in_dim(part, 0, depth, keepdims=False)
        send = lax.index_in_dim(part, 1, depth, keepdims=False).astype(bf16)
        part = keep.astype(f32) + swap(send, "page", masks[depth]).astype(f32)
    return part


def by_page(blocks):
    count = blocks.shape[0]
    order = jnp.arange(count, dtype=jnp.int32) ^ lax.axis_index("page")
    return jnp.take(blocks, order, axis=0)


def dot(left, right, dims):
    return lax.dot_general(left, right, (dims, ((), ())), preferred_element_type=f32)


AB = ((1,), (0,))
ABT = ((1,), (1,))
ATB = ((0,), (0,))


def hot_columns(ids_ref, which, buckets):
    rows = ids_ref.shape[0]
    lane = lax.broadcasted_iota(jnp.int32, (rows, buckets), 1)
    return jnp.where(ids_ref[:, which : which + 1] == lane, 1.0, 0.0).astype(bf16)


def attend_kernel(x_ref, s_ref, w_ref, table_ref, out_ref, idc_ref, idr_ref, proj_ref, prob_ref, head_ref, part_ref):
    heads, buckets = table_ref.shape[0], table_ref.shape[1]
    width = heads * 64
    proj_ref[:, : 3 * width] = dot(x_ref[...], w_ref[:, : 3 * width], AB).astype(bf16)
    proj_ref[:, 3 * width :] = dot(s_ref[...], w_ref[:, 3 * width :], AB).astype(bf16)
    hots = [hot_columns(idc_ref, which, buckets) for which in range(3)]
    same = idc_ref[:, 3:4] == idr_ref[3:4, :]
    for head in range(heads):
        at = [slice(which * width + head * 64, which * width + head * 64 + 64) for which in range(5)]
        tabled = [
            dot(hots[which], table_ref[head, :, which * buckets : (which + 1) * buckets], AB).astype(bf16)
            for which in range(3)
        ]
        left = jnp.concatenate(
            [proj_ref[:, at[0]] * bf16(0.125), proj_ref[:, at[3]] * bf16(0.125)] + tabled, axis=1
        )
        right = jnp.concatenate([proj_ref[:, at[1]], proj_ref[:, at[4]]] + hots, axis=1)
        score = jnp.where(same, dot(left, right, ABT), -1e30)
        top = jnp.max(score, axis=1, keepdims=True)
        weight = jnp.exp(score - top)
        total = jnp.sum(weight, axis=1, keepdims=True)
        prob = (weight / total).astype(bf16)
        prob_ref[head] = prob
        head_ref[:, head * 64 : head * 64 + 64] = dot(prob, proj_ref[:, at[2]], AB).astype(bf16)
    part_ref[...] = dot(head_ref[...], out_ref[...], ABT)


def attend(rows_x, rows_s, weight, table, out_t, ids_col, ids_row):
    rows, heads = rows_x.shape[0], table.shape[0]
    return pl.pallas_call(
        attend_kernel,
        out_shape=(
            jax.ShapeDtypeStruct((rows, weight.shape[1]), bf16),
            jax.ShapeDtypeStruct((heads, rows, rows), bf16),
            jax.ShapeDtypeStruct((rows, heads * 64), bf16),
            jax.ShapeDtypeStruct((rows, out_t.shape[0]), f32),
        ),
        compiler_params=pltpu.CompilerParams(vmem_limit_bytes=48 * 1024 * 1024),
        name="attend",
    )(rows_x, rows_s, weight, table, out_t, ids_col, ids_row)


def attend_back_kernel(grad_ref, proj_ref, prob_ref, w_ref, out_ref, idc_ref, idr_ref, dproj_ref, dtable_ref, rows_ref):
    heads, rows = prob_ref.shape[0], prob_ref.shape[1]
    buckets = dtable_ref.shape[1]
    width = heads * 64
    grad_heads = dot(grad_ref[...], out_ref[...], AB).astype(bf16)
    hots = [hot_columns(idc_ref, which, buckets) for which in range(3)]
    bucket = lax.broadcasted_iota(jnp.int32, (buckets, rows), 0)
    hots_t = [
        jnp.where(idr_ref[which : which + 1, :] == bucket, 1.0, 0.0).astype(bf16) for which in range(3)
    ]
    for head in range(heads):
        at = [slice(which * width + head * 64, which * width + head * 64 + 64) for which in range(5)]
        prob = prob_ref[head]
        grad_out = grad_heads[:, head * 64 : head * 64 + 64]
        grad_prob = dot(grad_out, proj_ref[:, at[2]], ABT)
        weighted = prob.astype(f32) * grad_prob
        row_dot = jnp.sum(weighted, axis=1, keepdims=True)
        grad_score = (weighted - prob.astype(f32) * row_dot).astype(bf16)
        dproj_ref[:, at[2]] = dot(prob, grad_out, ATB).astype(bf16)
        right = jnp.concatenate([proj_ref[:, at[1]], proj_ref[:, at[4]]] + hots, axis=1)
        spread = dot(grad_score, right, AB)
        dproj_ref[:, at[0]] = (spread[:, :64] * 0.125).astype(bf16)
        dproj_ref[:, at[3]] = (spread[:, 64:128] * 0.125).astype(bf16)
        left = jnp.concatenate([proj_ref[:, at[0]], proj_ref[:, at[3]]], axis=1)
        grad_keys = dot(grad_score, left, ATB) * 0.125
        dproj_ref[:, at[1]] = grad_keys[:, :64].astype(bf16)
        dproj_ref[:, at[4]] = grad_keys[:, 64:].astype(bf16)
        for which in range(3):
            piece = spread[:, 128 + which * buckets : 128 + (which + 1) * buckets].astype(bf16)
            dtable_ref[head, :, which * buckets : (which + 1) * buckets] = dot(hots_t[which], piece, AB)
    rows_ref[...] = dot(dproj_ref[:, : 3 * width], w_ref[:, : 3 * width], ABT)


def attend_back(grad_all, proj, prob, weight, out_t, ids_col, ids_row, buckets):
    rows, heads = proj.shape[0], prob.shape[0]
    return pl.pallas_call(
        attend_back_kernel,
        out_shape=(
            jax.ShapeDtypeStruct(proj.shape, bf16),
            jax.ShapeDtypeStruct((heads, buckets, 3 * buckets), f32),
            jax.ShapeDtypeStruct((rows, weight.shape[0]), f32),
        ),
        compiler_params=pltpu.CompilerParams(vmem_limit_bytes=48 * 1024 * 1024),
        name="attend_back",
    )(grad_all, proj, prob, weight, out_t, ids_col, ids_row)


def local(
    tokens,
    spatial,
    box_coords,
    reading_order,
    page_len,
    w_attn,
    tables,
    w_out,
    ln_gain,
    ln_shift,
    w_up,
    w_down,
    grad_out,
):
    batches, own_count = tokens.shape[1], tokens.shape[2]
    features = tokens.shape[3]
    rows = box_coords.shape[3]
    buckets = tables.shape[4]
    heads = tables.shape[2]
    own_width = w_attn.shape[3]
    share = w_attn.shape[2]
    coarse = COORD // buckets
    head_index = lax.axis_index("head")
    modality = head_index // 2
    pages = lax.axis_size("page")

    def mine(value):
        return lax.dynamic_index_in_dim(value, modality, 0, keepdims=False)

    def other(value):
        return lax.dynamic_index_in_dim(value, 1 - modality, 0, keepdims=False)

    def bundle_attn(pick):
        attn = pick(w_attn).transpose(1, 0, 2)
        table = pick(tables)
        proj = pick(w_out).T
        return attn, table, proj

    attn_own, table_own, proj_own = bundle_attn(mine)
    attn_send, table_send, proj_send = bundle_attn(other)
    attn_got = swap(attn_send, "head", 2)
    table_got = swap(table_send, "head", 2)
    proj_got = swap(proj_send, "head", 2)
    attn_share = jnp.stack([attn_own, attn_got], axis=2).reshape(share, -1)
    table_share = jnp.concatenate([table_own, table_got], axis=1).transpose(1, 2, 0, 3)
    table_share = table_share.reshape(share, 3 * buckets)
    proj_share = jnp.concatenate([proj_own, proj_got], axis=1)
    bundle = jnp.concatenate([attn_share, proj_share, table_share], axis=1)
    bundle_full = by_page(gather_pages(bundle))
    attn_cols = 10 * own_width
    proj_cols = 2 * own_width
    weight = bundle_full[..., :attn_cols].reshape(features, attn_cols)
    out_t = bundle_full[..., attn_cols : attn_cols + proj_cols].reshape(features, proj_cols)
    table = bundle_full[..., attn_cols + proj_cols :]
    table = table.reshape(pages, 2 * heads, buckets // pages, 3 * buckets).transpose(1, 0, 2, 3)
    table = table.reshape(2 * heads, buckets, 3 * buckets)

    keep_rows = jnp.stack([mine(tokens), mine(spatial)])
    send_rows = jnp.stack([other(tokens), other(spatial)])
    two = jnp.stack([keep_rows, swap(send_rows, "head", 2)], axis=2)
    four = jnp.concatenate([two, swap(two, "head", 1)], axis=2)
    rows_full = four.reshape(2, batches, rows, features)

    ff_full = gather_pages(jnp.concatenate([w_up.T, w_down], axis=1))
    up_t = ff_full[..., :features].reshape(-1, features)
    down = ff_full[..., features:].reshape(-1, features)

    norms = jnp.stack([ln_gain, ln_shift])
    order = jnp.array([0, 2, 1, 3], jnp.int32)
    norms_head = gather_rows(norms[None])
    slots = jnp.take(order, jnp.arange(4, dtype=jnp.int32) ^ head_index)
    norms_head = jnp.take(norms_head, slots, axis=0)
    norms_full = by_page(gather_pages(norms_head))
    norms_full = norms_full.transpose(2, 3, 0, 1, 4).reshape(2, 2, features).astype(f32)
    gain, shift = norms_full[0], norms_full[1]

    blocks = order ^ head_index
    ids = jnp.concatenate(
        [
            mine(reading_order)[None],
            mine(box_coords) // coarse,
        ]
    )
    ids = jnp.concatenate(
        [ids, jnp.arange(rows, dtype=jnp.int32)[None, None] // page_len.reshape(1, batches, 1)]
    )
    ids = jnp.take(ids.reshape(4, batches, 4, own_count), blocks, axis=2).reshape(4, batches, rows)

    saved = []
    for batch in range(batches):
        ids_row = ids[:, batch]
        ids_col = ids_row.T
        proj, prob, head_rows, part = attend(
            rows_full[0, batch], rows_full[1, batch], weight, table, out_t, ids_col, ids_row
        )
        saved.append((ids_row, ids_col, proj, prob, head_rows, part))

    results, token_grads, dprojs = [], [], []
    dtable = dout = dgain = dshift = dup = ddown = 0.0
    for batch in range(batches):
        ids_row, ids_col, proj, prob, head_rows, part = saved[batch]
        attn_sum = scatter_rows(part)
        residual = tokens[0, batch].astype(f32) + tokens[1, batch].astype(f32) + attn_sum
        hidden, first_back = jax.vjp(layer_norm, residual, gain[0], shift[0])
        hidden_all = gather_rows(hidden.astype(bf16))
        pre_act = dot(hidden_all, up_t, ABT)
        cdf = 0.5 * (1.0 + lax.erf(pre_act * 0.7071067811865476))
        act = (pre_act * cdf).astype(bf16)
        slope = cdf + pre_act * jnp.exp(-0.5 * pre_act * pre_act) * 0.3989422804014327
        branch = scatter_rows(dot(act, down, AB))
        result, last_back = jax.vjp(layer_norm, hidden + branch, gain[1], shift[1])
        results.append(result.astype(bf16))
        grad_sum, gain_two, shift_two = last_back(grad_out[batch].astype(f32))
        branch_all = gather_rows(grad_sum.astype(bf16))
        ddown = ddown + dot(act, branch_all, ATB)
        grad_pre = (dot(branch_all, down, ABT) * slope).astype(bf16)
        dup = dup + dot(grad_pre, hidden_all, ATB)
        grad_hidden = grad_sum + scatter_rows(dot(grad_pre, up_t, AB))
        grad_res, gain_one, shift_one = first_back(grad_hidden)
        dgain = dgain + jnp.stack([gain_one, gain_two])
        dshift = dshift + jnp.stack([shift_one, shift_two])
        grad_all = gather_rows(grad_res.astype(bf16))
        dout = dout + dot(grad_all, head_rows, ATB)
        dproj, dtable_part, grad_rows = attend_back(
            grad_all, proj, prob, weight, out_t, ids_col, ids_row, buckets
        )
        dtable = dtable + dtable_part
        dprojs.append(dproj)
        row_blocks = grad_rows.reshape(4, own_count, features)
        half = row_blocks[:2] + swap(row_blocks[2:].astype(bf16), "head", 1).astype(f32)
        from_other = swap(half[1].astype(bf16), "head", 2).astype(f32)
        both = jnp.where(modality == 0, jnp.stack([half[0], from_other]), jnp.stack([from_other, half[0]]))
        token_grads.append((both + grad_res[None]).astype(bf16))

    dprojs = jnp.concatenate(dprojs)
    all_x = rows_full[0].reshape(-1, features)
    all_s = rows_full[1].reshape(-1, features)
    split = 6 * own_width
    dweight = jnp.concatenate(
        [dot(all_x, dprojs[:, :split], ATB), dot(all_s, dprojs[:, split:], ATB)], axis=1
    ).astype(bf16)

    dff = jnp.concatenate([dup.astype(bf16), ddown.astype(bf16)], axis=1)
    dff = scatter_pages(dff.reshape(pages, -1, 2 * features))
    dup_share = dff[:, :features].T
    ddown_share = dff[:, features:]

    dnorms = jnp.stack([dgain, dshift]).reshape(2, 2, pages, 4, -1).transpose(3, 2, 0, 1, 4)
    dnorms = jnp.take(dnorms, blocks, axis=0)
    half = dnorms[:2] + swap(dnorms[2:], "head", 1)
    dnorms = half[0] + swap(half[1], "head", 2)
    dnorms = scatter_pages(by_page(dnorms))

    dtable = dtable.reshape(2 * heads, pages, buckets // pages, 3 * buckets).transpose(1, 0, 2, 3)
    dtable = dtable.reshape(pages, share, 3 * buckets).astype(bf16)
    dbundle = jnp.concatenate(
        [dweight.reshape(pages, share, attn_cols), dout.astype(bf16).reshape(pages, share, proj_cols), dtable],
        axis=2,
    )
    dbundle = scatter_pages(by_page(dbundle))
    dattn = dbundle[:, :attn_cols].reshape(share, 5, 2, own_width).transpose(2, 1, 0, 3)
    dproj_out = dbundle[:, attn_cols : attn_cols + proj_cols].reshape(share, 2, own_width).transpose(1, 2, 0)
    dtable = dbundle[:, attn_cols + proj_cols :].reshape(2, heads, buckets // pages, 3, buckets)
    dtable = dtable.transpose(0, 3, 1, 2, 4)

    def both_modalities(pair):
        got = swap(pair[1].astype(bf16), "head", 2).astype(f32)
        return jnp.where(modality == 0, jnp.stack([pair[0], got]), jnp.stack([got, pair[0]]))

    return (
        jnp.stack(results),
        jnp.stack(token_grads, axis=1),
        both_modalities(dattn),
        both_modalities(dtable),
        both_modalities(dproj_out),
        dnorms[0],
        dnorms[1],
        dup_share,
        ddown_share,
    )


def solution(mesh):
    return jax.shard_map(
        local,
        mesh=mesh,
        in_specs=(
            P(None, None, ("page", "head"), None),
            P(None, None, ("page", "head"), None),
            P(None, None, None, "page"),
            P(None, None, "page"),
            P(None, "page"),
            P(None, None, "page", "head"),
            P(None, None, "head", "page", None),
            P(None, "head", "page"),
            P(None, ("page", "head")),
            P(None, ("page", "head")),
            P(None, ("page", "head")),
            P(("page", "head"), None),
            P(None, ("page", "head"), None),
        ),
        out_specs=(
            P(None, ("page", "head"), None),
            P(None, None, ("page", "head"), None),
            P(None, None, "page", "head"),
            P(None, None, "head", "page", None),
            P(None, "head", "page"),
            P(None, ("page", "head")),
            P(None, ("page", "head")),
            P(None, ("page", "head")),
            P(("page", "head"), None),
        ),
        check_vma=False,
    )
```

```python
import functools

import jax
import jax.numpy as jnp
from jax import lax
from jax.experimental import pallas as pl
from jax.experimental.pallas import tpu as pltpu
from jax.sharding import PartitionSpec as P

COORD = 1024
EPS = 1e-05
GROUPS = 8
EXTRA = 16
f32 = jnp.float32
bf16 = jnp.bfloat16
AB = ((1,), (0,))
ABT = ((1,), (1,))
ATB = ((0,), (0,))
ANY = pl.BlockSpec(memory_space=pl.ANY)
SMEM = pl.BlockSpec(memory_space=pltpu.SMEM)
VM = pl.BlockSpec(memory_space=pltpu.VMEM)
PARAMS = pltpu.CompilerParams(vmem_limit_bytes=56 * 1024 * 1024)
FAR_X = (4, 2, 1)
FAR_Z = (4, 1, 2)


def struct(shape, kind):
    return jax.ShapeDtypeStruct(tuple(shape), kind)


def dot(left, right, dims):
    return lax.dot_general(left, right, (dims, ((), ())), preferred_element_type=f32)


def swap(value, axis, mask):
    count = lax.axis_size(axis)
    return lax.ppermute(value, axis, [(place, place ^ mask) for place in range(count)])


def after(value, *earlier):
    return lax.optimization_barrier((value, earlier))[0]


def gather_rows(own):
    side = swap(own, "head", 2)
    return own, side, swap(own, "head", 1), swap(side, "head", 1)


def scatter_rows(keep, send):
    own = keep.shape[0] // 2
    near = swap(send, "head", 1)
    far = swap((keep[own:] + near[own:].astype(f32)).astype(bf16), "head", 2)
    return keep, near, far


def page_bits():
    count = lax.axis_size("page")
    return [1 << bit for bit in reversed(range(count.bit_length() - 1))]


def gather_pages(own):
    full = own
    for depth, mask in enumerate(page_bits()):
        full = jnp.stack([full, swap(full, "page", mask)], axis=depth)
    return full.reshape((lax.axis_size("page"),) + own.shape)


def scatter_pages(blocks):
    masks = page_bits()
    part = blocks.reshape((2,) * len(masks) + blocks.shape[1:])
    for depth in reversed(range(len(masks))):
        keep = lax.index_in_dim(part, 0, depth, keepdims=False)
        send = lax.index_in_dim(part, 1, depth, keepdims=False)
        part = keep.astype(f32) + swap(send.astype(bf16), "page", masks[depth]).astype(f32)
    return part


def by_page(blocks):
    count = blocks.shape[0]
    order = jnp.arange(count, dtype=jnp.int32) ^ lax.axis_index("page")
    return jnp.take(blocks, order, axis=0)


def regroup(full, heads):
    pages, share, columns = full.shape
    if heads == 1:
        return full.reshape(GROUPS, -1, columns)
    parts = full.reshape(GROUPS, pages // GROUPS, heads, share // heads, columns)
    return parts.transpose(0, 2, 1, 3, 4).reshape(GROUPS, -1, columns)


def ungroup(full, pages, heads):
    columns = full.shape[2]
    if heads == 1:
        return full.reshape(pages, -1, columns)
    parts = full.reshape(GROUPS, heads, pages // GROUPS, -1, columns)
    return parts.transpose(0, 2, 1, 3, 4).reshape(pages, -1, columns)


def direct():
    return lax.axis_size("page") == GROUPS


class Link:
    def __init__(self):
        self.last = {}

    def swap(self, value, mask):
        if mask in self.last:
            value = after(value, self.last[mask])
        got = swap(value, "page", mask)
        self.last[mask] = got
        return got


def chunks_gather(link, shares, orders, heads):
    if direct():
        parts = [share[None] for share in shares]
        for depth in range(2):
            for at, masks in enumerate(orders):
                parts[at] = jnp.concatenate([parts[at], link.swap(parts[at], masks[depth])])
        return [(part, link.swap(part, masks[2])) for part, masks in zip(parts, orders)]
    pairs = []
    for share, groups in zip(shares, heads):
        full = by_page(gather_pages(share))
        width = share.shape[1] // len(groups)
        full = jnp.concatenate(
            [regroup(full[..., at * width : (at + 1) * width], count) for at, count in enumerate(groups)], axis=2
        )
        pairs.append((full[: GROUPS // 2], full[GROUPS // 2 :]))
    return pairs


class Scatter:
    def __init__(self, link, keep, send, masks):
        self.link, self.keep, self.send, self.masks = link, keep, send, list(masks)

    def step(self):
        total = self.keep + self.link.swap(self.send, self.masks.pop()).astype(f32)
        half = total.shape[0] // 2
        self.keep, self.send = total[:half], total[half:].astype(bf16)

    def result(self):
        return self.keep[0] + self.link.swap(self.send, self.masks.pop())[0].astype(f32)


def generic_scatter(keep, send, heads=(1,)):
    pages = lax.axis_size("page")
    full = jnp.concatenate([keep.astype(bf16), send])
    width = full.shape[2] // len(heads)
    full = jnp.concatenate(
        [ungroup(full[..., at * width : (at + 1) * width], pages, count) for at, count in enumerate(heads)], axis=2
    )
    return scatter_pages(by_page(full))


def places(masks):
    if not direct():
        masks = (1, 2, 4)
    return [
        sum(mask for bit, mask in enumerate(masks) if (place >> bit) & 1) for place in range(GROUPS)
    ]


class Copies:
    def __init__(self, sems):
        self.sems, self.count = sems, 0

    def start(self, source, target):
        copy = pltpu.make_async_copy(source, target, self.sems.at[self.count])
        self.count += 1
        copy.start()
        return copy


def wait_all(copies):
    for copy in copies:
        copy.wait()


def load_chunk(copies, page, refs, masks, target):
    started = []
    share = target.shape[0] // GROUPS
    for place, number in enumerate(places(masks)):
        source = refs[place // (GROUPS // 2)].at[place % (GROUPS // 2), pl.ds(0, share)]
        row = pl.multiple_of(jnp.bitwise_xor(page, number) * share, share)
        started.append(copies.start(source, target.at[pl.ds(row, share), :]))
    return started


def load_rows(copies, refs, target, pick=None):
    count = refs[0].shape[-2]
    return [
        copies.start(ref if pick is None else ref.at[pick], target.at[pl.ds(place * count, count), :])
        for place, ref in enumerate(refs)
    ]


def hot_columns(ids_ref, which, buckets):
    rows = ids_ref.shape[0]
    lane = lax.broadcasted_iota(jnp.int32, (rows, buckets), 1)
    return jnp.where(ids_ref[:, which : which + 1] == lane, 1.0, 0.0).astype(bf16)


def head_slices(head, half, size):
    group = half // size
    base = 0 if head < group else 6 * half
    at = [base + which * half + (head % group) * size for which in range(4)]
    query, key, space_query, space_key = [slice(start, start + size) for start in at]
    value = slice(4 * half + head * size, 4 * half + (head + 1) * size)
    return query, key, value, space_query, space_key


def attend_kernel(batch, heads, page_ref, *refs):
    (
        rows_refs, a_refs, m_refs, b_refs, o_refs,
        (idc_ref, idr_ref, proj_ref, prob_ref, head_ref, keep_ref, send_ref, x_ref, s_ref, wa_ref, wm_ref, wb_ref, wo_ref, sems),
    ) = refs[:4], refs[4:6], refs[6:8], refs[8:10], refs[10:12], refs[12:]
    page = page_ref[0]
    copies = Copies(sems)
    first = load_rows(copies, rows_refs, x_ref, (0, batch)) + load_rows(copies, rows_refs, s_ref, (1, batch))
    first += load_chunk(copies, page, a_refs, FAR_Z, wa_ref)
    second = load_chunk(copies, page, m_refs, FAR_X, wm_ref)
    third = load_chunk(copies, page, b_refs, FAR_X, wb_ref)
    last = load_chunk(copies, page, o_refs, FAR_X, wo_ref)
    rows = x_ref.shape[0]
    width = wo_ref.shape[1]
    half = width // 2
    size = width // heads
    buckets = (wm_ref.shape[1] - width) // 3
    share = wm_ref.shape[0] // GROUPS
    step = share // heads
    hots = [hot_columns(idc_ref, which, buckets) for which in range(3)]
    same = idc_ref[:, 3:4] == idr_ref[3:4, :]
    wait_all(first)
    proj_ref[:, :width] = dot(x_ref[...], wa_ref[:, :width], AB).astype(bf16)
    proj_ref[:, width : 2 * width] = dot(s_ref[...], wa_ref[:, width:], AB).astype(bf16)
    wait_all(second)
    proj_ref[:, 2 * width : 3 * width] = dot(x_ref[...], wm_ref[:, :width], AB).astype(bf16)
    wait_all(third)
    proj_ref[:, 3 * width : 4 * width] = dot(x_ref[...], wb_ref[:, :width], AB).astype(bf16)
    proj_ref[:, 4 * width :] = dot(s_ref[...], wb_ref[:, width:], AB).astype(bf16)
    for head in range(heads):
        query, key, value, space_query, space_key = head_slices(head, half, size)
        tabled = []
        for which in range(3):
            column = width + which * buckets
            table = jnp.concatenate(
                [
                    wm_ref[group * share + head * step : group * share + (head + 1) * step, column : column + buckets]
                    for group in range(GROUPS)
                ]
            )
            tabled.append(dot(hots[which], table, AB).astype(bf16))
        left = jnp.concatenate(
            [proj_ref[:, query] * bf16(0.125), proj_ref[:, space_query] * bf16(0.125)] + tabled, axis=1
        )
        right = jnp.concatenate([proj_ref[:, key], proj_ref[:, space_key]] + hots, axis=1)
        score = jnp.where(same, dot(left, right, ABT), -1e30)
        weight = jnp.exp(score - jnp.max(score, axis=1, keepdims=True))
        prob = (weight * (1.0 / jnp.sum(weight, axis=1, keepdims=True))).astype(bf16)
        prob_ref[head] = prob
        head_ref[:, head * size : (head + 1) * size] = dot(prob, proj_ref[:, value], AB).astype(bf16)
    wait_all(last)
    part = dot(head_ref[...], wo_ref[...], ABT)
    keep_ref[...] = part[: rows // 2]
    send_ref[...] = part[rows // 2 :].astype(bf16)


def attend(batch, heads, page, row_parts, chunks, ids_col, ids_row):
    rows = ids_row.shape[1]
    features = row_parts[0].shape[-1]
    width = chunks[3][0].shape[2]
    size = width // heads
    return pl.pallas_call(
        functools.partial(attend_kernel, batch, heads),
        in_specs=[SMEM] + [ANY] * 12 + [VM] * 2,
        out_shape=(
            struct((rows, 5 * width), bf16),
            struct((heads, rows, rows), bf16),
            struct((rows, width), bf16),
            struct((rows // 2, features), f32),
            struct((rows // 2, features), bf16),
        ),
        scratch_shapes=[pltpu.VMEM((rows, features), bf16)] * 2
        + [pltpu.VMEM((features, pair[0].shape[2]), bf16) for pair in chunks]
        + [pltpu.SemaphoreType.DMA((8 + 4 * GROUPS,))],
        compiler_params=PARAMS,
        name="attend",
    )(page, *row_parts, *[ref for pair in chunks for ref in pair], ids_col, ids_row)


def attend_back_kernel(heads, page_ref, *refs):
    (
        da_refs, a_refs, m_refs, b_refs, o_refs,
        (proj_ref, prob_ref, idc_ref, idr_ref, dproj_ref, dtable_ref, keep_ref, send_ref, da_ref, wa_ref, wm_ref, wb_ref, wo_ref, sems),
    ) = refs[:4], refs[4:6], refs[6:8], refs[8:10], refs[10:12], refs[12:]
    page = page_ref[0]
    copies = Copies(sems)
    first = load_rows(copies, da_refs, da_ref) + load_chunk(copies, page, o_refs, FAR_X, wo_ref)
    last = load_chunk(copies, page, a_refs, FAR_Z, wa_ref)
    last += load_chunk(copies, page, m_refs, FAR_X, wm_ref)
    last += load_chunk(copies, page, b_refs, FAR_X, wb_ref)
    rows = da_ref.shape[0]
    width = wo_ref.shape[1]
    half = width // 2
    size = width // heads
    buckets = (wm_ref.shape[1] - width) // 3
    step = buckets // GROUPS
    hots = [hot_columns(idc_ref, which, buckets) for which in range(3)]
    bucket = lax.broadcasted_iota(jnp.int32, (buckets, rows), 0)
    hots_t = [
        jnp.where(idr_ref[which : which + 1, :] == bucket, 1.0, 0.0).astype(bf16) for which in range(3)
    ]
    wait_all(first)
    grad_heads = dot(da_ref[...], wo_ref[...], AB).astype(bf16)
    for head in range(heads):
        query, key, value, space_query, space_key = head_slices(head, half, size)
        prob = prob_ref[head]
        grad_out = grad_heads[:, head * size : (head + 1) * size]
        grad_prob = dot(grad_out, proj_ref[:, value], ABT)
        weighted = prob.astype(f32) * grad_prob
        row_dot = jnp.sum(weighted, axis=1, keepdims=True)
        grad_score = (weighted - prob.astype(f32) * row_dot).astype(bf16)
        dproj_ref[:, value] = dot(prob, grad_out, ATB).astype(bf16)
        right = jnp.concatenate([proj_ref[:, key], proj_ref[:, space_key]] + hots, axis=1)
        spread = dot(grad_score, right, AB)
        dproj_ref[:, query] = (spread[:, :size] * 0.125).astype(bf16)
        dproj_ref[:, space_query] = (spread[:, size : 2 * size] * 0.125).astype(bf16)
        left = jnp.concatenate([proj_ref[:, query], proj_ref[:, space_query]], axis=1)
        grad_keys = dot(grad_score, left, ATB) * 0.125
        dproj_ref[:, key] = grad_keys[:, :size].astype(bf16)
        dproj_ref[:, space_key] = grad_keys[:, size:].astype(bf16)
        for which in range(3):
            start = 2 * size + which * buckets
            piece = dot(hots_t[which], spread[:, start : start + buckets].astype(bf16), AB)
            for group in range(GROUPS):
                dtable_ref[group, head * step : (head + 1) * step, which * buckets : (which + 1) * buckets] = piece[
                    group * step : (group + 1) * step
                ]
    wait_all(last)
    part = dot(dproj_ref[:, :width], wa_ref[:, :width], ABT)
    part = part + dot(dproj_ref[:, 2 * width : 3 * width], wm_ref[:, :width], ABT)
    part = part + dot(dproj_ref[:, 3 * width : 4 * width], wb_ref[:, :width], ABT)
    keep_ref[...] = part[: rows // 2]
    send_ref[...] = part[rows // 2 :].astype(bf16)


def attend_back(heads, page, da_parts, chunks, proj, prob, ids_col, ids_row):
    rows = ids_row.shape[1]
    features = da_parts[0].shape[-1]
    width = chunks[3][0].shape[2]
    buckets = (chunks[1][0].shape[2] - width) // 3
    return pl.pallas_call(
        functools.partial(attend_back_kernel, heads),
        in_specs=[SMEM] + [ANY] * 12 + [VM] * 4,
        out_shape=(
            struct(proj.shape, bf16),
            struct((GROUPS, heads * buckets // GROUPS, 3 * buckets), f32),
            struct((rows // 2, features), f32),
            struct((rows // 2, features), bf16),
        ),
        scratch_shapes=[pltpu.VMEM((rows, features), bf16)]
        + [pltpu.VMEM((features, pair[0].shape[2]), bf16) for pair in chunks]
        + [pltpu.SemaphoreType.DMA((4 + 4 * GROUPS,))],
        compiler_params=PARAMS,
        name="attend_back",
    )(page, *da_parts, *[ref for pair in chunks for ref in pair], proj, prob, ids_col, ids_row)


def put_blocks(page, masks, full_ref, keep_ref, send_ref):
    for place, number in enumerate(places(masks)):
        block = full_ref[jnp.bitwise_xor(page, number)]
        if place < GROUPS // 2:
            keep_ref[place] = block
        else:
            send_ref[place - GROUPS // 2] = block.astype(bf16)


def attn_weights_kernel(batches, page_ref, *refs):
    rows_refs, dproj_refs, dtable_refs = refs[:4], refs[4 : 4 + batches], refs[4 + batches : 4 + 2 * batches]
    (ka_ref, sa_ref, km_ref, sm_ref, kb_ref, sb_ref, x_ref, d_ref, full_ref, sems) = refs[4 + 2 * batches :]
    page = page_ref[0]
    copies = Copies(sems)
    rows = x_ref.shape[1] // batches
    started = []
    for batch in range(batches):
        at = pl.ds(batch * rows, rows)
        for which in range(2):
            started += load_rows(copies, rows_refs, x_ref.at[which, at], (which, batch))
        started.append(copies.start(dproj_refs[batch], d_ref.at[at]))
    wait_all(started)
    width = d_ref.shape[1] // 5
    shape = (GROUPS, x_ref.shape[2] // GROUPS, width)
    x_t = x_ref[0].T
    s_t = x_ref[1].T
    full_ref[:, :, :width] = dot(x_t, d_ref[:, 3 * width : 4 * width], AB).reshape(shape)
    full_ref[:, :, width:] = dot(s_t, d_ref[:, 4 * width :], AB).reshape(shape)
    put_blocks(page, FAR_X, full_ref, kb_ref, sb_ref)
    full_ref[:, :, :width] = dot(x_t, d_ref[:, 2 * width : 3 * width], AB).reshape(shape)
    total = dtable_refs[0][...]
    for ref in dtable_refs[1:]:
        total = total + ref[...]
    full_ref[:, :, width:] = total
    put_blocks(page, FAR_Z, full_ref, km_ref, sm_ref)
    full_ref[:, :, :width] = dot(x_t, d_ref[:, :width], AB).reshape(shape)
    full_ref[:, :, width:] = dot(s_t, d_ref[:, width : 2 * width], AB).reshape(shape)
    put_blocks(page, FAR_X, full_ref, ka_ref, sa_ref)


def attn_weights(page, row_parts, dprojs, dtables):
    batches = len(dprojs)
    rows, columns = dprojs[0].shape
    features = row_parts[0].shape[-1]
    chunk = (GROUPS // 2, features // GROUPS, 2 * columns // 5)
    return pl.pallas_call(
        functools.partial(attn_weights_kernel, batches),
        in_specs=[SMEM] + [ANY] * (4 + batches) + [VM] * batches,
        out_shape=(struct(chunk, f32), struct(chunk, bf16)) * 3,
        scratch_shapes=[
            pltpu.VMEM((2, batches * rows, features), bf16),
            pltpu.VMEM((batches * rows, columns), bf16),
            pltpu.VMEM((GROUPS,) + chunk[1:], f32),
            pltpu.SemaphoreType.DMA((9 * batches,)),
        ],
        compiler_params=PARAMS,
        name="attn_weights",
    )(page, *row_parts, *dprojs, *dtables)


def out_weights_kernel(batches, page_ref, *refs):
    da_refs, head_refs = refs[: 4 * batches], refs[4 * batches : 5 * batches]
    extra_ref, keep_ref, send_ref, da_ref, head_ref, full_ref, sems = refs[5 * batches :]
    page = page_ref[0]
    copies = Copies(sems)
    rows = da_ref.shape[0] // batches
    started = []
    for batch in range(batches):
        at = pl.ds(batch * rows, rows)
        started += load_rows(copies, da_refs[4 * batch : 4 * batch + 4], da_ref.at[at])
        started.append(copies.start(head_refs[batch], head_ref.at[at]))
    wait_all(started)
    share = full_ref.shape[1] - extra_ref.shape[1]
    full_ref[:, :share] = dot(da_ref[...], head_ref[...], ATB).reshape(GROUPS, share, full_ref.shape[2])
    full_ref[:, share:] = extra_ref[...]
    put_blocks(page, FAR_X, full_ref, keep_ref, send_ref)


def out_weights(page, da_parts, head_rows, extra):
    batches = len(head_rows)
    rows, width = head_rows[0].shape
    features = da_parts[0][0].shape[-1]
    chunk = (GROUPS // 2, features // GROUPS + extra.shape[1], width)
    return pl.pallas_call(
        functools.partial(out_weights_kernel, batches),
        in_specs=[SMEM] + [ANY] * (5 * batches) + [VM],
        out_shape=(struct(chunk, f32), struct(chunk, bf16)),
        scratch_shapes=[
            pltpu.VMEM((batches * rows, features), bf16),
            pltpu.VMEM((batches * rows, width), bf16),
            pltpu.VMEM((GROUPS,) + chunk[1:], f32),
            pltpu.SemaphoreType.DMA((5 * batches,)),
        ],
        compiler_params=PARAMS,
        name="out_weights",
    )(page, *[ref for parts in da_parts for ref in parts], *head_rows, extra)


def load_ff(copies, refs, target):
    share = target.shape[0] // GROUPS
    return [
        copies.start(
            refs[place // (GROUPS // 2)].at[place % (GROUPS // 2)], target.at[pl.ds(place * share, share), :]
        )
        for place in range(GROUPS)
    ]


def forward_kernel(*refs):
    h_refs, f_refs, (act_ref, slope_ref, keep_ref, send_ref, h_ref, w_ref, sems) = refs[:4], refs[4:6], refs[6:]
    copies = Copies(sems)
    wait_all(load_rows(copies, h_refs, h_ref) + load_ff(copies, f_refs, w_ref))
    rows, features = h_ref.shape
    pre = dot(h_ref[...], w_ref[:, :features], ABT)
    normal = 0.5 + 0.5 * lax.erf(pre * 0.7071067811865476)
    act = (pre * normal).astype(bf16)
    act_ref[...] = act
    slope_ref[...] = (normal + pre * jnp.exp(-0.5 * pre * pre) * 0.3989422804014327).astype(bf16)
    part = dot(act, w_ref[:, features:], AB)
    keep_ref[...] = part[: rows // 2]
    send_ref[...] = part[rows // 2 :].astype(bf16)


def backward_kernel(*refs):
    g_refs, f_refs, (act_ref, slope_ref, pre_ref, keep_ref, send_ref, g_ref, w_ref, sems) = refs[:4], refs[4:6], refs[6:]
    copies = Copies(sems)
    wait_all(load_rows(copies, g_refs, g_ref) + load_ff(copies, f_refs, w_ref))
    rows, features = g_ref.shape
    grad_act = dot(g_ref[...], w_ref[:, features:], ABT)
    grad_pre = (grad_act * slope_ref[...].astype(f32)).astype(bf16)
    pre_ref[...] = grad_pre
    part = dot(grad_pre, w_ref[:, :features], AB)
    keep_ref[...] = part[: rows // 2]
    send_ref[...] = part[rows // 2 :].astype(bf16)


def ff_scratch(rows, features, hidden):
    return [
        pltpu.VMEM((rows, features), bf16),
        pltpu.VMEM((hidden, 2 * features), bf16),
        pltpu.SemaphoreType.DMA((4 + GROUPS,)),
    ]


def forward(parts, pair):
    rows, features = 4 * parts[0].shape[0], parts[0].shape[1]
    hidden = GROUPS * pair[0].shape[1]
    return pl.pallas_call(
        forward_kernel,
        in_specs=[ANY] * 6,
        out_shape=(
            struct((rows, hidden), bf16),
            struct((rows, hidden), bf16),
            struct((rows // 2, features), f32),
            struct((rows // 2, features), bf16),
        ),
        scratch_shapes=ff_scratch(rows, features, hidden),
        compiler_params=PARAMS,
        name="forward",
    )(*parts, *pair)


def backward(parts, pair, act, slope):
    rows, features = 4 * parts[0].shape[0], parts[0].shape[1]
    hidden = GROUPS * pair[0].shape[1]
    return pl.pallas_call(
        backward_kernel,
        in_specs=[ANY] * 6 + [VM] * 2,
        out_shape=(
            struct((rows, hidden), bf16),
            struct((rows // 2, features), f32),
            struct((rows // 2, features), bf16),
        ),
        scratch_shapes=ff_scratch(rows, features, hidden),
        compiler_params=PARAMS,
        name="backward",
    )(*parts, *pair, act, slope)


def ff_weights_kernel(batches, *refs):
    h_refs, g_refs = refs[: 4 * batches], refs[4 * batches : 8 * batches]
    pre_refs, act_refs = refs[8 * batches : 9 * batches], refs[9 * batches : 10 * batches]
    keep_ref, send_ref, h_ref, g_ref, pre_ref, act_ref, sems = refs[10 * batches :]
    copies = Copies(sems)
    rows = h_ref.shape[0] // batches
    started = []
    for batch in range(batches):
        at = pl.ds(batch * rows, rows)
        started += load_rows(copies, h_refs[4 * batch : 4 * batch + 4], h_ref.at[at])
        started += load_rows(copies, g_refs[4 * batch : 4 * batch + 4], g_ref.at[at])
        started.append(copies.start(pre_refs[batch], pre_ref.at[at]))
        started.append(copies.start(act_refs[batch], act_ref.at[at]))
    wait_all(started)
    features = h_ref.shape[1]
    shape = keep_ref.shape[:2] + (features,)
    half = keep_ref.shape[0] * keep_ref.shape[1]
    up = dot(pre_ref[...], h_ref[...], ATB)
    keep_ref[:, :, :features] = up[:half].reshape(shape)
    send_ref[:, :, :features] = up[half:].astype(bf16).reshape(shape)
    down = dot(act_ref[...], g_ref[...], ATB)
    keep_ref[:, :, features:] = down[:half].reshape(shape)
    send_ref[:, :, features:] = down[half:].astype(bf16).reshape(shape)


def ff_weights(h_parts, g_parts, grad_pres, acts):
    batches = len(acts)
    rows, hidden = acts[0].shape
    features = h_parts[0][0].shape[1]
    chunk = (GROUPS // 2, hidden // GROUPS, 2 * features)
    return pl.pallas_call(
        functools.partial(ff_weights_kernel, batches),
        in_specs=[ANY] * (10 * batches),
        out_shape=(struct(chunk, f32), struct(chunk, bf16)),
        scratch_shapes=[pltpu.VMEM((batches * rows, features), bf16)] * 2
        + [pltpu.VMEM((batches * rows, hidden), bf16)] * 2
        + [pltpu.SemaphoreType.DMA((10 * batches,))],
        compiler_params=PARAMS,
        name="ff_weights",
    )(*[ref for parts in h_parts for ref in parts], *[ref for parts in g_parts for ref in parts], *grad_pres, *acts)


def normalize(value):
    centred = value - jnp.mean(value, axis=1, keepdims=True)
    scale = lax.rsqrt(jnp.mean(centred * centred, axis=1, keepdims=True) + EPS)
    return centred * scale, scale


def normalize_back(grad, normal, scale, gain):
    inner = grad * gain
    inner = inner - jnp.mean(inner, axis=1, keepdims=True) - normal * jnp.mean(inner * normal, axis=1, keepdims=True)
    return inner * scale


def norm_sums(grad, normal):
    gain = jnp.sum(grad * normal, axis=0, keepdims=True)
    shift = jnp.sum(grad, axis=0, keepdims=True)
    return jnp.concatenate([gain, shift], axis=0)


def norm_one_kernel(keep_ref, near_ref, far_ref, first_ref, second_ref, gain_ref, shift_ref, normal_ref, scale_ref, low_ref):
    value = first_ref[...].astype(f32) + second_ref[...].astype(f32)
    value = value + (keep_ref[...] + near_ref[...].astype(f32) + far_ref[...].astype(f32))
    normal, scale = normalize(value)
    normal_ref[...] = normal
    scale_ref[...] = scale
    low_ref[...] = (normal * gain_ref[0:1] + shift_ref[0:1]).astype(bf16)


def norm_two_kernel(keep_ref, near_ref, far_ref, normal_ref, grad_ref, gain_ref, shift_ref, out_ref, dc_ref, dz_ref, sums_ref):
    value = normal_ref[...] * gain_ref[0:1] + shift_ref[0:1]
    value = value + (keep_ref[...] + near_ref[...].astype(f32) + far_ref[...].astype(f32))
    normal, scale = normalize(value)
    out_ref[...] = (normal * gain_ref[1:2] + shift_ref[1:2]).astype(bf16)
    grad = grad_ref[...].astype(f32)
    dc = normalize_back(grad, normal, scale, gain_ref[1:2])
    dc_ref[...] = dc
    dz_ref[...] = dc.astype(bf16)
    sums_ref[...] = norm_sums(grad, normal)


def norm_back_kernel(keep_ref, near_ref, far_ref, dc_ref, normal_ref, scale_ref, gain_ref, da_ref, low_ref, sums_ref):
    grad = dc_ref[...] + (keep_ref[...] + near_ref[...].astype(f32) + far_ref[...].astype(f32))
    normal = normal_ref[...]
    da = normalize_back(grad, normal, scale_ref[...], gain_ref[0:1])
    da_ref[...] = da
    low_ref[...] = da.astype(bf16)
    sums_ref[...] = norm_sums(grad, normal)


def norm_call(kernel, name, outs, scattered, *rest):
    own, features = scattered[2].shape
    half = pl.BlockSpec((own, features), lambda step: (0, 0))
    return pl.pallas_call(
        kernel,
        grid=(1,),
        in_specs=[half, half] + [VM] * (1 + len(rest)),
        out_shape=outs,
        name=name,
    )(*scattered, *rest)


def local(
    tokens,
    spatial,
    box_coords,
    reading_order,
    page_len,
    w_attn,
    tables,
    w_out,
    ln_gain,
    ln_shift,
    w_up,
    w_down,
    grad_out,
):
    batches, own, features = tokens.shape[1:]
    rows = box_coords.shape[3]
    buckets = tables.shape[4]
    own_heads = tables.shape[2]
    heads = 2 * own_heads
    half = w_attn.shape[3]
    width = 2 * half
    share = w_attn.shape[2]
    step = tables.shape[3]
    coarse = COORD // buckets
    head_index = lax.axis_index("head")
    modality = head_index // 2
    pages = lax.axis_size("page")
    page_index = lax.axis_index("page")
    page = (page_index if direct() else page_index * 0).astype(jnp.int32).reshape(1)

    def mine(value):
        return lax.dynamic_index_in_dim(value, modality, 0, keepdims=False)

    def other(value):
        return lax.dynamic_index_in_dim(value, 1 - modality, 0, keepdims=False)

    attn_own = mine(w_attn)
    attn_got = swap(other(w_attn), "head", 2)
    table_got = swap(other(tables), "head", 2)
    out_got = swap(other(w_out), "head", 2)
    four = [0, 1, 3, 4]
    chunk_a = jnp.concatenate([attn_own[which] for which in four], axis=1)
    chunk_b = jnp.concatenate([attn_got[which] for which in four], axis=1)
    table = jnp.concatenate([mine(tables), table_got], axis=1).transpose(1, 2, 0, 3).reshape(share, 3 * buckets)
    chunk_m = jnp.concatenate([attn_own[2], attn_got[2], table], axis=1)
    chunk_o = jnp.concatenate([mine(w_out), out_got]).T
    order = jnp.array([0, 2, 1, 3], jnp.int32)
    blocks = order ^ head_index
    slots = jnp.take(order, jnp.arange(4, dtype=jnp.int32) ^ head_index)
    norms_head = jnp.stack(gather_rows(jnp.stack([ln_gain, ln_shift])))
    chunk_f = jnp.concatenate([w_up.T, w_down], axis=1)
    if direct():
        norms_row = jnp.pad(norms_head.reshape(1, -1), ((0, EXTRA - 1), (0, 0)))
        chunk_o = jnp.concatenate([chunk_o, norms_row])
    link = Link()
    pair_a, pair_m, pair_b, pair_o = chunks = chunks_gather(
        link,
        (chunk_a, chunk_m, chunk_b, chunk_o),
        (FAR_Z, FAR_X, FAR_X, FAR_X),
        ((1,), (1, heads), (1,), (1,)),
    )
    (pair_f,) = chunks_gather(link, (chunk_f,), (FAR_X,), ((1,),))

    if direct():
        norms_full = jnp.concatenate([pair_o[0][:, share], pair_o[1][:, share]])
        where = jnp.take(jnp.array(places(FAR_X), jnp.int32), jnp.arange(GROUPS, dtype=jnp.int32) ^ page_index)
        norms_full = jnp.take(norms_full, where, axis=0).reshape((pages,) + norms_head.shape)
    else:
        norms_full = by_page(gather_pages(norms_head))
    norms_full = jnp.take(norms_full, slots, axis=1)
    norms_full = norms_full.transpose(2, 3, 0, 1, 4).reshape(2, 2, features).astype(f32)
    gain, shift = norms_full[0], norms_full[1]

    row_parts = gather_rows_from(
        jnp.stack([mine(tokens), mine(spatial)]), after(jnp.stack([other(tokens), other(spatial)]), attn_got)
    )

    ids = jnp.concatenate(
        [
            mine(reading_order)[None],
            mine(box_coords) // coarse,
            jnp.arange(rows, dtype=jnp.int32)[None, None] // page_len.reshape(1, batches, 1),
        ]
    )
    ids = jnp.take(ids.reshape(4, batches, 4, own), blocks, axis=2).reshape(4, batches, rows)

    saved = []
    for batch in range(batches):
        ids_row = ids[:, batch]
        ids_col = ids_row.T
        saved.append((ids_col, ids_row) + tuple(attend(batch, heads, page, row_parts, chunks, ids_col, ids_row)))

    state = [dict() for _ in range(batches)]
    wide = struct((own, features), f32)
    low = struct((own, features), bf16)
    sums = struct((2, features), f32)
    for batch in range(batches):
        here = state[batch]
        ids_col, ids_row, proj, prob, head_rows, keep, send = saved[batch]
        here["normal"], here["scale"], hidden_low = norm_call(
            norm_one_kernel, "norm_one", (wide, struct((own, 1), f32), low),
            scatter_rows(keep, send), tokens[0, batch], tokens[1, batch], gain, shift,
        )
        here["h"] = gather_rows(hidden_low)
        here["act"], here["slope"], keep, send = forward(here["h"], pair_f)
        here["out"], here["dc"], dz, here["sums_two"] = norm_call(
            norm_two_kernel, "norm_two", (low, wide, low, sums),
            scatter_rows(keep, send), here["normal"], grad_out[batch], gain, shift,
        )
        here["g"] = gather_rows(dz)
        here["grad_pre"], keep, send = backward(here["g"], pair_f, here["act"], here["slope"])
        here["da"], da_low, here["sums_one"] = norm_call(
            norm_back_kernel, "norm_back", (wide, low, sums),
            scatter_rows(keep, send), here["dc"], here["normal"], here["scale"], gain,
        )
        here["a"] = gather_rows(da_low)

    keep, send = ff_weights(
        [here["h"] for here in state],
        [here["g"] for here in state],
        [here["grad_pre"] for here in state],
        [here["act"] for here in state],
    )
    link = Link()
    if direct():
        chunk = Scatter(link, keep, send, FAR_X)
        chunk.step()
        chunk.step()
        dff = chunk.result()
    else:
        dff = generic_scatter(keep, send)

    dnorms = sum(jnp.stack([here["sums_one"], here["sums_two"]], axis=1) for here in state)
    dnorms = dnorms.reshape(2, 2, pages, 4, -1).transpose(3, 2, 0, 1, 4)
    dnorms = jnp.take(dnorms, blocks, axis=0)
    pair = dnorms[:2] + swap(dnorms[2:], "head", 1)
    dnorms = pair[0] + swap(pair[1], "head", 2)
    extra = jnp.zeros((GROUPS, EXTRA, width), f32)
    if direct():
        flat = dnorms.reshape(GROUPS, 1, -1)
        extra = jnp.pad(flat, ((0, 0), (0, EXTRA - 1), (0, width - flat.shape[2])))
    keep, send = out_weights(page, [here["a"] for here in state], [kept[4] for kept in saved], extra)
    if direct():
        chunk = Scatter(link, keep, send, FAR_X)
        chunk.step()
        chunk.step()
        dout = chunk.result()
        dnorms = dout[share, : dnorms[0].size].reshape(dnorms.shape[1:])
        dout = dout[:share]
    else:
        inner = features // GROUPS
        dout = generic_scatter(keep[:, :inner], send[:, :inner])
        dnorms = scatter_pages(by_page(dnorms))

    token_grads = []
    for batch in range(batches):
        here = state[batch]
        ids_col, ids_row, proj, prob, head_rows, _, _ = saved[batch]
        here["dproj"], here["dtable"], keep, send = attend_back(
            heads, page, here["a"], chunks, proj, prob, ids_col, ids_row
        )
        near = swap(send, "head", 1).astype(f32)
        total = keep + near
        ours = total[:own]
        theirs = swap(total[own:].astype(bf16), "head", 2).astype(f32)
        both = jnp.where(modality == 0, jnp.stack([ours, theirs]), jnp.stack([theirs, ours]))
        token_grads.append((both + here["da"][None]).astype(bf16))

    keep_a, send_a, keep_m, send_m, keep_b, send_b = attn_weights(
        page, row_parts, [here["dproj"] for here in state], [here["dtable"] for here in state]
    )
    if direct():
        part_b = Scatter(link, keep_b, send_b, FAR_X)
        part_m = Scatter(link, keep_m, send_m, FAR_Z)
        part_a = Scatter(link, keep_a, send_a, FAR_X)
        for part in (part_b, part_m, part_m, part_b, part_a):
            part.step()
        grad_m, grad_b = part_m.result(), part_b.result()
        part_a.step()
        grad_a = part_a.result()
    else:
        grad_b = generic_scatter(keep_b, send_b)
        grad_m = generic_scatter(keep_m, send_m, (1, heads))
        grad_a = generic_scatter(keep_a, send_a)

    def both_modalities(ours, theirs):
        got = swap(theirs.astype(bf16), "head", 2).astype(f32)
        return jnp.where(modality == 0, jnp.stack([ours, got]), jnp.stack([got, ours]))

    def five(chunk, value):
        parts = [chunk[:, which * half : (which + 1) * half] for which in range(4)]
        return jnp.stack(parts[:2] + [value] + parts[2:])

    dattn = both_modalities(five(grad_a, grad_m[:, :half]), five(grad_b, grad_m[:, half:width]))
    dtable = grad_m[:, width:].reshape(2, own_heads, step, 3, buckets).transpose(0, 3, 1, 2, 4)
    dout = dout.reshape(share, 2, half).transpose(1, 2, 0)
    return (
        jnp.stack([here["out"] for here in state]),
        jnp.stack(token_grads, axis=1),
        dattn,
        both_modalities(dtable[0], dtable[1]),
        both_modalities(dout[0], dout[1]),
        dnorms[0],
        dnorms[1],
        dff[:, :features].T,
        dff[:, features:],
    )


def gather_rows_from(keep, send):
    side = swap(send, "head", 2)
    return keep, side, swap(keep, "head", 1), swap(side, "head", 1)


def solution(mesh):
    return jax.shard_map(
        local,
        mesh=mesh,
        in_specs=(
            P(None, None, ("page", "head"), None),
            P(None, None, ("page", "head"), None),
            P(None, None, None, "page"),
            P(None, None, "page"),
            P(None, "page"),
            P(None, None, "page", "head"),
            P(None, None, "head", "page", None),
            P(None, "head", "page"),
            P(None, ("page", "head")),
            P(None, ("page", "head")),
            P(None, ("page", "head")),
            P(("page", "head"), None),
            P(None, ("page", "head"), None),
        ),
        out_specs=(
            P(None, ("page", "head"), None),
            P(None, None, ("page", "head"), None),
            P(None, None, "page", "head"),
            P(None, None, "head", "page", None),
            P(None, "head", "page"),
            P(None, ("page", "head")),
            P(None, ("page", "head")),
            P(None, ("page", "head")),
            P(("page", "head"), None),
        ),
        check_vma=False,
    )
```

```python
import functools

import jax
import jax.numpy as jnp
from jax import lax
from jax.experimental import pallas as pl
from jax.experimental.pallas import tpu as pltpu
from jax.sharding import PartitionSpec as P

COORD = 1024
EPS = 1e-05
GROUPS = 8
EXTRA = 16
f32 = jnp.float32
bf16 = jnp.bfloat16
AB = ((1,), (0,))
ABT = ((1,), (1,))
ATB = ((0,), (0,))
ANY = pl.BlockSpec(memory_space=pl.ANY)
SMEM = pl.BlockSpec(memory_space=pltpu.SMEM)
VM = pl.BlockSpec(memory_space=pltpu.VMEM)
PARAMS = pltpu.CompilerParams(vmem_limit_bytes=56 * 1024 * 1024)
FAR_X = (4, 2, 1)
FAR_Z = (4, 1, 2)


def cost(microseconds):
    return pl.CostEstimate(
        flops=int(microseconds * 5e8), bytes_accessed=int(microseconds * 3e5), transcendentals=0
    )


def struct(shape, kind):
    return jax.ShapeDtypeStruct(tuple(shape), kind)


def dot(left, right, dims):
    return lax.dot_general(left, right, (dims, ((), ())), preferred_element_type=f32)


def swap(value, axis, mask):
    count = lax.axis_size(axis)
    return lax.ppermute(value, axis, [(place, place ^ mask) for place in range(count)])


def after(value, *earlier):
    return lax.optimization_barrier((value, earlier))[0]


def gather_rows(own):
    side = swap(own, "head", 2)
    return own, side, swap(own, "head", 1), swap(side, "head", 1)


def scatter_rows(keep, send):
    own = keep.shape[0] // 2
    near = swap(send, "head", 1)
    far = swap((keep[own:] + near[own:].astype(f32)).astype(bf16), "head", 2)
    return keep, near, far


def page_bits():
    count = lax.axis_size("page")
    return [1 << bit for bit in reversed(range(count.bit_length() - 1))]


def gather_pages(own):
    full = own
    for depth, mask in enumerate(page_bits()):
        full = jnp.stack([full, swap(full, "page", mask)], axis=depth)
    return full.reshape((lax.axis_size("page"),) + own.shape)


def scatter_pages(blocks):
    masks = page_bits()
    part = blocks.reshape((2,) * len(masks) + blocks.shape[1:])
    for depth in reversed(range(len(masks))):
        keep = lax.index_in_dim(part, 0, depth, keepdims=False)
        send = lax.index_in_dim(part, 1, depth, keepdims=False)
        part = keep.astype(f32) + swap(send.astype(bf16), "page", masks[depth]).astype(f32)
    return part


def by_page(blocks):
    count = blocks.shape[0]
    order = jnp.arange(count, dtype=jnp.int32) ^ lax.axis_index("page")
    return jnp.take(blocks, order, axis=0)


def regroup(full, heads):
    pages, share, columns = full.shape
    if heads == 1:
        return full.reshape(GROUPS, -1, columns)
    parts = full.reshape(GROUPS, pages // GROUPS, heads, share // heads, columns)
    return parts.transpose(0, 2, 1, 3, 4).reshape(GROUPS, -1, columns)


def ungroup(full, pages, heads):
    columns = full.shape[2]
    if heads == 1:
        return full.reshape(pages, -1, columns)
    parts = full.reshape(GROUPS, heads, pages // GROUPS, -1, columns)
    return parts.transpose(0, 2, 1, 3, 4).reshape(pages, -1, columns)


def direct():
    return lax.axis_size("page") == GROUPS


class Order:
    def __init__(self):
        self.last = None

    def tie(self, value):
        if self.last is not None:
            value = after(value, self.last)
        self.last = value
        return value

    def swap(self, value, axis, mask):
        return swap(self.tie(value), axis, mask)


class Gather:
    def __init__(self, order, share, masks):
        self.order, self.part, self.masks = order, share[None], list(masks)

    def start(self):
        self.part = self.order.tie(self.part)
        self.got = swap(self.part, "page", self.masks.pop(0))

    def step(self):
        self.part = jnp.concatenate([self.part, self.got])
        self.start()

    def result(self):
        return self.part, self.got


def generic_gather(share, columns=None, heads=1):
    full = by_page(gather_pages(share))
    if heads == 1:
        full = regroup(full, 1)
    else:
        full = jnp.concatenate([regroup(full[..., :columns], 1), regroup(full[..., columns:], heads)], axis=2)
    return full[: GROUPS // 2], full[GROUPS // 2 :]


class Scatter:
    def __init__(self, order, keep, send, masks):
        self.order, self.keep, self.send, self.masks = order, keep, send, list(masks)

    def start(self):
        self.send = self.order.tie(self.send)
        self.got = swap(self.send, "page", self.masks.pop())

    def step(self):
        total = self.keep + self.got.astype(f32)
        half = total.shape[0] // 2
        self.keep, self.send = total[:half], total[half:].astype(bf16)
        self.start()

    def result(self):
        return self.keep[0] + self.got[0].astype(f32)


def generic_scatter(keep, send, columns=None, heads=1):
    pages = lax.axis_size("page")
    full = jnp.concatenate([keep.astype(bf16), send])
    if heads == 1:
        full = ungroup(full, pages, 1)
    else:
        full = jnp.concatenate(
            [ungroup(full[..., :columns], pages, 1), ungroup(full[..., columns:], pages, heads)], axis=2
        )
    return scatter_pages(by_page(full))


def places(masks):
    if not direct():
        masks = (1, 2, 4)
    return [
        sum(mask for bit, mask in enumerate(masks) if (place >> bit) & 1) for place in range(GROUPS)
    ]


class Copies:
    def __init__(self, sems):
        self.sems, self.count = sems, 0

    def start(self, source, target):
        copy = pltpu.make_async_copy(source, target, self.sems.at[self.count])
        self.count += 1
        copy.start()
        return copy


def wait_all(copies):
    for copy in copies:
        copy.wait()


def load_chunk(copies, page, refs, masks, target, start=0, stop=None):
    started = []
    share = target.shape[0] // GROUPS
    for place, number in enumerate(places(masks)):
        source = refs[place // (GROUPS // 2)].at[place % (GROUPS // 2), pl.ds(0, share)]
        row = pl.multiple_of(jnp.bitwise_xor(page, number) * share, share)
        columns = pl.ds(start, (target.shape[1] if stop is None else stop) - start)
        started.append(copies.start(source, target.at[pl.ds(row, share), columns]))
    return started


def load_rows(copies, refs, target, pick=None):
    count = refs[0].shape[-2]
    return [
        copies.start(ref if pick is None else ref.at[pick], target.at[pl.ds(place * count, count), :])
        for place, ref in enumerate(refs)
    ]


def load_extra(copies, page, refs, masks, target):
    share = refs[0].shape[1] - EXTRA
    return [
        copies.start(
            refs[place // (GROUPS // 2)].at[place % (GROUPS // 2), pl.ds(share, EXTRA)],
            target.at[jnp.bitwise_xor(page, number)],
        )
        for place, number in enumerate(places(masks))
    ]


def load_split(copies, page, refs, target):
    if len(refs) == 2:
        return load_chunk(copies, page, refs, FAR_X, target)
    split = refs[0].shape[2]
    count = target.shape[1]
    return load_chunk(copies, page, refs[:2], FAR_Z, target, 0, split) + load_chunk(
        copies, page, refs[2:], FAR_X, target, split, count
    )


def hot_columns(ids_ref, which, buckets):
    rows = ids_ref.shape[0]
    lane = lax.broadcasted_iota(jnp.int32, (rows, buckets), 1)
    return jnp.where(ids_ref[:, which : which + 1] == lane, 1.0, 0.0).astype(bf16)


def head_slices(head, width, size):
    query, key, space_query, space_key, value = [
        slice(which * width + head * size, which * width + (head + 1) * size) for which in range(5)
    ]
    return query, key, value, space_query, space_key


def table_pieces(heads, buckets):
    small = buckets // GROUPS
    for group in range(GROUPS):
        for side in range(2):
            for head in range(heads):
                start = (side * heads + head) * small
                yield group, side, head, slice(start, start + small)


def read_table(w_ref, heads, buckets, head, which):
    width = w_ref.shape[1] // 6
    share = w_ref.shape[0] // GROUPS
    column = 5 * width + which * (buckets // 2)
    sides = [[], []]
    for group, side, at, rows in table_pieces(heads, buckets):
        if at == head:
            rows = slice(group * share + rows.start, group * share + rows.stop)
            sides[side].append(w_ref[rows, column : column + buckets // 2])
    return jnp.concatenate([jnp.concatenate(side) for side in sides], axis=1)


def attend_kernel(batch, heads, last, page_ref, *refs):
    parts = 2 if last else 4
    rows_refs, w_refs, refs = refs[:4], refs[4 : 4 + parts], refs[4 + parts :]
    if last:
        o_refs, other_ref, refs = refs[:2], refs[2], refs[3:]
    idc_ref, idr_ref, proj_ref, prob_ref, head_ref, refs = refs[0], refs[1], refs[2], refs[3], refs[4], refs[5:]
    if last:
        keep_ref, send_ref, norms_ref, refs = refs[0], refs[1], refs[2], refs[3:]
        x_ref, s_ref, w_ref, wo_ref, extra_ref, sems = refs
    else:
        x_ref, s_ref, w_ref, sems = refs
    page = page_ref[0]
    copies = Copies(sems)
    started = load_rows(copies, rows_refs, x_ref, (0, batch)) + load_rows(copies, rows_refs, s_ref, (1, batch))
    started += load_split(copies, page, w_refs, w_ref)
    if last:
        rest = load_chunk(copies, page, o_refs, FAR_X, wo_ref)
        rest += load_extra(copies, page, o_refs, FAR_X, extra_ref)
    rows = x_ref.shape[0]
    width = w_ref.shape[1] // 6
    size = width // heads
    buckets = 2 * width // 3
    hots = [hot_columns(idc_ref, which, buckets) for which in range(3)]
    same = idc_ref[:, 3:4] == idr_ref[3:4, :]
    wait_all(started)
    proj_ref[:, : 2 * width] = dot(x_ref[...], w_ref[:, : 2 * width], AB).astype(bf16)
    proj_ref[:, 2 * width : 4 * width] = dot(s_ref[...], w_ref[:, 2 * width : 4 * width], AB).astype(bf16)
    proj_ref[:, 4 * width :] = dot(x_ref[...], w_ref[:, 4 * width : 5 * width], AB).astype(bf16)
    for head in range(heads):
        query, key, value, space_query, space_key = head_slices(head, width, size)
        tabled = [
            dot(hots[which], read_table(w_ref, heads, buckets, head, which), AB).astype(bf16) for which in range(3)
        ]
        left = jnp.concatenate(
            [proj_ref[:, query] * bf16(0.125), proj_ref[:, space_query] * bf16(0.125)] + tabled, axis=1
        )
        right = jnp.concatenate([proj_ref[:, key], proj_ref[:, space_key]] + hots, axis=1)
        score = jnp.where(same, dot(left, right, ABT), -1e30)
        weight = jnp.exp(score - jnp.max(score, axis=1, keepdims=True))
        prob = (weight * (1.0 / jnp.sum(weight, axis=1, keepdims=True))).astype(bf16)
        prob_ref[head] = prob
        head_ref[:, head * size : (head + 1) * size] = dot(prob, proj_ref[:, value], AB).astype(bf16)
    if last:
        wait_all(rest)
        part = dot(other_ref[...], wo_ref[:, :width], ABT) + dot(head_ref[...], wo_ref[:, width:], ABT)
        keep_ref[...] = part[: rows // 2]
        send_ref[...] = part[rows // 2 :].astype(bf16)
        inner = norms_ref.shape[1] // GROUPS
        for group in range(GROUPS):
            for which in range(norms_ref.shape[0]):
                norms_ref[which : which + 1, group * inner : (group + 1) * inner] = extra_ref[
                    group, 0:1, which * inner : (which + 1) * inner
                ].astype(f32)


def attend(batch, heads, page, row_parts, chunk, ids_col, ids_row, final=None):
    rows = ids_row.shape[1]
    features = row_parts[0].shape[-1]
    columns = sum(ref.shape[2] for ref in chunk[::2])
    width = columns // 6
    outs = (struct((rows, 5 * width), bf16), struct((heads, rows, rows), bf16), struct((rows, width), bf16))
    scratch = [pltpu.VMEM((rows, features), bf16)] * 2 + [pltpu.VMEM((features, columns), bf16)]
    more = ()
    if final is not None:
        pair_o, other = final
        more = (*pair_o, other)
        outs += (struct((rows // 2, features), f32), struct((rows // 2, features), bf16), struct((4, features), f32))
        scratch += [pltpu.VMEM((features, 2 * width), bf16), pltpu.VMEM((GROUPS, EXTRA, 2 * width), bf16)]
    return pl.pallas_call(
        functools.partial(attend_kernel, batch, heads, final is not None),
        in_specs=[SMEM] + [ANY] * (4 + len(chunk)) + ([] if final is None else [ANY, ANY, VM]) + [VM] * 2,
        out_shape=outs,
        scratch_shapes=scratch + [pltpu.SemaphoreType.DMA((8 + 4 * GROUPS,))],
        compiler_params=PARAMS,
        cost_estimate=cost(9),
        name="attend",
    )(page, *row_parts, *chunk, *more, ids_col, ids_row)


def attend_back_kernel(heads, half, page_ref, *refs):
    parts = 4 if half == 0 else 2
    da_refs, w_refs, o_refs, refs = refs[:4], refs[4 : 4 + parts], refs[4 + parts : 6 + parts], refs[6 + parts :]
    proj_ref, prob_ref, idc_ref, idr_ref, refs = refs[0], refs[1], refs[2], refs[3], refs[4:]
    if half == 0:
        other_ref, dproj_ref, dtable_ref, keep_ref, send_ref, refs = refs[0], refs[1], refs[2], refs[3], refs[4], refs[5:]
    else:
        dproj_ref, dtable_ref, part_ref, refs = refs[0], refs[1], refs[2], refs[3:]
    da_ref, w_ref, wo_ref, sems = refs
    page = page_ref[0]
    copies = Copies(sems)
    first = load_rows(copies, da_refs, da_ref) + load_chunk(copies, page, o_refs, FAR_X, wo_ref)
    last = load_split(copies, page, w_refs, w_ref)
    rows = da_ref.shape[0]
    width = w_ref.shape[1] // 6
    size = width // heads
    buckets = 2 * width // 3
    hots = [hot_columns(idc_ref, which, buckets) for which in range(3)]
    bucket = lax.broadcasted_iota(jnp.int32, (buckets, rows), 0)
    hots_t = [
        jnp.where(idr_ref[which : which + 1, :] == bucket, 1.0, 0.0).astype(bf16) for which in range(3)
    ]
    wait_all(first)
    grad_heads = dot(da_ref[...], wo_ref[:, half * width : (half + 1) * width], AB).astype(bf16)
    for head in range(heads):
        query, key, value, space_query, space_key = head_slices(head, width, size)
        prob = prob_ref[head]
        grad_out = grad_heads[:, head * size : (head + 1) * size]
        grad_prob = dot(grad_out, proj_ref[:, value], ABT)
        weighted = prob.astype(f32) * grad_prob
        row_dot = jnp.sum(weighted, axis=1, keepdims=True)
        grad_score = (weighted - prob.astype(f32) * row_dot).astype(bf16)
        dproj_ref[:, value] = dot(prob, grad_out, ATB).astype(bf16)
        right = jnp.concatenate([proj_ref[:, key], proj_ref[:, space_key]] + hots, axis=1)
        spread = dot(grad_score, right, AB)
        dproj_ref[:, query] = (spread[:, :size] * 0.125).astype(bf16)
        dproj_ref[:, space_query] = (spread[:, size : 2 * size] * 0.125).astype(bf16)
        left = jnp.concatenate([proj_ref[:, query], proj_ref[:, space_query]], axis=1)
        grad_keys = dot(grad_score, left, ATB) * 0.125
        dproj_ref[:, key] = grad_keys[:, :size].astype(bf16)
        dproj_ref[:, space_key] = grad_keys[:, size:].astype(bf16)
        for which in range(3):
            start = 2 * size + which * buckets
            piece = dot(hots_t[which], spread[:, start : start + buckets].astype(bf16), AB)
            small, wide = buckets // GROUPS, buckets // 2
            for group, side, at, place in table_pieces(heads, buckets):
                if at == head:
                    dtable_ref[group, place, which * wide : (which + 1) * wide] = piece[
                        group * small : (group + 1) * small, side * wide : (side + 1) * wide
                    ]
    wait_all(last)
    part = dot(dproj_ref[:, : 2 * width], w_ref[:, : 2 * width], ABT)
    part = part + dot(dproj_ref[:, 4 * width :], w_ref[:, 4 * width : 5 * width], ABT)
    if half == 0:
        part = part + other_ref[...]
        keep_ref[...] = part[: rows // 2]
        send_ref[...] = part[rows // 2 :].astype(bf16)
    else:
        part_ref[...] = part


def attend_back(heads, half, page, da_parts, chunk, pair_o, proj, prob, ids_col, ids_row, other=None):
    rows = ids_row.shape[1]
    features = da_parts[0].shape[-1]
    columns = sum(ref.shape[2] for ref in chunk[::2])
    width = columns // 6
    outs = (struct(proj.shape, bf16), struct((GROUPS, features // GROUPS, width), f32))
    if half == 0:
        outs += (struct((rows // 2, features), f32), struct((rows // 2, features), bf16))
    else:
        outs += (struct((rows, features), f32),)
    return pl.pallas_call(
        functools.partial(attend_back_kernel, heads, half),
        in_specs=[SMEM] + [ANY] * (6 + len(chunk)) + [VM] * (5 if half == 0 else 4),
        out_shape=outs,
        scratch_shapes=[
            pltpu.VMEM((rows, features), bf16),
            pltpu.VMEM((features, columns), bf16),
            pltpu.VMEM((features, 2 * width), bf16),
            pltpu.SemaphoreType.DMA((4 + 3 * GROUPS,)),
        ],
        compiler_params=PARAMS,
        cost_estimate=cost(9.5),
        name="attend_back",
    )(page, *da_parts, *chunk, *pair_o, proj, prob, ids_col, ids_row, *([other] if half == 0 else []))


def put_blocks(page, masks, full_ref, columns, keep_ref, send_ref):
    for place, number in enumerate(places(masks)):
        block = full_ref[jnp.bitwise_xor(page, number), :, columns]
        if place < GROUPS // 2:
            keep_ref[place] = block
        else:
            send_ref[place - GROUPS // 2] = block.astype(bf16)


def attn_weights_kernel(batches, split, page_ref, *refs):
    rows_refs, dproj_refs, dtable_refs = refs[:4], refs[4 : 4 + batches], refs[4 + batches : 4 + 2 * batches]
    out_refs, (x_ref, d_ref, full_ref, sems) = refs[4 + 2 * batches : -4], refs[-4:]
    page = page_ref[0]
    copies = Copies(sems)
    rows = x_ref.shape[1] // batches
    started = []
    for batch in range(batches):
        at = pl.ds(batch * rows, rows)
        for which in range(2):
            started += load_rows(copies, rows_refs, x_ref.at[which, at], (which, batch))
        started.append(copies.start(dproj_refs[batch], d_ref.at[at]))
    wait_all(started)
    width = d_ref.shape[1] // 5

    def blocks(value):
        return value.reshape(GROUPS, value.shape[0] // GROUPS, value.shape[1])

    x_t = x_ref[0].T
    full_ref[:, :, : 2 * width] = blocks(dot(x_t, d_ref[:, : 2 * width], AB))
    full_ref[:, :, 2 * width : 4 * width] = blocks(dot(x_ref[1].T, d_ref[:, 2 * width : 4 * width], AB))
    full_ref[:, :, 4 * width : 5 * width] = blocks(dot(x_t, d_ref[:, 4 * width :], AB))
    total = dtable_refs[0][...]
    for ref in dtable_refs[1:]:
        total = total + ref[...]
    full_ref[:, :, 5 * width :] = total
    if split:
        put_blocks(page, FAR_Z, full_ref, slice(0, split), *out_refs[:2])
    put_blocks(page, FAR_X, full_ref, slice(split, 6 * width), *out_refs[-2:])


def attn_weights(page, row_parts, dprojs, dtables, split):
    batches = len(dprojs)
    rows, columns = dprojs[0].shape
    columns = 6 * (columns // 5)
    features = row_parts[0].shape[-1]
    inner = features // GROUPS
    outs = ()
    for count in (split, columns - split) if split else (columns,):
        outs += (struct((GROUPS // 2, inner, count), f32), struct((GROUPS // 2, inner, count), bf16))
    return pl.pallas_call(
        functools.partial(attn_weights_kernel, batches, split),
        in_specs=[SMEM] + [ANY] * (4 + batches) + [VM] * batches,
        out_shape=outs,
        scratch_shapes=[
            pltpu.VMEM((2, batches * rows, features), bf16),
            pltpu.VMEM((batches * rows, dprojs[0].shape[1]), bf16),
            pltpu.VMEM((GROUPS, inner, columns), f32),
            pltpu.SemaphoreType.DMA((9 * batches,)),
        ],
        compiler_params=PARAMS,
        cost_estimate=cost(8),
        name="attn_weights",
    )(page, *row_parts, *dprojs, *dtables)


def out_weights_kernel(batches, page_ref, *refs):
    da_refs, head_refs, refs = refs[: 4 * batches], refs[4 * batches : 6 * batches], refs[6 * batches :]
    sums_refs, refs = refs[: 2 * batches], refs[2 * batches :]
    keep_ref, send_ref, da_ref, head_ref, full_ref, sems = refs
    page = page_ref[0]
    copies = Copies(sems)
    rows = da_ref.shape[0] // batches
    width = head_ref.shape[2]
    started = []
    for batch in range(batches):
        at = pl.ds(batch * rows, rows)
        started += load_rows(copies, da_refs[4 * batch : 4 * batch + 4], da_ref.at[at])
        for half in range(2):
            started.append(copies.start(head_refs[2 * batch + half], head_ref.at[half, at]))
    share = da_ref.shape[1] // GROUPS
    full_ref[:, share:, :] = jnp.zeros((GROUPS, EXTRA, 2 * width), f32)
    for layer in range(2):
        total = sums_refs[layer][...]
        for batch in range(1, batches):
            total = total + sums_refs[2 * batch + layer][...]
        for which in range(2):
            for group in range(GROUPS):
                start = (2 * which + layer) * share
                full_ref[group, share : share + 1, start : start + share] = total[
                    which : which + 1, group * share : (group + 1) * share
                ]
    wait_all(started)
    da_t = da_ref[...].T
    for half in range(2):
        full_ref[:, :share, half * width : (half + 1) * width] = dot(da_t, head_ref[half], AB).reshape(
            GROUPS, share, width
        )
    put_blocks(page, FAR_X, full_ref, slice(0, 2 * width), keep_ref, send_ref)


def out_weights(page, da_parts, head_rows, sums):
    batches = len(da_parts)
    rows, width = head_rows[0].shape
    features = da_parts[0][0].shape[-1]
    chunk = (GROUPS // 2, features // GROUPS + EXTRA, 2 * width)
    return pl.pallas_call(
        functools.partial(out_weights_kernel, batches),
        in_specs=[SMEM] + [ANY] * (6 * batches) + [VM] * (2 * batches),
        out_shape=(struct(chunk, f32), struct(chunk, bf16)),
        scratch_shapes=[
            pltpu.VMEM((batches * rows, features), bf16),
            pltpu.VMEM((2, batches * rows, width), bf16),
            pltpu.VMEM((GROUPS,) + chunk[1:], f32),
            pltpu.SemaphoreType.DMA((6 * batches,)),
        ],
        compiler_params=PARAMS,
        cost_estimate=cost(5),
        name="out_weights",
    )(page, *[ref for parts in da_parts for ref in parts], *head_rows, *sums)


def hidden_weights(refs):
    return jnp.concatenate([ref[...].reshape(-1, ref.shape[2]) for ref in refs])


def forward_kernel(own_ref, side_ref, *refs):
    f_refs, (act_ref, slope_ref, keep_ref, send_ref) = refs[:4], refs[4:]
    own, features = own_ref.shape
    rows = jnp.concatenate([own_ref[...], side_ref[...]])
    weight = hidden_weights(f_refs)
    pre = dot(rows, weight[:, :features], ABT)
    normal = 0.5 + 0.5 * lax.erf(pre * 0.7071067811865476)
    act = (pre * normal).astype(bf16)
    act_ref[...] = act
    slope_ref[...] = (normal + pre * jnp.exp(-0.5 * pre * pre) * 0.3989422804014327).astype(bf16)
    part = dot(act, weight[:, features:], AB)
    keep_ref[...] = part[:own]
    send_ref[...] = part[own:].astype(bf16)


def backward_kernel(own_ref, side_ref, *refs):
    f_refs, (act_ref, slope_ref, pre_ref, keep_ref, send_ref) = refs[:4], refs[4:]
    own, features = own_ref.shape
    rows = jnp.concatenate([own_ref[...], side_ref[...]])
    weight = hidden_weights(f_refs)
    grad_act = dot(rows, weight[:, features:], ABT)
    grad_pre = (grad_act * slope_ref[...].astype(f32)).astype(bf16)
    pre_ref[...] = grad_pre
    part = dot(grad_pre, weight[:, :features], AB)
    keep_ref[...] = part[:own]
    send_ref[...] = part[own:].astype(bf16)


def ff_call(kernel, name, parts, weights, saved):
    own, features = parts[0].shape
    hidden = sum(ref.shape[0] * ref.shape[1] for ref in weights)
    outs = (struct((2 * own, hidden), bf16),) * (1 if saved else 2)
    return pl.pallas_call(
        kernel,
        in_specs=[VM] * (6 + len(saved)),
        out_shape=outs + (struct((own, features), f32), struct((own, features), bf16)),
        compiler_params=PARAMS,
        cost_estimate=cost(5),
        name=name,
    )(*parts, *weights, *saved)


def ff_weights_kernel(batches, *refs):
    h_refs, g_refs = refs[: 2 * batches], refs[2 * batches : 4 * batches]
    pre_refs, act_refs = refs[4 * batches : 5 * batches], refs[5 * batches : 6 * batches]
    ours_ref, theirs_ref = refs[6 * batches :]
    features = ours_ref.shape[2]
    features = features // 2
    half = GROUPS * ours_ref.shape[1]
    shape = ours_ref.shape[:2] + (features,)
    for left_refs, right_refs, at in ((pre_refs, h_refs, 0), (act_refs, g_refs, features)):
        left = jnp.concatenate([ref[...] for ref in left_refs])
        right = jnp.concatenate([ref[...] for ref in right_refs])
        total = dot(left, right, ATB).astype(bf16)
        ours_ref[:, :, at : at + features] = total[:half].reshape(shape)
        theirs_ref[:, :, at : at + features] = total[half:].reshape(shape)


def ff_weights(h_parts, g_parts, grad_pres, acts):
    batches = len(acts)
    hidden = acts[0].shape[1]
    features = h_parts[0][0].shape[1]
    chunk = (GROUPS, hidden // (2 * GROUPS), 2 * features)
    return pl.pallas_call(
        functools.partial(ff_weights_kernel, batches),
        in_specs=[VM] * (6 * batches),
        out_shape=(struct(chunk, bf16), struct(chunk, bf16)),
        compiler_params=PARAMS,
        cost_estimate=cost(7),
        name="ff_weights",
    )(*[ref for parts in h_parts for ref in parts], *[ref for parts in g_parts for ref in parts], *grad_pres, *acts)


def normalize(value):
    centred = value - jnp.mean(value, axis=1, keepdims=True)
    scale = lax.rsqrt(jnp.mean(centred * centred, axis=1, keepdims=True) + EPS)
    return centred * scale, scale


def normalize_back(grad, normal, scale, gain):
    inner = grad * gain
    inner = inner - jnp.mean(inner, axis=1, keepdims=True) - normal * jnp.mean(inner * normal, axis=1, keepdims=True)
    return inner * scale


def norm_sums(grad, normal):
    gain = jnp.sum(grad * normal, axis=0, keepdims=True)
    shift = jnp.sum(grad, axis=0, keepdims=True)
    return jnp.concatenate([gain, shift], axis=0)


def norm_one_kernel(keep_ref, near_ref, far_ref, first_ref, second_ref, norms_ref, normal_ref, scale_ref, low_ref):
    value = first_ref[...].astype(f32) + second_ref[...].astype(f32)
    value = value + (keep_ref[...] + near_ref[...].astype(f32) + far_ref[...].astype(f32))
    normal, scale = normalize(value)
    normal_ref[...] = normal
    scale_ref[...] = scale
    low_ref[...] = (normal * norms_ref[0:1] + norms_ref[2:3]).astype(bf16)


def norm_two_kernel(keep_ref, far_ref, normal_ref, grad_ref, norms_ref, out_ref, dc_ref, dz_ref, sums_ref):
    value = normal_ref[...] * norms_ref[0:1] + norms_ref[2:3]
    value = value + (keep_ref[...] + far_ref[...].astype(f32))
    normal, scale = normalize(value)
    out_ref[...] = (normal * norms_ref[1:2] + norms_ref[3:4]).astype(bf16)
    grad = grad_ref[...].astype(f32)
    dc = normalize_back(grad, normal, scale, norms_ref[1:2])
    dc_ref[...] = dc
    dz_ref[...] = dc.astype(bf16)
    sums_ref[...] = norm_sums(grad, normal)


def norm_back_kernel(keep_ref, far_ref, dc_ref, normal_ref, scale_ref, norms_ref, da_ref, low_ref, sums_ref):
    grad = dc_ref[...] + (keep_ref[...] + far_ref[...].astype(f32))
    normal = normal_ref[...]
    da = normalize_back(grad, normal, scale_ref[...], norms_ref[0:1])
    da_ref[...] = da
    low_ref[...] = da.astype(bf16)
    sums_ref[...] = norm_sums(grad, normal)


def norm_call(kernel, name, outs, *args):
    return pl.pallas_call(kernel, in_specs=[VM] * len(args), out_shape=outs, cost_estimate=cost(2.4), name=name)(*args)


def local(
    tokens,
    spatial,
    box_coords,
    reading_order,
    page_len,
    w_attn,
    tables,
    w_out,
    ln_gain,
    ln_shift,
    w_up,
    w_down,
    grad_out,
):
    batches, own, features = tokens.shape[1:]
    rows = box_coords.shape[3]
    buckets = tables.shape[4]
    own_heads = tables.shape[2]
    heads = 2 * own_heads
    half = w_attn.shape[3]
    width = 2 * half
    share = w_attn.shape[2]
    step = tables.shape[3]
    coarse = COORD // buckets
    head_index = lax.axis_index("head")
    modality = head_index // 2
    pages = lax.axis_size("page")
    page_index = lax.axis_index("page")
    page = (page_index if direct() else page_index * 0).astype(jnp.int32).reshape(1)

    def mine(value):
        return lax.dynamic_index_in_dim(value, modality, 0, keepdims=False)

    def other(value):
        return lax.dynamic_index_in_dim(value, 1 - modality, 0, keepdims=False)

    def split_table(value):
        pieces = value.reshape(3, own_heads, step, 2, buckets // 2).transpose(3, 1, 2, 0, 4)
        return pieces.reshape(share, half)

    attn_own = mine(w_attn)
    chunk_a = jnp.concatenate([attn_own[which] for which in (0, 1, 3, 4, 2)] + [split_table(mine(tables))], axis=1)
    split = 5 * features // 6
    order = Order()
    turns = jnp.array([0, 2, 1, 3], jnp.int32)
    blocks = turns ^ head_index
    slots = jnp.take(turns, jnp.arange(4, dtype=jnp.int32) ^ head_index)
    one_a, two_a = Gather(order, chunk_a[:, :split], FAR_Z), Gather(order, chunk_a[:, split:], FAR_X)
    if direct():
        one_a.start()
        two_a.start()
    attn_got = order.swap(other(w_attn), "head", 2)
    table_got = order.swap(other(tables), "head", 2)
    out_got = order.swap(other(w_out), "head", 2)
    norms_own = order.tie(jnp.stack([ln_gain, ln_shift]))
    norms_head = jnp.take(jnp.stack(gather_rows(norms_own)), slots, axis=0)
    rows_own = jnp.stack([mine(tokens), mine(spatial)])
    if direct():
        one_a.step()
        two_a.step()
    rows_side = order.swap(jnp.stack([other(tokens), other(spatial)]), "head", 2)
    rows_near = order.swap(rows_own, "head", 1)
    chunk_b = jnp.concatenate([attn_got[which] for which in (0, 1, 3, 4, 2)] + [split_table(table_got)], axis=1)
    chunk_o = jnp.concatenate([mine(w_out), out_got]).T
    chunk_f = jnp.concatenate([w_up.T, w_down], axis=1)
    if direct():
        norms_row = norms_head.transpose(1, 2, 0, 3).reshape(1, -1)
        chunk_o = jnp.concatenate([chunk_o, jnp.pad(norms_row, ((0, EXTRA - 1), (0, 0)))])
        part_b, part_o, part_f = [Gather(order, chunk, FAR_X) for chunk in (chunk_b, chunk_o, chunk_f)]
        part_b.start()
        part_o.start()
        one_a.step()
        two_a.step()
        part_b.step()
        half_a = one_a.result() + two_a.result()
    else:
        half_a = generic_gather(chunk_a, 5 * half, 2 * own_heads)
        half_a = tuple(ref[..., :split] for ref in half_a) + tuple(ref[..., split:] for ref in half_a)
        half_b = generic_gather(chunk_b, 5 * half, 2 * own_heads)
        norms_full = by_page(gather_pages(norms_head)).transpose(2, 3, 0, 1, 4).reshape(4, GROUPS, 1, -1)
        norms_full = norms_full.transpose(1, 2, 0, 3).reshape(GROUPS, 1, -1)
        norms_full = jnp.pad(norms_full, ((0, 0), (0, EXTRA - 1), (0, 0)))
        pair_o = generic_gather(chunk_o)
        pair_o = tuple(
            jnp.concatenate([ref, extra], axis=1)
            for ref, extra in zip(pair_o, (norms_full[: GROUPS // 2], norms_full[GROUPS // 2 :]))
        )
        pair_f = generic_gather(chunk_f)
    row_parts = rows_own, rows_side, rows_near, order.swap(rows_side, "head", 1)

    ids = jnp.concatenate(
        [
            mine(reading_order)[None],
            mine(box_coords) // coarse,
            jnp.arange(rows, dtype=jnp.int32)[None, None] // page_len.reshape(1, batches, 1),
        ]
    )
    ids = jnp.take(ids.reshape(4, batches, 4, own), blocks, axis=2).reshape(4, batches, rows)

    state = [dict() for _ in range(batches)]
    if direct():
        part_b.step()
        gate_b = order.last
        part_o.step()
        part_f.start()
        part_o.step()
        part_f.step()
        gate_f = order.last
        part_f.step()
        gate_last = order.last
    else:
        gate_b = gate_f = gate_last = page
    for batch, here in enumerate(state):
        here["ids"] = ids[:, batch].T, ids[:, batch]
        here["proj_a"], here["prob_a"], here["head_a"] = attend(
            batch, own_heads, after(page, gate_b), row_parts, half_a, *here["ids"]
        )
        gate_b = here["head_a"], gate_f
    if direct():
        half_b, pair_o, pair_f = part_b.result(), part_o.result(), part_f.result()
    for batch, here in enumerate(state):
        here["proj_b"], here["prob_b"], here["head_b"], here["keep"], here["send"], norms = attend(
            batch, own_heads, after(page, gate_b, gate_last), row_parts, half_b, *here["ids"],
            final=(pair_o, here["head_a"]),
        )
        gate_b = here["head_b"]
    ff_parts = pair_f + tuple(swap(ref, "head", 1) for ref in pair_f)

    wide = struct((own, features), f32)
    low = struct((own, features), bf16)
    sums = struct((2, features), f32)
    for batch, here in enumerate(state):
        keep, near, far = scatter_rows(here["keep"], here["send"])
        here["normal"], here["scale"], hidden_low = norm_call(
            norm_one_kernel, "norm_one", (wide, struct((own, 1), f32), low),
            keep[:own], near[:own], far, tokens[0, batch], tokens[1, batch], norms,
        )
        here["h"] = hidden_low, swap(hidden_low, "head", 2)
        here["act"], here["slope"], keep, send = ff_call(forward_kernel, "forward", here["h"], ff_parts, ())
        here["out"], here["dc"], dz, here["sums_two"] = norm_call(
            norm_two_kernel, "norm_two", (low, wide, low, sums),
            keep, swap(send, "head", 2), here["normal"], grad_out[batch], norms,
        )
        here["g"] = dz, swap(dz, "head", 2)
        here["grad_pre"], keep, send = ff_call(
            backward_kernel, "backward", here["g"], ff_parts, (here["act"], here["slope"])
        )
        here["da"], da_low, here["sums_one"] = norm_call(
            norm_back_kernel, "norm_back", (wide, low, sums),
            keep, swap(send, "head", 2), here["dc"], here["normal"], here["scale"], norms,
        )
        here["a"] = gather_rows(da_low)

    def every(name):
        return [here[name] for here in state]

    order, later = Order(), Order()
    ours, theirs = ff_weights(every("h"), every("g"), every("grad_pre"), every("act"))
    theirs = later.swap(theirs, "head", 1)
    order.last = theirs

    def back_b(here):
        here["dproj_b"], here["dtable_b"], here["part"] = attend_back(
            own_heads, 1, order.tie(page), here["a"], half_b, pair_o, here["proj_b"], here["prob_b"], *here["ids"]
        )
        order.last = here["dproj_b"]

    def back_a(here):
        here["dproj_a"], here["dtable_a"], here["keep"], here["send"] = attend_back(
            own_heads, 0, order.tie(page), here["a"], half_a, pair_o, here["proj_a"], here["prob_a"], *here["ids"],
            here["part"],
        )
        order.last = here["dproj_a"]
        here["near"] = swap(here["send"], "head", 1)

    order.last = [here["a"][0] for here in state]
    back_b(state[0])
    ours = ours.astype(f32) + theirs.astype(f32)
    keep_f, send_f = ours[: GROUPS // 2], ours[GROUPS // 2 :].astype(bf16)
    part_f = Scatter(later, keep_f, send_f, FAR_X)
    if direct():
        part_f.start()
    keep_o, send_o = out_weights(
        order.tie(page),
        every("a"),
        [here[name] for here in state for name in ("head_a", "head_b")],
        [here[name] for here in state for name in ("sums_one", "sums_two")],
    )
    order.last = send_o, later.last
    part_o = Scatter(later, keep_o, send_o, FAR_X)
    if direct():
        part_o.start()
    for here in state[1:]:
        back_b(here)
    weights_b = attn_weights(order.tie(page), row_parts, every("dproj_b"), every("dtable_b"), 0)
    part_b = Scatter(later, *weights_b, FAR_X)
    if direct():
        part_f.step()
    order.last = weights_b[1], later.last
    if direct():
        part_b.start()
    back_a(state[0])
    if direct():
        part_o.step()
    order.last = order.last, later.last
    for here in state[1:]:
        back_a(here)
    if direct():
        part_f.step()
    order.last = order.last, later.last
    weights_a = attn_weights(order.tie(page), row_parts, every("dproj_a"), every("dtable_a"), split)
    if direct():
        part_o.step()
        part_b.step()
    one_a, two_a = Scatter(later, *weights_a[:2], FAR_Z), Scatter(later, *weights_a[2:], FAR_X)
    if direct():
        two_a.start()
        one_a.start()

    if direct():
        part_b.step()
        two_a.step()
        one_a.step()
        dff, dout, grad_b = part_f.result(), part_o.result(), part_b.result()
        two_a.step()
        one_a.step()
        grad_a = jnp.concatenate([one_a.result(), two_a.result()], axis=1)
        dnorms = dout[share].reshape(4, 4, -1).transpose(1, 0, 2)
        dout = dout[:share]
    else:
        inner = features // GROUPS
        dff = generic_scatter(keep_f, send_f)
        dout = generic_scatter(keep_o[:, :inner], send_o[:, :inner])
        flat = jnp.concatenate([keep_o[:, inner], send_o[:, inner].astype(f32)]).reshape(GROUPS, 4, -1)
        flat = flat.transpose(1, 0, 2).reshape(4, pages, 4, -1).transpose(1, 2, 0, 3)
        dnorms = scatter_pages(by_page(flat))
        grads = []
        for weights in (weights_a, weights_b):
            keep = jnp.concatenate(weights[::2], axis=2)
            send = jnp.concatenate(weights[1::2], axis=2)
            grads.append(generic_scatter(keep, send, 5 * half, 2 * own_heads))
        grad_a, grad_b = grads

    dnorms = jnp.take(dnorms, blocks, axis=0)
    pair = dnorms[:2] + swap(dnorms[2:], "head", 1)
    dnorms = (pair[0] + swap(pair[1], "head", 2)).reshape(2, 2, -1)

    def both_modalities(ours, theirs):
        got = swap(theirs.astype(bf16), "head", 2).astype(f32)
        return jnp.where(modality == 0, jnp.stack([ours, got]), jnp.stack([got, ours]))

    token_grads = []
    for here in state:
        total = here["keep"] + here["near"].astype(f32)
        token_grads.append(both_modalities(total[:own], total[own:]) + here["da"][None])

    got_b = swap(grad_b.astype(bf16), "head", 2).astype(f32)
    chunks = jnp.where(modality == 0, jnp.stack([grad_a, got_b]), jnp.stack([got_b, grad_a]))
    dattn = jnp.stack([chunks[:, :, which * half : (which + 1) * half] for which in (0, 1, 4, 2, 3)], axis=1)
    dtable = chunks[:, :, 5 * half :].reshape(2, 2, own_heads, step, 3, buckets // 2)
    dtable = dtable.transpose(0, 4, 2, 3, 1, 5).reshape(2, 3, own_heads, step, buckets)
    dout = dout.reshape(share, 2, half).transpose(1, 2, 0)
    return (
        jnp.stack([here["out"] for here in state]),
        jnp.stack(token_grads, axis=1).astype(bf16),
        dattn,
        dtable,
        both_modalities(dout[0], dout[1]),
        dnorms[0],
        dnorms[1],
        dff[:, :features].T,
        dff[:, features:],
    )


def solution(mesh):
    return jax.shard_map(
        local,
        mesh=mesh,
        in_specs=(
            P(None, None, ("page", "head"), None),
            P(None, None, ("page", "head"), None),
            P(None, None, None, "page"),
            P(None, None, "page"),
            P(None, "page"),
            P(None, None, "page", "head"),
            P(None, None, "head", "page", None),
            P(None, "head", "page"),
            P(None, ("page", "head")),
            P(None, ("page", "head")),
            P(None, ("page", "head")),
            P(("page", "head"), None),
            P(None, ("page", "head"), None),
        ),
        out_specs=(
            P(None, ("page", "head"), None),
            P(None, None, ("page", "head"), None),
            P(None, None, "page", "head"),
            P(None, None, "head", "page", None),
            P(None, "head", "page"),
            P(None, ("page", "head")),
            P(None, ("page", "head")),
            P(None, ("page", "head")),
            P(("page", "head"), None),
        ),
        check_vma=False,
    )
```

```python
import functools

import jax
import jax.numpy as jnp
from jax import lax
from jax.experimental import pallas as pl
from jax.experimental.pallas import tpu as pltpu
from jax.sharding import PartitionSpec as P

COORD = 1024
EPS = 1e-05
GROUPS = 8
SCALE = 5e8
EXTRA = 16
f32 = jnp.float32
bf16 = jnp.bfloat16
AB = ((1,), (0,))
ABT = ((1,), (1,))
ATB = ((0,), (0,))
SMEM = pl.BlockSpec(memory_space=pltpu.SMEM)
ANY = VM = pl.BlockSpec(memory_space=pltpu.VMEM)
PARAMS = pltpu.CompilerParams(vmem_limit_bytes=14 * 1024 * 1024)
FAR_X = (4, 2, 1)
FAR_Z = (4, 1, 2)


def cost(microseconds):
    return pl.CostEstimate(
        flops=int(microseconds * SCALE), bytes_accessed=int(microseconds * 3e5), transcendentals=0
    )


def struct(shape, kind):
    return pltpu.VMEM(tuple(shape), kind)


def pin(*values):
    return [pltpu.with_memory_space_constraint(value, pltpu.VMEM) for value in values]


def dot(left, right, dims):
    return lax.dot_general(left, right, (dims, ((), ())), preferred_element_type=f32)


def swap(value, axis, mask):
    count = lax.axis_size(axis)
    return lax.ppermute(value, axis, [(place, place ^ mask) for place in range(count)])


def after(value, *earlier):
    return lax.optimization_barrier((value, earlier))[0]


def gather_rows(own):
    side = swap(own, "head", 2)
    return own, side, swap(own, "head", 1), swap(side, "head", 1)


def scatter_rows(keep, send):
    own = keep.shape[0] // 2
    near = swap(send, "head", 1)
    far = swap((keep[own:] + near[own:].astype(f32)).astype(bf16), "head", 2)
    return keep, near, far


def page_bits():
    count = lax.axis_size("page")
    return [1 << bit for bit in reversed(range(count.bit_length() - 1))]


def gather_pages(own):
    full = own
    for depth, mask in enumerate(page_bits()):
        full = jnp.stack([full, swap(full, "page", mask)], axis=depth)
    return full.reshape((lax.axis_size("page"),) + own.shape)


def scatter_pages(blocks):
    masks = page_bits()
    part = blocks.reshape((2,) * len(masks) + blocks.shape[1:])
    for depth in reversed(range(len(masks))):
        keep = lax.index_in_dim(part, 0, depth, keepdims=False)
        send = lax.index_in_dim(part, 1, depth, keepdims=False)
        part = keep.astype(f32) + swap(send.astype(bf16), "page", masks[depth]).astype(f32)
    return part


def by_page(blocks):
    count = blocks.shape[0]
    order = jnp.arange(count, dtype=jnp.int32) ^ lax.axis_index("page")
    return jnp.take(blocks, order, axis=0)


def regroup(full, heads):
    pages, share, columns = full.shape
    if heads == 1:
        return full.reshape(GROUPS, -1, columns)
    parts = full.reshape(GROUPS, pages // GROUPS, heads, share // heads, columns)
    return parts.transpose(0, 2, 1, 3, 4).reshape(GROUPS, -1, columns)


def ungroup(full, pages, heads):
    columns = full.shape[2]
    if heads == 1:
        return full.reshape(pages, -1, columns)
    parts = full.reshape(GROUPS, heads, pages // GROUPS, -1, columns)
    return parts.transpose(0, 2, 1, 3, 4).reshape(pages, -1, columns)


def direct():
    return lax.axis_size("page") == GROUPS


def join_kernel(first_ref, second_ref, out_ref):
    half = first_ref.shape[0]
    out_ref[:half] = first_ref[...]
    out_ref[half:] = second_ref[...]


def join(first, second):
    return pl.pallas_call(
        join_kernel,
        in_specs=[VM] * 2,
        out_shape=struct((2 * first.shape[0],) + first.shape[1:], first.dtype),
        compiler_params=PARAMS,
        cost_estimate=cost(0.4),
        name="join",
    )(*pin(first, second))


def fold_kernel(first_ref, second_ref, keep_ref, send_ref):
    half = keep_ref.shape[0]
    keep_ref[...] = first_ref[:half].astype(f32) + second_ref[:half].astype(f32)
    send_ref[...] = (first_ref[half:].astype(f32) + second_ref[half:].astype(f32)).astype(bf16)


def fold(first, second):
    half = (first.shape[0] // 2,) + first.shape[1:]
    return pl.pallas_call(
        fold_kernel,
        in_specs=[VM] * 2,
        out_shape=(struct(half, f32), struct(half, bf16)),
        compiler_params=PARAMS,
        cost_estimate=cost(0.6),
        name="fold",
    )(*pin(first, second))


class Gather:
    def __init__(self, share, masks):
        self.part, self.masks = share[None], list(masks)

    def start(self, *earlier):
        self.part = after(self.part, *earlier)
        self.got = swap(self.part, "page", self.masks.pop(0))

    def step(self, *earlier):
        self.part = join(self.part, after(self.got, *earlier))
        self.start(*earlier)

    def result(self):
        return self.part, self.got


def generic_gather(share, columns=None, heads=1):
    full = by_page(gather_pages(share))
    if heads == 1:
        full = regroup(full, 1)
    else:
        full = jnp.concatenate([regroup(full[..., :columns], 1), regroup(full[..., columns:], heads)], axis=2)
    return full[: GROUPS // 2], full[GROUPS // 2 :]


class Scatter:
    def __init__(self, keep, send, masks):
        self.keep, self.send, self.masks = keep, send, list(masks)

    def start(self, *earlier):
        self.send = after(self.send, *earlier)
        self.got = swap(self.send, "page", self.masks.pop())

    def step(self, *earlier):
        self.keep, self.send = fold(self.keep, after(self.got, *earlier))
        self.start(*earlier)

    def result(self, *earlier):
        return self.keep[0] + after(self.got, *earlier)[0].astype(f32)


def generic_scatter(keep, send, columns=None, heads=1):
    pages = lax.axis_size("page")
    full = jnp.concatenate([keep.astype(bf16), send])
    if heads == 1:
        full = ungroup(full, pages, 1)
    else:
        full = jnp.concatenate(
            [ungroup(full[..., :columns], pages, 1), ungroup(full[..., columns:], pages, heads)], axis=2
        )
    return scatter_pages(by_page(full))


def places(masks):
    if not direct():
        masks = (1, 2, 4)
    return [
        sum(mask for bit, mask in enumerate(masks) if (place >> bit) & 1) for place in range(GROUPS)
    ]


def load_chunk(page, refs, masks, target, start=0):
    share = target.shape[0] // GROUPS
    stop = start + refs[0].shape[2]
    for place, number in enumerate(places(masks)):
        row = pl.multiple_of(jnp.bitwise_xor(page, number) * share, share)
        target[pl.ds(row, share), start:stop] = refs[place // (GROUPS // 2)][place % (GROUPS // 2), :share]


def load_rows(refs, target, *pick):
    count = refs[0].shape[-2]
    for place, ref in enumerate(refs):
        target[place * count : (place + 1) * count] = ref[pick] if pick else ref[...]


def load_extra(page, refs, masks, target):
    share = refs[0].shape[1] - EXTRA
    for place, number in enumerate(places(masks)):
        target[jnp.bitwise_xor(page, number)] = refs[place // (GROUPS // 2)][place % (GROUPS // 2), share:]


def load_split(page, refs, target):
    if len(refs) == 2:
        load_chunk(page, refs, FAR_X, target)
    else:
        load_chunk(page, refs[:2], FAR_Z, target)
        load_chunk(page, refs[2:], FAR_X, target, refs[0].shape[2])


def turned(ids_ref):
    ids = ids_ref[...].astype(f32)
    return jnp.concatenate([ids, ids]).T


def hot_columns(ids, which, buckets):
    lane = lax.broadcasted_iota(jnp.int32, (ids.shape[0], buckets), 1).astype(f32)
    return jnp.where(ids[:, which : which + 1] == lane, 1.0, 0.0).astype(bf16)


def head_slices(head, width, size):
    query, key, space_query, space_key, value = [
        slice(which * width + head * size, which * width + (head + 1) * size) for which in range(5)
    ]
    return query, key, value, space_query, space_key


def table_pieces(heads, buckets):
    small = buckets // GROUPS
    for group in range(GROUPS):
        for side in range(2):
            for head in range(heads):
                start = (side * heads + head) * small
                yield group, side, head, slice(start, start + small)


def read_table(w_ref, heads, buckets, head, which):
    width = w_ref.shape[1] // 6
    share = w_ref.shape[0] // GROUPS
    column = 5 * width + which * (buckets // 2)
    sides = [[], []]
    for group, side, at, rows in table_pieces(heads, buckets):
        if at == head:
            rows = slice(group * share + rows.start, group * share + rows.stop)
            sides[side].append(w_ref[rows, column : column + buckets // 2])
    return jnp.concatenate([jnp.concatenate(side) for side in sides], axis=1)


def attend_kernel(batch, heads, last, page_ref, *refs):
    parts = 2 if last else 4
    rows_refs, w_refs, refs = refs[:4], refs[4 : 4 + parts], refs[4 + parts :]
    if last:
        o_refs, other_ref, refs = refs[:2], refs[2], refs[3:]
    idr_ref, proj_ref, prob_ref, head_ref, refs = refs[0], refs[1], refs[2], refs[3], refs[4:]
    if last:
        keep_ref, send_ref, norms_ref, refs = refs[0], refs[1], refs[2], refs[3:]
        x_ref, s_ref, w_ref, wo_ref, extra_ref = refs
    else:
        x_ref, s_ref, w_ref = refs
    page = page_ref[0]
    load_rows(rows_refs, x_ref, 0, batch)
    load_rows(rows_refs, s_ref, 1, batch)
    load_split(page, w_refs, w_ref)
    rows = x_ref.shape[0]
    width = w_ref.shape[1] // 6
    size = width // heads
    buckets = 2 * width // 3
    columns = turned(idr_ref)
    hots = [hot_columns(columns, which, buckets) for which in range(3)]
    same = columns[:, 3:4] == idr_ref[3:4, :].astype(f32)
    proj_ref[:, : 2 * width] = dot(x_ref[...], w_ref[:, : 2 * width], AB).astype(bf16)
    proj_ref[:, 2 * width : 4 * width] = dot(s_ref[...], w_ref[:, 2 * width : 4 * width], AB).astype(bf16)
    proj_ref[:, 4 * width :] = dot(x_ref[...], w_ref[:, 4 * width : 5 * width], AB).astype(bf16)
    for head in range(heads):
        query, key, value, space_query, space_key = head_slices(head, width, size)
        tabled = [
            dot(hots[which], read_table(w_ref, heads, buckets, head, which), AB).astype(bf16) for which in range(3)
        ]
        left = jnp.concatenate(
            [proj_ref[:, query] * bf16(0.125), proj_ref[:, space_query] * bf16(0.125)] + tabled, axis=1
        )
        right = jnp.concatenate([proj_ref[:, key], proj_ref[:, space_key]] + hots, axis=1)
        score = jnp.where(same, dot(left, right, ABT), -1e30)
        weight = jnp.exp(score - jnp.max(score, axis=1, keepdims=True))
        prob = (weight * (1.0 / jnp.sum(weight, axis=1, keepdims=True))).astype(bf16)
        prob_ref[head] = prob
        head_ref[:, head * size : (head + 1) * size] = dot(prob, proj_ref[:, value], AB).astype(bf16)
    if last:
        load_chunk(page, o_refs, FAR_Z, wo_ref)
        load_extra(page, o_refs, FAR_Z, extra_ref)
        part = dot(other_ref[...], wo_ref[:, :width], ABT) + dot(head_ref[...], wo_ref[:, width:], ABT)
        keep_ref[...] = part[: rows // 2]
        send_ref[...] = part[rows // 2 :].astype(bf16)
        inner = norms_ref.shape[1] // GROUPS
        for group in range(GROUPS):
            for which in range(norms_ref.shape[0]):
                norms_ref[which : which + 1, group * inner : (group + 1) * inner] = extra_ref[
                    group, 0:1, which * inner : (which + 1) * inner
                ].astype(f32)


def attend(batch, heads, page, row_parts, chunk, ids_row, final=None):
    rows = ids_row.shape[1]
    features = row_parts[0].shape[-1]
    columns = sum(ref.shape[2] for ref in chunk[::2])
    width = columns // 6
    outs = (struct((rows, 5 * width), bf16), struct((heads, rows, rows), bf16), struct((rows, width), bf16))
    scratch = [pltpu.VMEM((rows, features), bf16)] * 2 + [pltpu.VMEM((features, columns), bf16)]
    more = ()
    if final is not None:
        pair_o, other = final
        more = (*pair_o, other)
        outs += (struct((rows // 2, features), f32), struct((rows // 2, features), bf16), struct((4, features), f32))
        scratch += [pltpu.VMEM((features, 2 * width), bf16), pltpu.VMEM((GROUPS, EXTRA, 2 * width), bf16)]
    return pl.pallas_call(
        functools.partial(attend_kernel, batch, heads, final is not None),
        in_specs=[SMEM] + [ANY] * (4 + len(chunk)) + ([] if final is None else [ANY, ANY, VM]) + [VM],
        out_shape=outs,
        scratch_shapes=scratch,
        compiler_params=PARAMS,
        cost_estimate=cost(6.3),
        name="attend",
    )(page, *pin(*row_parts, *chunk, *more, ids_row))


def attend_back_kernel(heads, half, page_ref, *refs):
    parts = 4 if half == 0 else 2
    da_refs, w_refs, o_refs, refs = refs[:4], refs[4 : 4 + parts], refs[4 + parts : 6 + parts], refs[6 + parts :]
    proj_ref, prob_ref, idr_ref, refs = refs[0], refs[1], refs[2], refs[3:]
    if half == 0:
        other_ref, dproj_ref, dtable_ref, keep_ref, send_ref, refs = refs[0], refs[1], refs[2], refs[3], refs[4], refs[5:]
    else:
        dproj_ref, dtable_ref, part_ref, refs = refs[0], refs[1], refs[2], refs[3:]
    da_ref, w_ref, wo_ref = refs
    page = page_ref[0]
    load_rows(da_refs, da_ref)
    load_chunk(page, o_refs, FAR_Z, wo_ref)
    load_split(page, w_refs, w_ref)
    rows = da_ref.shape[0]
    width = w_ref.shape[1] // 6
    size = width // heads
    buckets = 2 * width // 3
    columns = turned(idr_ref)
    hots = [hot_columns(columns, which, buckets) for which in range(3)]
    bucket = lax.broadcasted_iota(jnp.int32, (buckets, rows), 0)
    hots_t = [
        jnp.where(idr_ref[which : which + 1, :] == bucket, 1.0, 0.0).astype(bf16) for which in range(3)
    ]
    grad_heads = dot(da_ref[...], wo_ref[:, half * width : (half + 1) * width], AB).astype(bf16)
    for head in range(heads):
        query, key, value, space_query, space_key = head_slices(head, width, size)
        prob = prob_ref[head]
        grad_out = grad_heads[:, head * size : (head + 1) * size]
        grad_prob = dot(grad_out, proj_ref[:, value], ABT)
        weighted = prob.astype(f32) * grad_prob
        row_dot = jnp.sum(weighted, axis=1, keepdims=True)
        grad_score = (weighted - prob.astype(f32) * row_dot).astype(bf16)
        dproj_ref[:, value] = dot(prob, grad_out, ATB).astype(bf16)
        right = jnp.concatenate([proj_ref[:, key], proj_ref[:, space_key]] + hots, axis=1)
        spread = dot(grad_score, right, AB)
        dproj_ref[:, query] = (spread[:, :size] * 0.125).astype(bf16)
        dproj_ref[:, space_query] = (spread[:, size : 2 * size] * 0.125).astype(bf16)
        left = jnp.concatenate([proj_ref[:, query], proj_ref[:, space_query]], axis=1)
        grad_keys = dot(grad_score, left, ATB) * 0.125
        dproj_ref[:, key] = grad_keys[:, :size].astype(bf16)
        dproj_ref[:, space_key] = grad_keys[:, size:].astype(bf16)
        for which in range(3):
            start = 2 * size + which * buckets
            piece = dot(hots_t[which], spread[:, start : start + buckets].astype(bf16), AB)
            small, wide = buckets // GROUPS, buckets // 2
            for group, side, at, place in table_pieces(heads, buckets):
                if at == head:
                    dtable_ref[group, place, which * wide : (which + 1) * wide] = piece[
                        group * small : (group + 1) * small, side * wide : (side + 1) * wide
                    ]
    part = dot(dproj_ref[:, : 2 * width], w_ref[:, : 2 * width], ABT)
    part = part + dot(dproj_ref[:, 4 * width :], w_ref[:, 4 * width : 5 * width], ABT)
    if half == 0:
        part = part + other_ref[...]
        keep_ref[...] = part[: rows // 2]
        send_ref[...] = part[rows // 2 :].astype(bf16)
    else:
        part_ref[...] = part


def attend_back(heads, half, page, da_parts, chunk, pair_o, proj, prob, ids_row, other=None):
    rows = ids_row.shape[1]
    features = da_parts[0].shape[-1]
    columns = sum(ref.shape[2] for ref in chunk[::2])
    width = columns // 6
    outs = (struct(proj.shape, bf16), struct((GROUPS, features // GROUPS, width), f32))
    if half == 0:
        outs += (struct((rows // 2, features), f32), struct((rows // 2, features), bf16))
    else:
        outs += (struct((rows, features), f32),)
    return pl.pallas_call(
        functools.partial(attend_back_kernel, heads, half),
        in_specs=[SMEM] + [ANY] * (6 + len(chunk)) + [VM] * (4 if half == 0 else 3),
        out_shape=outs,
        scratch_shapes=[
            pltpu.VMEM((rows, features), bf16),
            pltpu.VMEM((features, columns), bf16),
            pltpu.VMEM((features, 2 * width), bf16),
        ],
        compiler_params=PARAMS,
        cost_estimate=cost(6),
        name="attend_back",
    )(page, *pin(*da_parts, *chunk, *pair_o, proj, prob, ids_row, *([other] if half == 0 else [])))


def put_blocks(page, masks, full_ref, columns, keep_ref, send_ref):
    for place, number in enumerate(places(masks)):
        block = full_ref[jnp.bitwise_xor(page, number), :, columns]
        if place < GROUPS // 2:
            keep_ref[place] = block
        else:
            send_ref[place - GROUPS // 2] = block.astype(bf16)


def attn_weights_kernel(batches, split, page_ref, *refs):
    rows_refs, dproj_refs, dtable_refs = refs[:4], refs[4 : 4 + batches], refs[4 + batches : 4 + 2 * batches]
    out_refs, (x_ref, d_ref, full_ref) = refs[4 + 2 * batches : -3], refs[-3:]
    page = page_ref[0]
    rows = x_ref.shape[1] // batches
    for batch in range(batches):
        at = pl.ds(batch * rows, rows)
        for which in range(2):
            load_rows(rows_refs, x_ref.at[which, at], which, batch)
        d_ref[at] = dproj_refs[batch][...]
    width = d_ref.shape[1] // 5

    def blocks(value):
        return value.reshape(GROUPS, value.shape[0] // GROUPS, value.shape[1])

    x_t = x_ref[0].T
    full_ref[:, :, : 2 * width] = blocks(dot(x_t, d_ref[:, : 2 * width], AB))
    full_ref[:, :, 2 * width : 4 * width] = blocks(dot(x_ref[1].T, d_ref[:, 2 * width : 4 * width], AB))
    full_ref[:, :, 4 * width : 5 * width] = blocks(dot(x_t, d_ref[:, 4 * width :], AB))
    total = dtable_refs[0][...]
    for ref in dtable_refs[1:]:
        total = total + ref[...]
    full_ref[:, :, 5 * width :] = total
    if split:
        put_blocks(page, FAR_Z, full_ref, slice(0, split), *out_refs[:2])
    put_blocks(page, FAR_X, full_ref, slice(split, 6 * width), *out_refs[-2:])


def attn_weights(page, row_parts, dprojs, dtables, split):
    batches = len(dprojs)
    rows, columns = dprojs[0].shape
    columns = 6 * (columns // 5)
    features = row_parts[0].shape[-1]
    inner = features // GROUPS
    outs = ()
    for count in (split, columns - split) if split else (columns,):
        outs += (struct((GROUPS // 2, inner, count), f32), struct((GROUPS // 2, inner, count), bf16))
    return pl.pallas_call(
        functools.partial(attn_weights_kernel, batches, split),
        in_specs=[SMEM] + [ANY] * (4 + batches) + [VM] * batches,
        out_shape=outs,
        scratch_shapes=[
            pltpu.VMEM((2, batches * rows, features), bf16),
            pltpu.VMEM((batches * rows, dprojs[0].shape[1]), bf16),
            pltpu.VMEM((GROUPS, inner, columns), f32),
        ],
        compiler_params=PARAMS,
        cost_estimate=cost(4.8),
        name="attn_weights",
    )(page, *pin(*row_parts, *dprojs, *dtables))


def out_weights_kernel(batches, page_ref, *refs):
    da_refs, head_refs, refs = refs[: 4 * batches], refs[4 * batches : 6 * batches], refs[6 * batches :]
    sums_refs, refs = refs[: 2 * batches], refs[2 * batches :]
    keep_ref, send_ref, da_ref, head_ref, full_ref = refs
    page = page_ref[0]
    rows = da_ref.shape[0] // batches
    width = head_ref.shape[2]
    for batch in range(batches):
        at = pl.ds(batch * rows, rows)
        load_rows(da_refs[4 * batch : 4 * batch + 4], da_ref.at[at])
        for half in range(2):
            head_ref[half, at] = head_refs[2 * batch + half][...]
    share = da_ref.shape[1] // GROUPS
    full_ref[:, share:, :] = jnp.zeros((GROUPS, EXTRA, 2 * width), f32)
    for layer in range(2):
        total = sums_refs[layer][...]
        for batch in range(1, batches):
            total = total + sums_refs[2 * batch + layer][...]
        for which in range(2):
            for group in range(GROUPS):
                start = (2 * which + layer) * share
                full_ref[group, share : share + 1, start : start + share] = total[
                    which : which + 1, group * share : (group + 1) * share
                ]
    da_t = da_ref[...].T
    for half in range(2):
        full_ref[:, :share, half * width : (half + 1) * width] = dot(da_t, head_ref[half], AB).reshape(
            GROUPS, share, width
        )
    put_blocks(page, FAR_X, full_ref, slice(0, 2 * width), keep_ref, send_ref)


def out_weights(page, da_parts, head_rows, sums):
    batches = len(da_parts)
    rows, width = head_rows[0].shape
    features = da_parts[0][0].shape[-1]
    chunk = (GROUPS // 2, features // GROUPS + EXTRA, 2 * width)
    return pl.pallas_call(
        functools.partial(out_weights_kernel, batches),
        in_specs=[SMEM] + [ANY] * (6 * batches) + [VM] * (2 * batches),
        out_shape=(struct(chunk, f32), struct(chunk, bf16)),
        scratch_shapes=[
            pltpu.VMEM((batches * rows, features), bf16),
            pltpu.VMEM((2, batches * rows, width), bf16),
            pltpu.VMEM((GROUPS,) + chunk[1:], f32),
        ],
        compiler_params=PARAMS,
        cost_estimate=cost(2.7),
        name="out_weights",
    )(page, *pin(*[ref for parts in da_parts for ref in parts], *head_rows, *sums))


def hidden_weights(refs):
    return jnp.concatenate([ref[...].reshape(-1, ref.shape[2]) for ref in refs])


def forward_kernel(own_ref, side_ref, *refs):
    f_refs, (act_ref, slope_ref, keep_ref, send_ref) = refs[:4], refs[4:]
    own, features = own_ref.shape
    rows = jnp.concatenate([own_ref[...], side_ref[...]])
    weight = hidden_weights(f_refs)
    pre = dot(rows, weight[:, :features], ABT)
    normal = 0.5 + 0.5 * lax.erf(pre * 0.7071067811865476)
    act = (pre * normal).astype(bf16)
    act_ref[...] = act
    slope_ref[...] = (normal + pre * jnp.exp(-0.5 * pre * pre) * 0.3989422804014327).astype(bf16)
    part = dot(act, weight[:, features:], AB)
    keep_ref[...] = part[:own]
    send_ref[...] = part[own:].astype(bf16)


def backward_kernel(own_ref, side_ref, *refs):
    f_refs, (act_ref, slope_ref, pre_ref, keep_ref, send_ref) = refs[:4], refs[4:]
    own, features = own_ref.shape
    rows = jnp.concatenate([own_ref[...], side_ref[...]])
    weight = hidden_weights(f_refs)
    grad_act = dot(rows, weight[:, features:], ABT)
    grad_pre = (grad_act * slope_ref[...].astype(f32)).astype(bf16)
    pre_ref[...] = grad_pre
    part = dot(grad_pre, weight[:, :features], AB)
    keep_ref[...] = part[:own]
    send_ref[...] = part[own:].astype(bf16)


def ff_call(kernel, name, parts, weights, saved):
    own, features = parts[0].shape
    hidden = sum(ref.shape[0] * ref.shape[1] for ref in weights)
    outs = (struct((2 * own, hidden), bf16),) * (1 if saved else 2)
    return pl.pallas_call(
        kernel,
        in_specs=[VM] * (6 + len(saved)),
        out_shape=outs + (struct((own, features), f32), struct((own, features), bf16)),
        compiler_params=PARAMS,
        cost_estimate=cost(1.8),
        name=name,
    )(*pin(*parts, *weights, *saved))


def ff_weights_kernel(batches, *refs):
    h_refs, g_refs = refs[: 2 * batches], refs[2 * batches : 4 * batches]
    pre_refs, act_refs = refs[4 * batches : 5 * batches], refs[5 * batches : 6 * batches]
    ours_ref, theirs_ref = refs[6 * batches :]
    features = ours_ref.shape[2]
    features = features // 2
    half = GROUPS * ours_ref.shape[1]
    shape = ours_ref.shape[:2] + (features,)
    for left_refs, right_refs, at in ((pre_refs, h_refs, 0), (act_refs, g_refs, features)):
        left = jnp.concatenate([ref[...] for ref in left_refs])
        right = jnp.concatenate([ref[...] for ref in right_refs])
        total = dot(left, right, ATB).astype(bf16)
        ours_ref[:, :, at : at + features] = total[:half].reshape(shape)
        theirs_ref[:, :, at : at + features] = total[half:].reshape(shape)


def ff_weights(h_parts, g_parts, grad_pres, acts):
    batches = len(acts)
    hidden = acts[0].shape[1]
    features = h_parts[0][0].shape[1]
    chunk = (GROUPS, hidden // (2 * GROUPS), 2 * features)
    return pl.pallas_call(
        functools.partial(ff_weights_kernel, batches),
        in_specs=[VM] * (6 * batches),
        out_shape=(struct(chunk, bf16), struct(chunk, bf16)),
        compiler_params=PARAMS,
        cost_estimate=cost(4.2),
        name="ff_weights",
    )(*pin(*[ref for parts in h_parts + g_parts for ref in parts], *grad_pres, *acts))


def normalize(value):
    centred = value - jnp.mean(value, axis=1, keepdims=True)
    scale = lax.rsqrt(jnp.mean(centred * centred, axis=1, keepdims=True) + EPS)
    return centred * scale, scale


def normalize_back(grad, normal, scale, gain):
    inner = grad * gain
    inner = inner - jnp.mean(inner, axis=1, keepdims=True) - normal * jnp.mean(inner * normal, axis=1, keepdims=True)
    return inner * scale


def norm_sums(grad, normal):
    gain = jnp.sum(grad * normal, axis=0, keepdims=True)
    shift = jnp.sum(grad, axis=0, keepdims=True)
    return jnp.concatenate([gain, shift], axis=0)


def norm_one_kernel(keep_ref, near_ref, far_ref, first_ref, second_ref, norms_ref, normal_ref, scale_ref, low_ref):
    value = first_ref[...].astype(f32) + second_ref[...].astype(f32)
    value = value + (keep_ref[...] + near_ref[...].astype(f32) + far_ref[...].astype(f32))
    normal, scale = normalize(value)
    normal_ref[...] = normal
    scale_ref[...] = scale
    low_ref[...] = (normal * norms_ref[0:1] + norms_ref[2:3]).astype(bf16)


def norm_two_kernel(keep_ref, far_ref, normal_ref, grad_ref, norms_ref, out_ref, dc_ref, dz_ref, sums_ref):
    value = normal_ref[...] * norms_ref[0:1] + norms_ref[2:3]
    value = value + (keep_ref[...] + far_ref[...].astype(f32))
    normal, scale = normalize(value)
    out_ref[...] = (normal * norms_ref[1:2] + norms_ref[3:4]).astype(bf16)
    grad = grad_ref[...].astype(f32)
    dc = normalize_back(grad, normal, scale, norms_ref[1:2])
    dc_ref[...] = dc
    dz_ref[...] = dc.astype(bf16)
    sums_ref[...] = norm_sums(grad, normal)


def norm_back_kernel(keep_ref, far_ref, dc_ref, normal_ref, scale_ref, norms_ref, da_ref, low_ref, sums_ref):
    grad = dc_ref[...] + (keep_ref[...] + far_ref[...].astype(f32))
    normal = normal_ref[...]
    da = normalize_back(grad, normal, scale_ref[...], norms_ref[0:1])
    da_ref[...] = da
    low_ref[...] = da.astype(bf16)
    sums_ref[...] = norm_sums(grad, normal)


def norm_call(kernel, name, outs, *args):
    return pl.pallas_call(kernel, in_specs=[VM] * len(args), out_shape=outs, compiler_params=PARAMS, cost_estimate=cost(0.6), name=name)(*pin(*args))


def local(
    tokens,
    spatial,
    box_coords,
    reading_order,
    page_len,
    w_attn,
    tables,
    w_out,
    ln_gain,
    ln_shift,
    w_up,
    w_down,
    grad_out,
):
    batches, own, features = tokens.shape[1:]
    rows = box_coords.shape[3]
    buckets = tables.shape[4]
    own_heads = tables.shape[2]
    heads = 2 * own_heads
    half = w_attn.shape[3]
    width = 2 * half
    share = w_attn.shape[2]
    step = tables.shape[3]
    coarse = COORD // buckets
    head_index = lax.axis_index("head")
    modality = head_index // 2
    pages = lax.axis_size("page")
    page_index = lax.axis_index("page")
    page = (page_index if direct() else page_index * 0).astype(jnp.int32).reshape(1)

    def mine(value):
        return lax.dynamic_index_in_dim(value, modality, 0, keepdims=False)

    def other(value):
        return lax.dynamic_index_in_dim(value, 1 - modality, 0, keepdims=False)

    def split_table(value):
        pieces = value.reshape(3, own_heads, step, 2, buckets // 2).transpose(3, 1, 2, 0, 4)
        return pieces.reshape(share, half)

    split = 5 * features // 6
    turns = jnp.array([0, 2, 1, 3], jnp.int32)
    blocks = turns ^ head_index
    slots = jnp.take(turns, jnp.arange(4, dtype=jnp.int32) ^ head_index)
    sequence = (0, 1, 3, 4, 2)
    attn_own = mine(w_attn)
    chunk_a = jnp.concatenate([attn_own[which] for which in sequence], axis=1)
    one_a = Gather(chunk_a[:, :split], FAR_Z)
    if direct():
        one_a.start()
    first = one_a.part
    attn_got = swap(other(after(w_attn, first)), "head", 2)
    table_own = split_table(mine(after(tables, first)))
    two_a = Gather(jnp.concatenate([chunk_a[:, split:], table_own], axis=1), FAR_X)
    if direct():
        two_a.start()
    table_got = swap(other(after(tables, two_a.part)), "head", 2)
    out_got = swap(other(after(w_out, two_a.part)), "head", 2)
    if direct():
        one_a.step(two_a.part)
        two_a.step(one_a.part)
    else:
        chunk_a = jnp.concatenate([chunk_a, table_own], axis=1)
    norms_own = after(jnp.stack([ln_gain, ln_shift]), one_a.part)
    norms_head = jnp.take(jnp.stack(gather_rows(norms_own)), slots, axis=0)
    tokens_late, spatial_late = after((tokens, spatial), first)
    rows_own = jnp.stack([mine(tokens_late), mine(spatial_late)])
    rows_side = swap(
        after(jnp.stack([other(tokens_late), other(spatial_late)]), attn_got, one_a.part), "head", 2
    )
    rows_near = swap(after(rows_own, attn_got, two_a.part), "head", 1)
    attn_got, table_got = after((attn_got, table_got), one_a.part, two_a.part)
    chunk_b = jnp.concatenate([attn_got[which] for which in sequence] + [split_table(table_got)], axis=1)
    chunk_f = jnp.concatenate([w_up.T, w_down], axis=1)
    part_b = Gather(chunk_b, FAR_X)
    if direct():
        part_b.start()
        one_a.step(part_b.part)
        two_a.step(one_a.part)
        out_got, norms_head = after((out_got, norms_head), two_a.part)
    chunk_o = jnp.concatenate([mine(w_out), out_got]).T
    if direct():
        norms_row = norms_head.transpose(1, 2, 0, 3).reshape(1, -1)
        chunk_o = jnp.concatenate([chunk_o, jnp.pad(norms_row, ((0, EXTRA - 1), (0, 0)))])
        part_o, part_f = Gather(chunk_o, FAR_Z), Gather(chunk_f, FAR_X)
        part_o.start()
        part_b.step(part_o.part)
        part_o.step(part_b.part)
        part_f.start(part_b.part)
        half_a = one_a.result() + two_a.result()
    else:
        half_a = generic_gather(chunk_a, 5 * half, 2 * own_heads)
        half_a = tuple(ref[..., :split] for ref in half_a) + tuple(ref[..., split:] for ref in half_a)
        half_b = generic_gather(chunk_b, 5 * half, 2 * own_heads)
        norms_full = by_page(gather_pages(norms_head)).transpose(2, 3, 0, 1, 4).reshape(4, GROUPS, 1, -1)
        norms_full = norms_full.transpose(1, 2, 0, 3).reshape(GROUPS, 1, -1)
        norms_full = jnp.pad(norms_full, ((0, 0), (0, EXTRA - 1), (0, 0)))
        pair_o = generic_gather(chunk_o)
        pair_o = tuple(
            jnp.concatenate([ref, extra], axis=1)
            for ref, extra in zip(pair_o, (norms_full[: GROUPS // 2], norms_full[GROUPS // 2 :]))
        )
        pair_f = generic_gather(chunk_f)
    row_parts = rows_own, rows_side, rows_near, swap(rows_side, "head", 1)

    ids = jnp.concatenate(
        [
            mine(reading_order)[None],
            mine(box_coords) // coarse,
            jnp.arange(rows, dtype=jnp.int32)[None, None] // page_len.reshape(1, batches, 1),
        ]
    )
    ids = jnp.take(ids.reshape(4, batches, 4, own), blocks, axis=2).reshape(4, batches, rows)

    state = [dict() for _ in range(batches)]
    if direct():
        part_b.step(part_o.part)
        gate_b = part_b.part
        part_o.step(part_b.part)
        part_f.step(part_o.part)
        gate_f = part_f.part
        part_f.step(gate_f)
        gate_last = part_f.part
    else:
        gate_b = gate_f = gate_last = page
    for batch, here in enumerate(state):
        here["ids"] = (ids[:, batch],)
        here["proj_a"], here["prob_a"], here["head_a"] = attend(
            batch, own_heads, after(page, gate_b), row_parts, half_a, *here["ids"]
        )
        gate_b = here["head_a"], gate_f
    if direct():
        half_b, pair_o, pair_f = part_b.result(), part_o.result(), part_f.result()
    for batch, here in enumerate(state):
        here["proj_b"], here["prob_b"], here["head_b"], here["keep"], here["send"], norms = attend(
            batch, own_heads, after(page, gate_b, gate_last), row_parts, half_b, *here["ids"],
            final=(pair_o, here["head_a"]),
        )
        gate_b = here["head_b"]
    ff_parts = pair_f + tuple(swap(ref, "head", 1) for ref in pair_f)

    wide = struct((own, features), f32)
    low = struct((own, features), bf16)
    sums = struct((2, features), f32)
    for batch, here in enumerate(state):
        keep, near, far = scatter_rows(here["keep"], here["send"])
        here["normal"], here["scale"], hidden_low = norm_call(
            norm_one_kernel, "norm_one", (wide, struct((own, 1), f32), low),
            keep[:own], near[:own], far, tokens[0, batch], tokens[1, batch], norms,
        )
        here["h"] = hidden_low, swap(hidden_low, "head", 2)
        here["act"], here["slope"], keep, send = ff_call(forward_kernel, "forward", here["h"], ff_parts, ())
        here["out"], here["dc"], dz, here["sums_two"] = norm_call(
            norm_two_kernel, "norm_two", (low, wide, low, sums),
            keep, swap(send, "head", 2), here["normal"], grad_out[batch], norms,
        )
        here["g"] = dz, swap(dz, "head", 2)
        here["grad_pre"], keep, send = ff_call(
            backward_kernel, "backward", here["g"], ff_parts, (here["act"], here["slope"])
        )
        here["da"], da_low, here["sums_one"] = norm_call(
            norm_back_kernel, "norm_back", (wide, low, sums),
            keep, swap(send, "head", 2), here["dc"], here["normal"], here["scale"], norms,
        )
        here["a"] = gather_rows(da_low)

    def every(name):
        return [here[name] for here in state]

    ours, theirs = ff_weights(every("h"), every("g"), every("grad_pre"), every("act"))
    keep_f, send_f = fold(ours, swap(theirs, "head", 1))
    part_f = Scatter(keep_f, send_f, FAR_X)
    if direct():
        part_f.start()

    def back_b(here, *gate):
        here["dproj_b"], here["dtable_b"], here["part"] = attend_back(
            own_heads, 1, after(page, *gate), here["a"], half_b, pair_o, here["proj_b"], here["prob_b"], *here["ids"]
        )
        return here["dproj_b"]

    def back_a(here, *gate):
        here["dproj_a"], here["dtable_a"], here["keep"], here["send"] = attend_back(
            own_heads, 0, after(page, *gate), here["a"], half_a, pair_o, here["proj_a"], here["prob_a"], *here["ids"],
            here["part"],
        )
        here["near"] = swap(here["send"], "head", 1)
        return here["dproj_a"]

    gate = back_b(state[0], part_f.send, *[here["a"][0] for here in state])
    keep_o, send_o = out_weights(
        after(page, gate),
        every("a"),
        [here[name] for here in state for name in ("head_a", "head_b")],
        [here[name] for here in state for name in ("sums_one", "sums_two")],
    )
    part_o = Scatter(keep_o, send_o, FAR_X)
    gate = (send_o,)
    if direct():
        part_o.start(part_f.send)
        part_f.step(part_o.send)
        gate += (part_f.send,)
    for here in state[1:]:
        gate = (back_b(here, *gate),)
    weights_b = attn_weights(after(page, *gate), row_parts, every("dproj_b"), every("dtable_b"), split)
    one_b, two_b = Scatter(*weights_b[:2], FAR_Z), Scatter(*weights_b[2:], FAR_X)
    gate = (weights_b[1],)
    if direct():
        two_b.start(part_f.send)
        one_b.start(two_b.send)
        part_o.step(one_b.send)
        gate = (part_o.send,)
    gate = (back_a(state[0], *gate),)
    if direct():
        part_f.step(part_o.send)
        gate += (part_f.send,)
    for here in state[1:]:
        gate = (back_a(here, *gate),)
    if direct():
        two_b.step(part_f.send)
        gate += (two_b.send,)
    weights_a = attn_weights(after(page, *gate), row_parts, every("dproj_a"), every("dtable_a"), split)
    one_a, two_a = Scatter(*weights_a[:2], FAR_Z), Scatter(*weights_a[2:], FAR_X)
    if direct():
        two_a.start(two_b.send)
        one_a.start(two_a.send)
        one_b.step(one_a.send)
        part_o.step(one_b.send)
        two_b.step(part_o.send)
        two_a.step(two_b.send)
        one_b.step(two_a.send)
        one_a.step(one_b.send)
        two_a.step(one_a.send)
        grad_b = jnp.concatenate([one_b.result(one_a.send), two_b.result(one_a.send)], axis=1)
        one_a.step(two_a.send)
        dff, dout = part_f.result(one_a.send), part_o.result(one_a.send)
        grad_a = jnp.concatenate([one_a.result(), two_a.result()], axis=1)
        dnorms = dout[share].reshape(4, 4, -1).transpose(1, 0, 2)
        dout = dout[:share]
    else:
        inner = features // GROUPS
        dff = generic_scatter(keep_f, send_f)
        dout = generic_scatter(keep_o[:, :inner], send_o[:, :inner])
        flat = jnp.concatenate([keep_o[:, inner], send_o[:, inner].astype(f32)]).reshape(GROUPS, 4, -1)
        flat = flat.transpose(1, 0, 2).reshape(4, pages, 4, -1).transpose(1, 2, 0, 3)
        dnorms = scatter_pages(by_page(flat))
        grads = []
        for weights in (weights_a, weights_b):
            keep = jnp.concatenate(weights[::2], axis=2)
            send = jnp.concatenate(weights[1::2], axis=2)
            grads.append(generic_scatter(keep, send, 5 * half, 2 * own_heads))
        grad_a, grad_b = grads

    dnorms = jnp.take(dnorms, blocks, axis=0)
    pair = dnorms[:2] + swap(dnorms[2:], "head", 1)
    dnorms = (pair[0] + swap(pair[1], "head", 2)).reshape(2, 2, -1)

    def both_modalities(ours, theirs):
        got = swap(theirs.astype(bf16), "head", 2).astype(f32)
        return jnp.where(modality == 0, jnp.stack([ours, got]), jnp.stack([got, ours]))

    token_grads = []
    for here in state:
        total = here["keep"] + after(here["near"], weights_a[1]).astype(f32)
        token_grads.append(both_modalities(total[:own], total[own:]) + here["da"][None])

    got_b = swap(grad_b.astype(bf16), "head", 2).astype(f32)
    chunks = jnp.where(modality == 0, jnp.stack([grad_a, got_b]), jnp.stack([got_b, grad_a]))
    dattn = jnp.stack([chunks[:, :, which * half : (which + 1) * half] for which in (0, 1, 4, 2, 3)], axis=1)
    dtable = chunks[:, :, 5 * half :].reshape(2, 2, own_heads, step, 3, buckets // 2)
    dtable = dtable.transpose(0, 4, 2, 3, 1, 5).reshape(2, 3, own_heads, step, buckets)
    dout = dout.reshape(share, 2, half).transpose(1, 2, 0)
    return (
        jnp.stack([here["out"] for here in state]),
        jnp.stack(token_grads, axis=1).astype(bf16),
        dattn,
        dtable,
        both_modalities(dout[0], dout[1]),
        dnorms[0],
        dnorms[1],
        dff[:, :features].T,
        dff[:, features:],
    )


def solution(mesh):
    return jax.shard_map(
        local,
        mesh=mesh,
        in_specs=(
            P(None, None, ("page", "head"), None),
            P(None, None, ("page", "head"), None),
            P(None, None, None, "page"),
            P(None, None, "page"),
            P(None, "page"),
            P(None, None, "page", "head"),
            P(None, None, "head", "page", None),
            P(None, "head", "page"),
            P(None, ("page", "head")),
            P(None, ("page", "head")),
            P(None, ("page", "head")),
            P(("page", "head"), None),
            P(None, ("page", "head"), None),
        ),
        out_specs=(
            P(None, ("page", "head"), None),
            P(None, None, ("page", "head"), None),
            P(None, None, "page", "head"),
            P(None, None, "head", "page", None),
            P(None, "head", "page"),
            P(None, ("page", "head")),
            P(None, ("page", "head")),
            P(None, ("page", "head")),
            P(("page", "head"), None),
        ),
        check_vma=False,
    )
```

```python
import functools

import jax
import jax.numpy as jnp
from jax import lax
from jax.experimental import pallas as pl
from jax.experimental.pallas import tpu as pltpu
from jax.sharding import PartitionSpec as P

COORD = 1024
EPS = 1e-05
GROUPS = 8
SCALE = 7e8
EXTRA = 16
f32 = jnp.float32
bf16 = jnp.bfloat16
AB = ((1,), (0,))
ABT = ((1,), (1,))
ATB = ((0,), (0,))
SMEM = pl.BlockSpec(memory_space=pltpu.SMEM)
VM = pl.BlockSpec(memory_space=pltpu.VMEM)
HBM = pl.BlockSpec(memory_space=pltpu.HBM)
PARAMS = pltpu.CompilerParams(vmem_limit_bytes=14 * 1024 * 1024)
FAR_X = (4, 2, 1)
FAR_Z = (4, 1, 2)
X_FIRST = (1, 4, 2)


def cost(microseconds):
    return pl.CostEstimate(
        flops=int(microseconds * SCALE), bytes_accessed=int(microseconds * 3e5), transcendentals=0
    )


def struct(shape, kind):
    return pltpu.VMEM(tuple(shape), kind)


def pin(*values):
    return [pltpu.with_memory_space_constraint(value, pltpu.VMEM) for value in values]


def dot(left, right, dims):
    return lax.dot_general(left, right, (dims, ((), ())), preferred_element_type=f32)


def swap(value, axis, mask):
    count = lax.axis_size(axis)
    return lax.ppermute(value, axis, [(place, place ^ mask) for place in range(count)])


def after(value, *earlier):
    return lax.optimization_barrier((value, earlier))[0]


def gather_rows(own):
    side = swap(own, "head", 2)
    return own, side, swap(own, "head", 1), swap(side, "head", 1)


def scatter_rows(keep, send):
    own = keep.shape[0] // 2
    near = swap(send, "head", 1)
    far = swap((keep[own:] + near[own:].astype(f32)).astype(bf16), "head", 2)
    return keep, near, far


def page_bits():
    count = lax.axis_size("page")
    return [1 << bit for bit in reversed(range(count.bit_length() - 1))]


def gather_pages(own):
    full = own
    for depth, mask in enumerate(page_bits()):
        full = jnp.stack([full, swap(full, "page", mask)], axis=depth)
    return full.reshape((lax.axis_size("page"),) + own.shape)


def scatter_pages(blocks):
    masks = page_bits()
    part = blocks.reshape((2,) * len(masks) + blocks.shape[1:])
    for depth in reversed(range(len(masks))):
        keep = lax.index_in_dim(part, 0, depth, keepdims=False)
        send = lax.index_in_dim(part, 1, depth, keepdims=False)
        part = keep.astype(f32) + swap(send.astype(bf16), "page", masks[depth]).astype(f32)
    return part


def by_page(blocks):
    count = blocks.shape[0]
    order = jnp.arange(count, dtype=jnp.int32) ^ lax.axis_index("page")
    return jnp.take(blocks, order, axis=0)


def regroup(full, heads):
    pages, share, columns = full.shape
    if heads == 1:
        return full.reshape(GROUPS, -1, columns)
    parts = full.reshape(GROUPS, pages // GROUPS, heads, share // heads, columns)
    return parts.transpose(0, 2, 1, 3, 4).reshape(GROUPS, -1, columns)


def ungroup(full, pages, heads):
    columns = full.shape[2]
    if heads == 1:
        return full.reshape(pages, -1, columns)
    parts = full.reshape(GROUPS, heads, pages // GROUPS, -1, columns)
    return parts.transpose(0, 2, 1, 3, 4).reshape(pages, -1, columns)


def direct():
    return lax.axis_size("page") == GROUPS


def join_kernel(first_ref, second_ref, out_ref):
    half = first_ref.shape[0]
    out_ref[:half] = first_ref[...]
    out_ref[half:] = second_ref[...]


def join(first, second):
    return pl.pallas_call(
        join_kernel,
        in_specs=[VM] * 2,
        out_shape=struct((2 * first.shape[0],) + first.shape[1:], first.dtype),
        compiler_params=PARAMS,
        cost_estimate=cost(0.4),
        name="join",
    )(*pin(first, second))


def fold_kernel(first_ref, second_ref, keep_ref, send_ref):
    half = keep_ref.shape[0]
    keep_ref[...] = first_ref[:half].astype(f32) + second_ref[:half].astype(f32)
    send_ref[...] = (first_ref[half:].astype(f32) + second_ref[half:].astype(f32)).astype(bf16)


def fold(first, second):
    half = (first.shape[0] // 2,) + first.shape[1:]
    return pl.pallas_call(
        fold_kernel,
        in_specs=[VM] * 2,
        out_shape=(struct(half, f32), struct(half, bf16)),
        compiler_params=PARAMS,
        cost_estimate=cost(0.6),
        name="fold",
    )(*pin(first, second))


class Gather:
    def __init__(self, share, masks):
        self.part, self.masks = share[None], list(masks)

    def start(self, *earlier):
        self.part = after(self.part, *earlier)
        self.got = swap(self.part, "page", self.masks.pop(0))

    def step(self, *earlier):
        self.part = join(self.part, after(self.got, *earlier))
        self.start(*earlier)

    def result(self):
        return self.part, self.got


def generic_gather(share, columns=None, heads=1):
    full = by_page(gather_pages(share))
    if heads == 1:
        full = regroup(full, 1)
    else:
        full = jnp.concatenate([regroup(full[..., :columns], 1), regroup(full[..., columns:], heads)], axis=2)
    return full[: GROUPS // 2], full[GROUPS // 2 :]


class Scatter:
    def __init__(self, keep, send, masks):
        self.keep, self.send, self.masks = keep, send, list(masks)

    def start(self, *earlier):
        self.send = after(self.send, *earlier)
        self.got = swap(self.send, "page", self.masks.pop())

    def step(self, *earlier):
        self.keep, self.send = fold(self.keep, after(self.got, *earlier))
        self.start(*earlier)

    def result(self, *earlier):
        return self.keep[0] + after(self.got, *earlier)[0].astype(f32)


def generic_scatter(keep, send, columns=None, heads=1):
    pages = lax.axis_size("page")
    full = jnp.concatenate([keep.astype(bf16), send])
    if heads == 1:
        full = ungroup(full, pages, 1)
    else:
        full = jnp.concatenate(
            [ungroup(full[..., :columns], pages, 1), ungroup(full[..., columns:], pages, heads)], axis=2
        )
    return scatter_pages(by_page(full))


def places(masks):
    if not direct():
        masks = (1, 2, 4)
    return [
        sum(mask for bit, mask in enumerate(masks) if (place >> bit) & 1) for place in range(GROUPS)
    ]


def load_chunk(page, refs, masks, target, start=0):
    share = target.shape[0] // GROUPS
    stop = start + refs[0].shape[2]
    for place, number in enumerate(places(masks)):
        row = pl.multiple_of(jnp.bitwise_xor(page, number) * share, share)
        target[pl.ds(row, share), start:stop] = refs[place // (GROUPS // 2)][place % (GROUPS // 2), :share]


def load_rows(refs, target, *pick):
    count = refs[0].shape[-2]
    for place, ref in enumerate(refs):
        target[place * count : (place + 1) * count] = ref[pick] if pick else ref[...]


def load_extra(page, refs, masks, target):
    share = refs[0].shape[1] - EXTRA
    for place, number in enumerate(places(masks)):
        target[jnp.bitwise_xor(page, number)] = refs[place // (GROUPS // 2)][place % (GROUPS // 2), share:]


def load_split(page, refs, target):
    if len(refs) == 2:
        load_chunk(page, refs, FAR_X, target)
    else:
        load_chunk(page, refs[:2], FAR_Z, target)
        load_chunk(page, refs[2:], FAR_X, target, refs[0].shape[2])


def turned(ids_ref):
    ids = ids_ref[...].astype(f32)
    return jnp.concatenate([ids, ids]).T


def hot_columns(ids, which, buckets):
    lane = lax.broadcasted_iota(jnp.int32, (ids.shape[0], buckets), 1).astype(f32)
    return jnp.where(ids[:, which : which + 1] == lane, 1.0, 0.0).astype(bf16)


def table_rows(head, heads, small):
    return [pl.multiple_of((side * heads + head) * small, small) for side in range(2)]


def attend_kernel(batch, heads, last, page_ref, *refs):
    parts = 2 if last else 4
    rows_refs, w_refs, refs = refs[:4], refs[4 : 4 + parts], refs[4 + parts :]
    if last:
        o_refs, other_ref, refs = refs[:2], refs[2], refs[3:]
    idr_ref, saved, head_ref, refs = refs[0], refs[1:6], refs[6], refs[7:]
    if last:
        saved += refs[:1]
        keep_ref, send_ref, norms_ref, refs = refs[1], refs[2], refs[3], refs[4:]
        wo_ref, extra_ref, refs = refs[0], refs[1], refs[2:]
    left_ref, right_ref, value_ref, prob_ref, w_ref, x_ref, s_ref, hot_ref, head_part_ref, sems = refs
    page = page_ref[0]
    load_rows(rows_refs, x_ref, 0, batch)
    load_rows(rows_refs, s_ref, 1, batch)
    load_split(page, w_refs, w_ref)
    copies = [pltpu.make_async_copy(w_ref, saved[4], sems.at[0])]
    if last:
        load_chunk(page, o_refs, X_FIRST, wo_ref)
        load_extra(page, o_refs, X_FIRST, extra_ref)
        copies.append(pltpu.make_async_copy(wo_ref, saved[5], sems.at[1]))
    rows = x_ref.shape[0]
    width = w_ref.shape[1] // 6
    share = w_ref.shape[0] // GROUPS
    size = width // heads
    buckets = 2 * width // 3
    small, wide = buckets // GROUPS, buckets // 2
    columns = turned(idr_ref)
    for which in range(3):
        hot_ref[:, which * buckets : (which + 1) * buckets] = hot_columns(columns, which, buckets)
    same = columns[:, 3:4] == idr_ref[3:4, :].astype(f32)
    first = dot(x_ref[...], w_ref[:, : 2 * width], AB).astype(bf16)
    second = dot(s_ref[...], w_ref[:, 2 * width : 4 * width], AB).astype(bf16)
    third = dot(x_ref[...], w_ref[:, 4 * width : 5 * width], AB).astype(bf16)
    for head in range(heads):
        low, high = slice(head * size, (head + 1) * size), slice(width + head * size, width + (head + 1) * size)
        left_ref[head] = jnp.concatenate([first[:, low], second[:, low]], axis=1) * bf16(0.125)
        right_ref[head] = jnp.concatenate([first[:, high], second[:, high]], axis=1)
        value_ref[head] = third[:, low]
    for at, ref in enumerate((left_ref, right_ref, value_ref)):
        copies.append(pltpu.make_async_copy(ref, saved[at], sems.at[2 + at]))
    for copy in copies:
        copy.start()

    def save_prob(head):
        return pltpu.make_async_copy(prob_ref.at[head], saved[3].at[head], sems.at[5 + head])

    def body(head, carry):
        sides = []
        for start in table_rows(head, heads, small):
            pieces = [w_ref[pl.ds(group * share + start, small), 5 * width :] for group in range(GROUPS)]
            sides.append(jnp.concatenate(pieces))
        parts = [left_ref[head]]
        for which in range(3):
            table = jnp.concatenate([side[:, which * wide : (which + 1) * wide] for side in sides], axis=1)
            parts.append(dot(hot_ref[:, which * buckets : (which + 1) * buckets], table, AB).astype(bf16))
        left = jnp.concatenate(parts, axis=1)
        right = jnp.concatenate([right_ref[head], hot_ref[...]], axis=1)
        score = jnp.where(same, dot(left, right, ABT), -1e30)
        weight = jnp.exp(score - jnp.max(score, axis=1, keepdims=True))
        prob = (weight * (1.0 / jnp.sum(weight, axis=1, keepdims=True))).astype(bf16)
        prob_ref[head] = prob
        save_prob(head).start()
        head_part_ref[head] = dot(prob, value_ref[head], AB).astype(bf16)
        return carry

    lax.fori_loop(0, heads, body, 0)
    head_ref[...] = jnp.concatenate([head_part_ref[head] for head in range(heads)], axis=1)
    if last:
        part = dot(other_ref[...], wo_ref[:, :width], ABT) + dot(head_ref[...], wo_ref[:, width:], ABT)
        keep_ref[...] = part[: rows // 2]
        send_ref[...] = part[rows // 2 :].astype(bf16)
        inner = norms_ref.shape[1] // GROUPS
        for group in range(GROUPS):
            for which in range(norms_ref.shape[0]):
                norms_ref[which : which + 1, group * inner : (group + 1) * inner] = extra_ref[
                    group, 0:1, which * inner : (which + 1) * inner
                ].astype(f32)
    for copy in copies:
        copy.wait()
    for head in range(heads):
        save_prob(head).wait()


def attend(batch, heads, page, row_parts, chunk, ids_row, final=None):
    rows = ids_row.shape[1]
    features = row_parts[0].shape[-1]
    columns = sum(ref.shape[2] for ref in chunk[::2])
    width = columns // 6
    size = width // heads
    saved = [
        ((heads, rows, 2 * size), bf16),
        ((heads, rows, 2 * size), bf16),
        ((heads, rows, size), bf16),
        ((heads, rows, rows), bf16),
        ((features, columns), bf16),
    ]
    scratch = [pltpu.VMEM(shape, kind) for shape, kind in saved]
    more = ()
    extra_outs, first_scratch = (), []
    if final is not None:
        pair_o, other = final
        more = (*pair_o, other)
        extra_outs = (
            pltpu.HBM((features, 2 * width), bf16),
            struct((rows // 2, features), f32), struct((rows // 2, features), bf16), struct((4, features), f32),
        )
        first_scratch = [pltpu.VMEM((features, 2 * width), bf16), pltpu.VMEM((GROUPS, EXTRA, 2 * width), bf16)]
    outs = tuple(pltpu.HBM(shape, kind) for shape, kind in saved) + (struct((rows, width), bf16),)
    return pl.pallas_call(
        functools.partial(attend_kernel, batch, heads, final is not None),
        in_specs=[SMEM] + [VM] * (4 + len(chunk) + len(more) + 1),
        out_specs=[HBM] * 5 + [VM] + ([] if final is None else [HBM, VM, VM, VM]),
        out_shape=outs + extra_outs,
        scratch_shapes=first_scratch + scratch + [
            pltpu.VMEM((rows, features), bf16),
            pltpu.VMEM((rows, features), bf16),
            pltpu.VMEM((rows, 2 * width), bf16),
            pltpu.VMEM((heads, rows, size), bf16),
            pltpu.SemaphoreType.DMA((5 + heads,)),
        ],
        compiler_params=PARAMS,
        cost_estimate=cost(6.3),
        name="attend",
    )(page, *pin(*row_parts, *chunk, *more, ids_row))


def attend_back_kernel(heads, half, page_ref, *refs):
    da_refs, saved, idr_ref, refs = refs[:4], refs[4:10], refs[10], refs[11:]
    if half == 0:
        other_ref, dproj_ref, dtable_ref, keep_ref, send_ref, refs = refs[0], refs[1], refs[2], refs[3], refs[4], refs[5:]
    else:
        dproj_ref, dtable_ref, part_ref, refs = refs[0], refs[1], refs[2], refs[3:]
    left_ref, right_ref, value_ref, prob_ref, w_ref, wo_ref, refs = refs[0], refs[1], refs[2], refs[3], refs[4], refs[5], refs[6:]
    da_ref, hot_ref, grad_ref, dleft_ref, dright_ref, dvalue_ref, sems = refs
    early = [
        pltpu.make_async_copy(source, target, sems.at[at])
        for at, (source, target) in enumerate(
            ((saved[5], wo_ref), (saved[2], value_ref), (saved[1], right_ref), (saved[0], left_ref))
        )
    ]
    late = pltpu.make_async_copy(saved[4], w_ref, sems.at[4])

    def fetch_prob(head):
        return pltpu.make_async_copy(saved[3].at[head], prob_ref.at[head], sems.at[5 + head])

    early[0].start()
    early[1].start()
    fetch_prob(0).start()
    early[2].start()
    early[3].start()
    for head in range(1, heads):
        fetch_prob(head).start()
    late.start()
    load_rows(da_refs, da_ref)
    rows = da_ref.shape[0]
    width = w_ref.shape[1] // 6
    size = width // heads
    buckets = 2 * width // 3
    small, wide = buckets // GROUPS, buckets // 2
    columns = turned(idr_ref)
    for which in range(3):
        hot_ref[:, which * buckets : (which + 1) * buckets] = hot_columns(columns, which, buckets)
    bucket = lax.broadcasted_iota(jnp.int32, (buckets, rows), 0)
    early[0].wait()
    grad_heads = dot(da_ref[...], wo_ref[:, half * width : (half + 1) * width], AB).astype(bf16)
    for head in range(heads):
        grad_ref[head] = grad_heads[:, head * size : (head + 1) * size]
    for copy in early[1:]:
        copy.wait()

    def body(head, carry):
        fetch_prob(head).wait()
        prob = prob_ref[head]
        grad_out = grad_ref[head]
        grad_prob = dot(grad_out, value_ref[head], ABT)
        weighted = prob.astype(f32) * grad_prob
        row_dot = jnp.sum(weighted, axis=1, keepdims=True)
        grad_score = (weighted - prob.astype(f32) * row_dot).astype(bf16)
        dvalue_ref[head] = dot(prob, grad_out, ATB).astype(bf16)
        right = jnp.concatenate([right_ref[head], hot_ref[...]], axis=1)
        spread = dot(grad_score, right, AB)
        dleft_ref[head] = (spread[:, : 2 * size] * 0.125).astype(bf16)
        dright_ref[head] = dot(grad_score, left_ref[head], ATB).astype(bf16)
        pieces = []
        for which in range(3):
            start = 2 * size + which * buckets
            hot_t = jnp.where(idr_ref[which : which + 1, :] == bucket, 1.0, 0.0).astype(bf16)
            pieces.append(dot(hot_t, spread[:, start : start + buckets].astype(bf16), AB))
        for side, start in enumerate(table_rows(head, heads, small)):
            block = jnp.concatenate([piece[:, side * wide : (side + 1) * wide] for piece in pieces], axis=1)
            for group in range(GROUPS):
                dtable_ref[group, pl.ds(start, small), :] = block[group * small : (group + 1) * small]
        return carry

    lax.fori_loop(0, heads, body, 0)
    every = range(heads)
    dproj_ref[:, :width] = jnp.concatenate([dleft_ref[head][:, :size] for head in every], axis=1)
    dproj_ref[:, width : 2 * width] = jnp.concatenate([dright_ref[head][:, :size] for head in every], axis=1)
    dproj_ref[:, 2 * width : 3 * width] = jnp.concatenate([dleft_ref[head][:, size:] for head in every], axis=1)
    dproj_ref[:, 3 * width : 4 * width] = jnp.concatenate([dright_ref[head][:, size:] for head in every], axis=1)
    dproj_ref[:, 4 * width :] = jnp.concatenate([dvalue_ref[head] for head in every], axis=1)
    late.wait()
    part = dot(dproj_ref[:, : 2 * width], w_ref[:, : 2 * width], ABT)
    part = part + dot(dproj_ref[:, 4 * width :], w_ref[:, 4 * width : 5 * width], ABT)
    if half == 0:
        part = part + other_ref[...]
        keep_ref[...] = part[: rows // 2]
        send_ref[...] = part[rows // 2 :].astype(bf16)
    else:
        part_ref[...] = part


def attend_back(heads, half, page, da_parts, saved, ids_row, other=None):
    rows = ids_row.shape[1]
    features = da_parts[0].shape[-1]
    width = saved[4].shape[1] // 6
    size = width // heads
    outs = (struct((rows, 5 * width), bf16), struct((GROUPS, features // GROUPS, width), f32))
    if half == 0:
        outs += (struct((rows // 2, features), f32), struct((rows // 2, features), bf16))
    else:
        outs += (struct((rows, features), f32),)
    return pl.pallas_call(
        functools.partial(attend_back_kernel, heads, half),
        in_specs=[SMEM] + [VM] * 4 + [HBM] * 6 + [VM] * (2 if half == 0 else 1),
        out_shape=outs,
        scratch_shapes=[pltpu.VMEM(ref.shape, ref.dtype) for ref in saved]
        + [
            pltpu.VMEM((rows, features), bf16),
            pltpu.VMEM((rows, 2 * width), bf16),
            pltpu.VMEM((heads, rows, size), bf16),
            pltpu.VMEM((heads, rows, 2 * size), bf16),
            pltpu.VMEM((heads, rows, 2 * size), bf16),
            pltpu.VMEM((heads, rows, size), bf16),
            pltpu.SemaphoreType.DMA((5 + heads,)),
        ],
        compiler_params=PARAMS,
        cost_estimate=cost(6),
        name="attend_back",
    )(page, *pin(*da_parts), *[pltpu.with_memory_space_constraint(ref, pltpu.HBM) for ref in saved], *pin(ids_row, *([other] if half == 0 else [])))


def put_blocks(page, masks, full_ref, columns, keep_ref, send_ref):
    for place, number in enumerate(places(masks)):
        block = full_ref[jnp.bitwise_xor(page, number), :, columns]
        if place < GROUPS // 2:
            keep_ref[place] = block
        else:
            send_ref[place - GROUPS // 2] = block.astype(bf16)


def attn_weights_kernel(batches, split, page_ref, *refs):
    rows_refs, dproj_refs, dtable_refs = refs[:4], refs[4 : 4 + batches], refs[4 + batches : 4 + 2 * batches]
    out_refs, (x_ref, d_ref, full_ref) = refs[4 + 2 * batches : -3], refs[-3:]
    page = page_ref[0]
    rows = x_ref.shape[1] // batches
    for batch in range(batches):
        at = pl.ds(batch * rows, rows)
        for which in range(2):
            load_rows(rows_refs, x_ref.at[which, at], which, batch)
        d_ref[at] = dproj_refs[batch][...]
    width = d_ref.shape[1] // 5

    def blocks(value):
        return value.reshape(GROUPS, value.shape[0] // GROUPS, value.shape[1])

    x_t = x_ref[0].T
    full_ref[:, :, : 2 * width] = blocks(dot(x_t, d_ref[:, : 2 * width], AB))
    full_ref[:, :, 2 * width : 4 * width] = blocks(dot(x_ref[1].T, d_ref[:, 2 * width : 4 * width], AB))
    full_ref[:, :, 4 * width : 5 * width] = blocks(dot(x_t, d_ref[:, 4 * width :], AB))
    total = dtable_refs[0][...]
    for ref in dtable_refs[1:]:
        total = total + ref[...]
    full_ref[:, :, 5 * width :] = total
    if split:
        put_blocks(page, FAR_Z, full_ref, slice(0, split), *out_refs[:2])
    put_blocks(page, FAR_X, full_ref, slice(split, 6 * width), *out_refs[-2:])


def attn_weights(page, row_parts, dprojs, dtables, split):
    batches = len(dprojs)
    rows, columns = dprojs[0].shape
    columns = 6 * (columns // 5)
    features = row_parts[0].shape[-1]
    inner = features // GROUPS
    outs = ()
    for count in (split, columns - split) if split else (columns,):
        outs += (struct((GROUPS // 2, inner, count), f32), struct((GROUPS // 2, inner, count), bf16))
    return pl.pallas_call(
        functools.partial(attn_weights_kernel, batches, split),
        in_specs=[SMEM] + [VM] * (4 + batches) + [VM] * batches,
        out_shape=outs,
        scratch_shapes=[
            pltpu.VMEM((2, batches * rows, features), bf16),
            pltpu.VMEM((batches * rows, dprojs[0].shape[1]), bf16),
            pltpu.VMEM((GROUPS, inner, columns), f32),
        ],
        compiler_params=PARAMS,
        cost_estimate=cost(4.8),
        name="attn_weights",
    )(page, *pin(*row_parts, *dprojs, *dtables))


def out_weights_kernel(batches, page_ref, *refs):
    da_refs, head_refs, refs = refs[: 4 * batches], refs[4 * batches : 6 * batches], refs[6 * batches :]
    sums_refs, refs = refs[: 2 * batches], refs[2 * batches :]
    keep_ref, send_ref, da_ref, head_ref, full_ref = refs
    page = page_ref[0]
    rows = da_ref.shape[0] // batches
    width = head_ref.shape[2]
    for batch in range(batches):
        at = pl.ds(batch * rows, rows)
        load_rows(da_refs[4 * batch : 4 * batch + 4], da_ref.at[at])
        for half in range(2):
            head_ref[half, at] = head_refs[2 * batch + half][...]
    share = da_ref.shape[1] // GROUPS
    full_ref[:, share:, :] = jnp.zeros((GROUPS, EXTRA, 2 * width), f32)
    for layer in range(2):
        total = sums_refs[layer][...]
        for batch in range(1, batches):
            total = total + sums_refs[2 * batch + layer][...]
        for which in range(2):
            for group in range(GROUPS):
                start = (2 * which + layer) * share
                full_ref[group, share : share + 1, start : start + share] = total[
                    which : which + 1, group * share : (group + 1) * share
                ]
    da_t = da_ref[...].T
    for half in range(2):
        full_ref[:, :share, half * width : (half + 1) * width] = dot(da_t, head_ref[half], AB).reshape(
            GROUPS, share, width
        )
    put_blocks(page, FAR_X, full_ref, slice(0, 2 * width), keep_ref, send_ref)


def out_weights(page, da_parts, head_rows, sums):
    batches = len(da_parts)
    rows, width = head_rows[0].shape
    features = da_parts[0][0].shape[-1]
    chunk = (GROUPS // 2, features // GROUPS + EXTRA, 2 * width)
    return pl.pallas_call(
        functools.partial(out_weights_kernel, batches),
        in_specs=[SMEM] + [VM] * (6 * batches) + [VM] * (2 * batches),
        out_shape=(struct(chunk, f32), struct(chunk, bf16)),
        scratch_shapes=[
            pltpu.VMEM((batches * rows, features), bf16),
            pltpu.VMEM((2, batches * rows, width), bf16),
            pltpu.VMEM((GROUPS,) + chunk[1:], f32),
        ],
        compiler_params=PARAMS,
        cost_estimate=cost(2.7),
        name="out_weights",
    )(page, *pin(*[ref for parts in da_parts for ref in parts], *head_rows, *sums))


def hidden_weights(refs):
    return jnp.concatenate([ref[...].reshape(-1, ref.shape[2]) for ref in refs])


def forward_kernel(own_ref, side_ref, *refs):
    f_refs, (act_ref, slope_ref, keep_ref, send_ref) = refs[:4], refs[4:]
    own, features = own_ref.shape
    rows = jnp.concatenate([own_ref[...], side_ref[...]])
    weight = hidden_weights(f_refs)
    pre = dot(rows, weight[:, :features], ABT)
    normal = 0.5 + 0.5 * lax.erf(pre * 0.7071067811865476)
    act = (pre * normal).astype(bf16)
    act_ref[...] = act
    slope_ref[...] = (normal + pre * jnp.exp(-0.5 * pre * pre) * 0.3989422804014327).astype(bf16)
    part = dot(act, weight[:, features:], AB)
    keep_ref[...] = part[:own]
    send_ref[...] = part[own:].astype(bf16)


def backward_kernel(own_ref, side_ref, *refs):
    f_refs, (act_ref, slope_ref, pre_ref, keep_ref, send_ref) = refs[:4], refs[4:]
    own, features = own_ref.shape
    rows = jnp.concatenate([own_ref[...], side_ref[...]])
    weight = hidden_weights(f_refs)
    grad_act = dot(rows, weight[:, features:], ABT)
    grad_pre = (grad_act * slope_ref[...].astype(f32)).astype(bf16)
    pre_ref[...] = grad_pre
    part = dot(grad_pre, weight[:, :features], AB)
    keep_ref[...] = part[:own]
    send_ref[...] = part[own:].astype(bf16)


def ff_call(kernel, name, parts, weights, saved):
    own, features = parts[0].shape
    hidden = sum(ref.shape[0] * ref.shape[1] for ref in weights)
    outs = (struct((2 * own, hidden), bf16),) * (1 if saved else 2)
    return pl.pallas_call(
        kernel,
        in_specs=[VM] * (6 + len(saved)),
        out_shape=outs + (struct((own, features), f32), struct((own, features), bf16)),
        compiler_params=PARAMS,
        cost_estimate=cost(1.8),
        name=name,
    )(*pin(*parts, *weights, *saved))


def ff_weights_kernel(batches, *refs):
    h_refs, g_refs = refs[: 2 * batches], refs[2 * batches : 4 * batches]
    pre_refs, act_refs = refs[4 * batches : 5 * batches], refs[5 * batches : 6 * batches]
    ours_ref, theirs_ref = refs[6 * batches :]
    features = ours_ref.shape[2]
    features = features // 2
    half = GROUPS * ours_ref.shape[1]
    shape = ours_ref.shape[:2] + (features,)
    for left_refs, right_refs, at in ((pre_refs, h_refs, 0), (act_refs, g_refs, features)):
        left = jnp.concatenate([ref[...] for ref in left_refs])
        right = jnp.concatenate([ref[...] for ref in right_refs])
        total = dot(left, right, ATB).astype(bf16)
        ours_ref[:, :, at : at + features] = total[:half].reshape(shape)
        theirs_ref[:, :, at : at + features] = total[half:].reshape(shape)


def ff_weights(h_parts, g_parts, grad_pres, acts):
    batches = len(acts)
    hidden = acts[0].shape[1]
    features = h_parts[0][0].shape[1]
    chunk = (GROUPS, hidden // (2 * GROUPS), 2 * features)
    return pl.pallas_call(
        functools.partial(ff_weights_kernel, batches),
        in_specs=[VM] * (6 * batches),
        out_shape=(struct(chunk, bf16), struct(chunk, bf16)),
        compiler_params=PARAMS,
        cost_estimate=cost(4.2),
        name="ff_weights",
    )(*pin(*[ref for parts in h_parts + g_parts for ref in parts], *grad_pres, *acts))


def normalize(value):
    centred = value - jnp.mean(value, axis=1, keepdims=True)
    scale = lax.rsqrt(jnp.mean(centred * centred, axis=1, keepdims=True) + EPS)
    return centred * scale, scale


def normalize_back(grad, normal, scale, gain):
    inner = grad * gain
    inner = inner - jnp.mean(inner, axis=1, keepdims=True) - normal * jnp.mean(inner * normal, axis=1, keepdims=True)
    return inner * scale


def norm_sums(grad, normal):
    gain = jnp.sum(grad * normal, axis=0, keepdims=True)
    shift = jnp.sum(grad, axis=0, keepdims=True)
    return jnp.concatenate([gain, shift], axis=0)


def norm_one_kernel(keep_ref, near_ref, far_ref, first_ref, second_ref, norms_ref, normal_ref, scale_ref, low_ref):
    value = first_ref[...].astype(f32) + second_ref[...].astype(f32)
    value = value + (keep_ref[...] + near_ref[...].astype(f32) + far_ref[...].astype(f32))
    normal, scale = normalize(value)
    normal_ref[...] = normal
    scale_ref[...] = scale
    low_ref[...] = (normal * norms_ref[0:1] + norms_ref[2:3]).astype(bf16)


def norm_two_kernel(keep_ref, far_ref, normal_ref, grad_ref, norms_ref, out_ref, dc_ref, dz_ref, sums_ref):
    value = normal_ref[...] * norms_ref[0:1] + norms_ref[2:3]
    value = value + (keep_ref[...] + far_ref[...].astype(f32))
    normal, scale = normalize(value)
    out_ref[...] = (normal * norms_ref[1:2] + norms_ref[3:4]).astype(bf16)
    grad = grad_ref[...].astype(f32)
    dc = normalize_back(grad, normal, scale, norms_ref[1:2])
    dc_ref[...] = dc
    dz_ref[...] = dc.astype(bf16)
    sums_ref[...] = norm_sums(grad, normal)


def norm_back_kernel(keep_ref, far_ref, dc_ref, normal_ref, scale_ref, norms_ref, da_ref, low_ref, sums_ref):
    grad = dc_ref[...] + (keep_ref[...] + far_ref[...].astype(f32))
    normal = normal_ref[...]
    da = normalize_back(grad, normal, scale_ref[...], norms_ref[0:1])
    da_ref[...] = da
    low_ref[...] = da.astype(bf16)
    sums_ref[...] = norm_sums(grad, normal)


def norm_call(kernel, name, outs, *args):
    return pl.pallas_call(kernel, in_specs=[VM] * len(args), out_shape=outs, compiler_params=PARAMS, cost_estimate=cost(0.6), name=name)(*pin(*args))


def local(
    tokens,
    spatial,
    box_coords,
    reading_order,
    page_len,
    w_attn,
    tables,
    w_out,
    ln_gain,
    ln_shift,
    w_up,
    w_down,
    grad_out,
):
    batches, own, features = tokens.shape[1:]
    rows = box_coords.shape[3]
    buckets = tables.shape[4]
    own_heads = tables.shape[2]
    heads = 2 * own_heads
    half = w_attn.shape[3]
    width = 2 * half
    share = w_attn.shape[2]
    step = tables.shape[3]
    coarse = COORD // buckets
    head_index = lax.axis_index("head")
    modality = head_index // 2
    pages = lax.axis_size("page")
    page_index = lax.axis_index("page")
    page = (page_index if direct() else page_index * 0).astype(jnp.int32).reshape(1)

    def mine(value):
        return lax.dynamic_index_in_dim(value, modality, 0, keepdims=False)

    def other(value):
        return lax.dynamic_index_in_dim(value, 1 - modality, 0, keepdims=False)

    def split_table(value):
        pieces = value.reshape(3, own_heads, step, 2, buckets // 2).transpose(3, 1, 2, 0, 4)
        return pieces.reshape(share, half)

    split = 5 * features // 6
    turns = jnp.array([0, 2, 1, 3], jnp.int32)
    blocks = turns ^ head_index
    slots = jnp.take(turns, jnp.arange(4, dtype=jnp.int32) ^ head_index)
    sequence = (0, 1, 3, 4, 2)
    attn_own = mine(w_attn)
    chunk_a = jnp.concatenate([attn_own[which] for which in sequence], axis=1)
    one_a = Gather(chunk_a[:, :split], FAR_Z)
    if direct():
        one_a.start()
    first = one_a.part
    attn_send = other(after(w_attn, first))
    attn_got = swap(attn_send, "head", 2)
    table_own = split_table(mine(after(tables, attn_send)))
    two_a = Gather(jnp.concatenate([chunk_a[:, split:], table_own], axis=1), FAR_X)
    if direct():
        two_a.start()
    table_got = swap(other(after(tables, two_a.part)), "head", 2)
    out_got = swap(other(after(w_out, two_a.part)), "head", 2)
    norms_own = after(jnp.stack([ln_gain, ln_shift]), two_a.part)
    norms_four = gather_rows(norms_own)
    if direct():
        one_a.step(two_a.part)
        out_got, norms_four = after((out_got, norms_four), one_a.part)
    else:
        chunk_a = jnp.concatenate([chunk_a, table_own], axis=1)
    norms_head = jnp.take(jnp.stack(norms_four), slots, axis=0)
    chunk_o = jnp.concatenate([mine(w_out), out_got]).T
    gate, rows_gate = (norms_head,), norms_head
    if direct():
        norms_row = norms_head.transpose(1, 2, 0, 3).reshape(1, -1)
        chunk_o = jnp.concatenate([chunk_o, jnp.pad(norms_row, ((0, EXTRA - 1), (0, 0)))])
        part_o = Gather(chunk_o, X_FIRST)
        two_a.step(one_a.part)
        part_o.start(two_a.part)
        gate = (part_o.part,)
    tokens_late, spatial_late = after((tokens, spatial), first)
    rows_own = jnp.stack([mine(tokens_late), mine(spatial_late)])
    rows_side = swap(after(jnp.stack([other(tokens_late), other(spatial_late)]), *gate), "head", 2)
    rows_near = swap(after(rows_own, *gate), "head", 1)
    attn_got, table_got = after((attn_got, table_got), *gate)
    chunk_b = jnp.concatenate([attn_got[which] for which in sequence] + [split_table(table_got)], axis=1)
    chunk_f = jnp.concatenate([w_up.T, w_down], axis=1)
    part_b = Gather(chunk_b, FAR_X)
    if direct():
        part_f = Gather(chunk_f, FAR_X)
        part_b.start()
        one_a.step(part_b.part)
        two_a.step(one_a.part)
        part_b.step(two_a.part)
        part_o.step(part_b.part)
        rows_gate = part_b.part
        part_f.start(part_b.part, one_a.got, two_a.got)
        half_a = one_a.result() + two_a.result()
    else:
        half_a = generic_gather(chunk_a, 5 * half, 2 * own_heads)
        half_a = tuple(ref[..., :split] for ref in half_a) + tuple(ref[..., split:] for ref in half_a)
        half_b = generic_gather(chunk_b, 5 * half, 2 * own_heads)
        norms_full = by_page(gather_pages(norms_head)).transpose(2, 3, 0, 1, 4).reshape(4, GROUPS, 1, -1)
        norms_full = norms_full.transpose(1, 2, 0, 3).reshape(GROUPS, 1, -1)
        norms_full = jnp.pad(norms_full, ((0, 0), (0, EXTRA - 1), (0, 0)))
        pair_o = generic_gather(chunk_o)
        pair_o = tuple(
            jnp.concatenate([ref, extra], axis=1)
            for ref, extra in zip(pair_o, (norms_full[: GROUPS // 2], norms_full[GROUPS // 2 :]))
        )
        pair_f = generic_gather(chunk_f)
    row_parts = rows_own, rows_side, rows_near, swap(after(rows_side, rows_gate), "head", 1)

    ids = jnp.concatenate(
        [
            mine(reading_order)[None],
            mine(box_coords) // coarse,
            jnp.arange(rows, dtype=jnp.int32)[None, None] // page_len.reshape(1, batches, 1),
        ]
    )
    ids = jnp.take(ids.reshape(4, batches, 4, own), blocks, axis=2).reshape(4, batches, rows)

    state = [dict() for _ in range(batches)]
    gate_b = gate_f = gate_last = page
    if direct():
        gate_b = part_f.part
    for batch, here in enumerate(state):
        here["ids"] = (ids[:, batch],)
        *here["saved_a"], here["head_a"] = attend(
            batch, own_heads, after(page, gate_b), row_parts, half_a, *here["ids"]
        )
        gate_b = here["head_a"]
        if direct() and batch == 0:
            part_b.step(gate_b)
            part_o.step(part_b.part)
            part_f.step(part_o.part)
            gate_b = part_b.part
        elif direct():
            part_f.step(gate_b)
            gate_last = part_f.part
    if direct():
        half_b, pair_o, pair_f = part_b.result(), part_o.result(), part_f.result()
    for batch, here in enumerate(state):
        *here["saved_b"], here["head_b"], here["out_t"], here["keep"], here["send"], norms = attend(
            batch, own_heads, after(page, gate_b, gate_last), row_parts, half_b, *here["ids"],
            final=(pair_o, here["head_a"]),
        )
        gate_b = here["head_b"]
    ff_parts = pair_f + tuple(swap(ref, "head", 1) for ref in pair_f)

    wide = struct((own, features), f32)
    low = struct((own, features), bf16)
    sums = struct((2, features), f32)
    for batch, here in enumerate(state):
        keep, near, far = scatter_rows(here["keep"], here["send"])
        here["normal"], here["scale"], hidden_low = norm_call(
            norm_one_kernel, "norm_one", (wide, struct((own, 1), f32), low),
            keep[:own], near[:own], far, tokens[0, batch], tokens[1, batch], norms,
        )
        here["h"] = hidden_low, swap(hidden_low, "head", 2)
        here["act"], here["slope"], keep, send = ff_call(forward_kernel, "forward", here["h"], ff_parts, ())
        here["out"], here["dc"], dz, here["sums_two"] = norm_call(
            norm_two_kernel, "norm_two", (low, wide, low, sums),
            keep, swap(send, "head", 2), here["normal"], grad_out[batch], norms,
        )
        here["g"] = dz, swap(dz, "head", 2)
        here["grad_pre"], keep, send = ff_call(
            backward_kernel, "backward", here["g"], ff_parts, (here["act"], here["slope"])
        )
        here["da"], da_low, here["sums_one"] = norm_call(
            norm_back_kernel, "norm_back", (wide, low, sums),
            keep, swap(send, "head", 2), here["dc"], here["normal"], here["scale"], norms,
        )
        here["a"] = gather_rows(da_low)

    def every(name):
        return [here[name] for here in state]

    ours, theirs = ff_weights(every("h"), every("g"), every("grad_pre"), every("act"))
    keep_f, send_f = fold(ours, swap(theirs, "head", 1))
    part_f = Scatter(keep_f, send_f, FAR_X)
    if direct():
        part_f.start()

    def saved_of(here, name):
        return [*here[name][:4], state[0][name][4], state[0]["out_t"]]

    def back_b(here, *gate):
        here["dproj_b"], here["dtable_b"], here["part"] = attend_back(
            own_heads, 1, after(page, *gate), here["a"], saved_of(here, "saved_b"), *here["ids"]
        )
        return here["dproj_b"]

    def back_a(here, *gate):
        here["dproj_a"], here["dtable_a"], here["keep"], here["send"] = attend_back(
            own_heads, 0, after(page, *gate), here["a"], saved_of(here, "saved_a"), *here["ids"],
            here["part"],
        )
        here["near"] = swap(here["send"], "head", 1)
        return here["dproj_a"]

    gate = back_b(state[0], part_f.send, *[here["a"][0] for here in state])
    keep_o, send_o = out_weights(
        after(page, gate),
        every("a"),
        [here[name] for here in state for name in ("head_a", "head_b")],
        [here[name] for here in state for name in ("sums_one", "sums_two")],
    )
    part_o = Scatter(keep_o, send_o, FAR_X)
    gate = (send_o,)
    if direct():
        part_o.start(part_f.send)
        part_f.step(part_o.send)
        gate += (part_f.send,)
    for here in state[1:]:
        gate = (back_b(here, *gate),)
    weights_b = attn_weights(after(page, *gate), row_parts, every("dproj_b"), every("dtable_b"), split)
    one_b, two_b = Scatter(*weights_b[:2], FAR_Z), Scatter(*weights_b[2:], FAR_X)
    gate = (weights_b[1],)
    if direct():
        two_b.start(part_f.send)
        one_b.start(two_b.send)
        part_o.step(one_b.send)
        gate = (part_o.send,)
    gate = (back_a(state[0], *gate),)
    if direct():
        part_f.step(part_o.send)
        gate += (part_f.send,)
    for here in state[1:]:
        gate = (back_a(here, *gate),)
    if direct():
        two_b.step(part_f.send)
        gate += (two_b.send,)
    weights_a = attn_weights(after(page, *gate), row_parts, every("dproj_a"), every("dtable_a"), split)
    one_a, two_a = Scatter(*weights_a[:2], FAR_Z), Scatter(*weights_a[2:], FAR_X)
    if direct():
        two_a.start(two_b.send)
        one_a.start(two_a.send)
        one_b.step(one_a.send)
        part_o.step(one_b.send)
        two_b.step(part_o.send)
        two_a.step(two_b.send)
        one_b.step(two_a.send)
        one_a.step(one_b.send)
        two_a.step(one_a.send)
        grad_b = jnp.concatenate([one_b.result(one_a.send), two_b.result(one_a.send)], axis=1)
        one_a.step(two_a.send)
        dff, dout = part_f.result(one_a.send), part_o.result(one_a.send)
        grad_a = jnp.concatenate([one_a.result(), two_a.result()], axis=1)
        dnorms = dout[share].reshape(4, 4, -1).transpose(1, 0, 2)
        dout = dout[:share]
    else:
        inner = features // GROUPS
        dff = generic_scatter(keep_f, send_f)
        dout = generic_scatter(keep_o[:, :inner], send_o[:, :inner])
        flat = jnp.concatenate([keep_o[:, inner], send_o[:, inner].astype(f32)]).reshape(GROUPS, 4, -1)
        flat = flat.transpose(1, 0, 2).reshape(4, pages, 4, -1).transpose(1, 2, 0, 3)
        dnorms = scatter_pages(by_page(flat))
        grads = []
        for weights in (weights_a, weights_b):
            keep = jnp.concatenate(weights[::2], axis=2)
            send = jnp.concatenate(weights[1::2], axis=2)
            grads.append(generic_scatter(keep, send, 5 * half, 2 * own_heads))
        grad_a, grad_b = grads

    dnorms = jnp.take(dnorms, blocks, axis=0)
    pair = dnorms[:2] + swap(dnorms[2:], "head", 1)
    dnorms = (pair[0] + swap(pair[1], "head", 2)).reshape(2, 2, -1)

    def both_modalities(ours, theirs):
        got = swap(theirs.astype(bf16), "head", 2).astype(f32)
        return jnp.where(modality == 0, jnp.stack([ours, got]), jnp.stack([got, ours]))

    token_grads = []
    for here in state:
        total = here["keep"] + after(here["near"], weights_a[1]).astype(f32)
        token_grads.append(both_modalities(total[:own], total[own:]) + here["da"][None])

    got_b = swap(grad_b.astype(bf16), "head", 2).astype(f32)
    chunks = jnp.where(modality == 0, jnp.stack([grad_a, got_b]), jnp.stack([got_b, grad_a]))
    dattn = jnp.stack([chunks[:, :, which * half : (which + 1) * half] for which in (0, 1, 4, 2, 3)], axis=1)
    dtable = chunks[:, :, 5 * half :].reshape(2, 2, own_heads, step, 3, buckets // 2)
    dtable = dtable.transpose(0, 4, 2, 3, 1, 5).reshape(2, 3, own_heads, step, buckets)
    dout = dout.reshape(share, 2, half).transpose(1, 2, 0)
    return (
        jnp.stack([here["out"] for here in state]),
        jnp.stack(token_grads, axis=1).astype(bf16),
        dattn,
        dtable,
        both_modalities(dout[0], dout[1]),
        dnorms[0],
        dnorms[1],
        dff[:, :features].T,
        dff[:, features:],
    )


def solution(mesh):
    return jax.shard_map(
        local,
        mesh=mesh,
        in_specs=(
            P(None, None, ("page", "head"), None),
            P(None, None, ("page", "head"), None),
            P(None, None, None, "page"),
            P(None, None, "page"),
            P(None, "page"),
            P(None, None, "page", "head"),
            P(None, None, "head", "page", None),
            P(None, "head", "page"),
            P(None, ("page", "head")),
            P(None, ("page", "head")),
            P(None, ("page", "head")),
            P(("page", "head"), None),
            P(None, ("page", "head"), None),
        ),
        out_specs=(
            P(None, ("page", "head"), None),
            P(None, None, ("page", "head"), None),
            P(None, None, "page", "head"),
            P(None, None, "head", "page", None),
            P(None, "head", "page"),
            P(None, ("page", "head")),
            P(None, ("page", "head")),
            P(None, ("page", "head")),
            P(("page", "head"), None),
        ),
        check_vma=False,
    )
```

```python
import functools

import jax
import jax.numpy as jnp
from jax import lax
from jax.experimental import pallas as pl
from jax.experimental.pallas import tpu as pltpu
from jax.sharding import PartitionSpec as P

COORD = 1024
EPS = 1e-05
GROUPS = 8
SCALE = 7e+08
EXTRA = 16
f32 = jnp.float32
bf16 = jnp.bfloat16
AB = ((1,), (0,))
ABT = ((1,), (1,))
ATB = ((0,), (0,))
SMEM = pl.BlockSpec(memory_space=pltpu.SMEM)
VM = pl.BlockSpec(memory_space=pltpu.VMEM)
HBM = pl.BlockSpec(memory_space=pltpu.HBM)
PARAMS = pltpu.CompilerParams(vmem_limit_bytes=14 * 1024 * 1024)
FAR_X = (4, 2, 1)
FAR_Z = (4, 1, 2)
X_FIRST = (1, 4, 2)


def cost(microseconds):
    return pl.CostEstimate(
        flops=int(microseconds * SCALE), bytes_accessed=int(microseconds * 3e5), transcendentals=0
    )


def struct(shape, kind):
    return pltpu.VMEM(tuple(shape), kind)


def pin(*values):
    return [pltpu.with_memory_space_constraint(value, pltpu.VMEM) for value in values]


def dot(left, right, dims):
    return lax.dot_general(left, right, (dims, ((), ())), preferred_element_type=f32)


def swap(value, axis, mask):
    count = lax.axis_size(axis)
    return lax.ppermute(value, axis, [(place, place ^ mask) for place in range(count)])


def after(value, *earlier):
    return lax.optimization_barrier((value, earlier))[0]


def gather_rows(own):
    side = swap(own, "head", 2)
    return own, side, swap(own, "head", 1), swap(side, "head", 1)


def scatter_rows(keep, send):
    own = keep.shape[0] // 2
    near = swap(send, "head", 1)
    far = swap((keep[own:] + near[own:].astype(f32)).astype(bf16), "head", 2)
    return keep, near, far


def page_bits():
    count = lax.axis_size("page")
    return [1 << bit for bit in reversed(range(count.bit_length() - 1))]


def gather_pages(own):
    full = own
    for depth, mask in enumerate(page_bits()):
        full = jnp.stack([full, swap(full, "page", mask)], axis=depth)
    return full.reshape((lax.axis_size("page"),) + own.shape)


def scatter_pages(blocks):
    masks = page_bits()
    part = blocks.reshape((2,) * len(masks) + blocks.shape[1:])
    for depth in reversed(range(len(masks))):
        keep = lax.index_in_dim(part, 0, depth, keepdims=False)
        send = lax.index_in_dim(part, 1, depth, keepdims=False)
        part = keep.astype(f32) + swap(send.astype(bf16), "page", masks[depth]).astype(f32)
    return part


def by_page(blocks):
    count = blocks.shape[0]
    order = jnp.arange(count, dtype=jnp.int32) ^ lax.axis_index("page")
    return jnp.take(blocks, order, axis=0)


def regroup(full, heads):
    pages, share, columns = full.shape
    if heads == 1:
        return full.reshape(GROUPS, -1, columns)
    parts = full.reshape(GROUPS, pages // GROUPS, heads, share // heads, columns)
    return parts.transpose(0, 2, 1, 3, 4).reshape(GROUPS, -1, columns)


def ungroup(full, pages, heads):
    columns = full.shape[2]
    if heads == 1:
        return full.reshape(pages, -1, columns)
    parts = full.reshape(GROUPS, heads, pages // GROUPS, -1, columns)
    return parts.transpose(0, 2, 1, 3, 4).reshape(pages, -1, columns)


def direct():
    return lax.axis_size("page") == GROUPS


def join_kernel(first_ref, second_ref, out_ref):
    half = first_ref.shape[0]
    out_ref[:half] = first_ref[...]
    out_ref[half:] = second_ref[...]


def join(first, second):
    return pl.pallas_call(
        join_kernel,
        in_specs=[VM] * 2,
        out_shape=struct((2 * first.shape[0],) + first.shape[1:], first.dtype),
        compiler_params=PARAMS,
        cost_estimate=cost(0.4),
        name="join",
    )(*pin(first, second))


def fold_kernel(first_ref, second_ref, keep_ref, send_ref):
    half = keep_ref.shape[0]
    keep_ref[...] = first_ref[:half].astype(f32) + second_ref[:half].astype(f32)
    send_ref[...] = (first_ref[half:].astype(f32) + second_ref[half:].astype(f32)).astype(bf16)


def fold(first, second):
    half = (first.shape[0] // 2,) + first.shape[1:]
    return pl.pallas_call(
        fold_kernel,
        in_specs=[VM] * 2,
        out_shape=(struct(half, f32), struct(half, bf16)),
        compiler_params=PARAMS,
        cost_estimate=cost(0.48),
        name="fold",
    )(*pin(first, second))


class Gather:
    def __init__(self, share, masks):
        self.part, self.masks = share[None], list(masks)

    def start(self, *earlier):
        self.part = after(self.part, *earlier)
        self.got = swap(self.part, "page", self.masks.pop(0))

    def step(self, *earlier):
        self.part = join(self.part, after(self.got, *earlier))
        self.start(*earlier)

    def result(self):
        return self.part, self.got


def generic_gather(share, columns=None, heads=1):
    full = by_page(gather_pages(share))
    if heads == 1:
        full = regroup(full, 1)
    else:
        full = jnp.concatenate([regroup(full[..., :columns], 1), regroup(full[..., columns:], heads)], axis=2)
    return full[: GROUPS // 2], full[GROUPS // 2 :]


class Scatter:
    def __init__(self, keep, send, masks):
        self.keep, self.send, self.masks = keep, send, list(masks)

    def start(self, *earlier):
        self.send = after(self.send, *earlier)
        self.got = swap(self.send, "page", self.masks.pop())

    def step(self, *earlier):
        self.keep, self.send = fold(self.keep, after(self.got, *earlier))
        self.start(*earlier)

    def result(self, *earlier):
        return self.keep[0] + after(self.got, *earlier)[0].astype(f32)


def generic_scatter(keep, send, columns=None, heads=1):
    pages = lax.axis_size("page")
    full = jnp.concatenate([keep.astype(bf16), send])
    if heads == 1:
        full = ungroup(full, pages, 1)
    else:
        full = jnp.concatenate(
            [ungroup(full[..., :columns], pages, 1), ungroup(full[..., columns:], pages, heads)], axis=2
        )
    return scatter_pages(by_page(full))


def places(masks):
    if not direct():
        masks = (1, 2, 4)
    return [
        sum(mask for bit, mask in enumerate(masks) if (place >> bit) & 1) for place in range(GROUPS)
    ]


def page_of(place, page, masks):
    if not direct():
        masks = (1, 2, 4)
    for bit, mask in enumerate(masks):
        page = jnp.bitwise_xor(page, jnp.bitwise_and(lax.shift_right_logical(place, bit), 1) * mask)
    return page


def load_chunk(page, refs, masks, target, start=0):
    share = target.shape[0] // GROUPS
    stop = start + refs[0].shape[2]
    for half, ref in enumerate(refs):

        def body(place, carry):
            row = page_of(place + half * (GROUPS // 2), page, masks) * share
            target[pl.ds(pl.multiple_of(row, share), share), start:stop] = ref[place, :share]
            return carry

        lax.fori_loop(0, GROUPS // 2, body, 0)


def load_rows(refs, target, *pick):
    count = refs[0].shape[-2]
    for place, ref in enumerate(refs):
        target[place * count : (place + 1) * count] = ref[pick] if pick else ref[...]


def load_extra(page, refs, masks, target):
    share = refs[0].shape[1] - EXTRA
    for place, number in enumerate(places(masks)):
        target[jnp.bitwise_xor(page, number)] = refs[place // (GROUPS // 2)][place % (GROUPS // 2), share:]


def load_split(page, refs, target):
    if len(refs) == 2:
        load_chunk(page, refs, FAR_X, target)
    else:
        load_chunk(page, refs[:2], FAR_Z, target)
        load_chunk(page, refs[2:], FAR_X, target, refs[0].shape[2])


def turned(ids_ref):
    ids = ids_ref[...].astype(f32)
    return jnp.concatenate([ids, ids]).T


def hot_columns(ids, which, buckets):
    lane = lax.broadcasted_iota(jnp.int32, (ids.shape[0], buckets), 1).astype(f32)
    return jnp.where(ids[:, which : which + 1] == lane, 1.0, 0.0).astype(bf16)


def table_rows(head, heads, small):
    return [pl.multiple_of((side * heads + head) * small, small) for side in range(2)]


def attend_kernel(batch, heads, last, page_ref, *refs):
    parts = 2 if last else 4
    rows_refs, w_refs, refs = refs[:4], refs[4 : 4 + parts], refs[4 + parts :]
    if last:
        o_refs, other_ref, refs = refs[:2], refs[2], refs[3:]
    idr_ref, saved, head_ref, refs = refs[0], refs[1:6], refs[6], refs[7:]
    if last:
        saved += refs[:1]
        keep_ref, send_ref, norms_ref, refs = refs[1], refs[2], refs[3], refs[4:]
        wo_ref, extra_ref, refs = refs[0], refs[1], refs[2:]
    left_ref, right_ref, value_ref, prob_ref, w_ref, x_ref, s_ref, hot_ref, head_part_ref, sems = refs
    page = page_ref[0]
    load_rows(rows_refs, x_ref, 0, batch)
    load_rows(rows_refs, s_ref, 1, batch)
    load_split(page, w_refs, w_ref)
    copies = [pltpu.make_async_copy(w_ref, saved[4], sems.at[0])]
    if last:
        load_chunk(page, o_refs, X_FIRST, wo_ref)
        load_extra(page, o_refs, X_FIRST, extra_ref)
        copies.append(pltpu.make_async_copy(wo_ref, saved[5], sems.at[1]))
    rows = x_ref.shape[0]
    width = w_ref.shape[1] // 6
    share = w_ref.shape[0] // GROUPS
    size = width // heads
    buckets = 2 * width // 3
    small, wide = buckets // GROUPS, buckets // 2
    columns = turned(idr_ref)
    for which in range(3):
        hot_ref[:, which * buckets : (which + 1) * buckets] = hot_columns(columns, which, buckets)
    same = columns[:, 3:4] == idr_ref[3:4, :].astype(f32)
    first = dot(x_ref[...], w_ref[:, : 2 * width], AB).astype(bf16)
    second = dot(s_ref[...], w_ref[:, 2 * width : 4 * width], AB).astype(bf16)
    third = dot(x_ref[...], w_ref[:, 4 * width : 5 * width], AB).astype(bf16)
    for head in range(heads):
        low, high = slice(head * size, (head + 1) * size), slice(width + head * size, width + (head + 1) * size)
        left_ref[head] = jnp.concatenate([first[:, low], second[:, low]], axis=1) * bf16(0.125)
        right_ref[head] = jnp.concatenate([first[:, high], second[:, high]], axis=1)
        value_ref[head] = third[:, low]
    for at, ref in enumerate((left_ref, right_ref, value_ref)):
        copies.append(pltpu.make_async_copy(ref, saved[at], sems.at[2 + at]))
    for copy in copies:
        copy.start()

    def save_prob(head):
        return pltpu.make_async_copy(prob_ref.at[head], saved[3].at[head], sems.at[5 + head])

    def body(head, carry):
        sides = []
        for start in table_rows(head, heads, small):
            pieces = [w_ref[pl.ds(group * share + start, small), 5 * width :] for group in range(GROUPS)]
            sides.append(jnp.concatenate(pieces))
        parts = [left_ref[head]]
        for which in range(3):
            table = jnp.concatenate([side[:, which * wide : (which + 1) * wide] for side in sides], axis=1)
            parts.append(dot(hot_ref[:, which * buckets : (which + 1) * buckets], table, AB).astype(bf16))
        left = jnp.concatenate(parts, axis=1)
        right = jnp.concatenate([right_ref[head], hot_ref[...]], axis=1)
        score = jnp.where(same, dot(left, right, ABT), -1e30)
        weight = jnp.exp(score - jnp.max(score, axis=1, keepdims=True))
        prob = (weight * (1.0 / jnp.sum(weight, axis=1, keepdims=True))).astype(bf16)
        prob_ref[head] = prob
        save_prob(head).start()
        head_part_ref[head] = dot(prob, value_ref[head], AB).astype(bf16)
        return carry

    lax.fori_loop(0, heads, body, 0)
    head_ref[...] = jnp.concatenate([head_part_ref[head] for head in range(heads)], axis=1)
    if last:
        part = dot(other_ref[...], wo_ref[:, :width], ABT) + dot(head_ref[...], wo_ref[:, width:], ABT)
        keep_ref[...] = part[: rows // 2]
        send_ref[...] = part[rows // 2 :].astype(bf16)
        inner = norms_ref.shape[1] // GROUPS
        for group in range(GROUPS):
            for which in range(norms_ref.shape[0]):
                norms_ref[which : which + 1, group * inner : (group + 1) * inner] = extra_ref[
                    group, 0:1, which * inner : (which + 1) * inner
                ].astype(f32)
    for copy in copies:
        copy.wait()
    for head in range(heads):
        save_prob(head).wait()


def attend(batch, heads, page, row_parts, chunk, ids_row, final=None):
    rows = ids_row.shape[1]
    features = row_parts[0].shape[-1]
    columns = sum(ref.shape[2] for ref in chunk[::2])
    width = columns // 6
    size = width // heads
    saved = [
        ((heads, rows, 2 * size), bf16),
        ((heads, rows, 2 * size), bf16),
        ((heads, rows, size), bf16),
        ((heads, rows, rows), bf16),
        ((features, columns), bf16),
    ]
    scratch = [pltpu.VMEM(shape, kind) for shape, kind in saved]
    more = ()
    extra_outs, first_scratch = (), []
    if final is not None:
        pair_o, other = final
        more = (*pair_o, other)
        extra_outs = (
            pltpu.HBM((features, 2 * width), bf16),
            struct((rows // 2, features), f32), struct((rows // 2, features), bf16), struct((4, features), f32),
        )
        first_scratch = [pltpu.VMEM((features, 2 * width), bf16), pltpu.VMEM((GROUPS, EXTRA, 2 * width), bf16)]
    outs = tuple(pltpu.HBM(shape, kind) for shape, kind in saved) + (struct((rows, width), bf16),)
    return pl.pallas_call(
        functools.partial(attend_kernel, batch, heads, final is not None),
        in_specs=[SMEM] + [VM] * (4 + len(chunk) + len(more) + 1),
        out_specs=[HBM] * 5 + [VM] + ([] if final is None else [HBM, VM, VM, VM]),
        out_shape=outs + extra_outs,
        scratch_shapes=first_scratch + scratch + [
            pltpu.VMEM((rows, features), bf16),
            pltpu.VMEM((rows, features), bf16),
            pltpu.VMEM((rows, 2 * width), bf16),
            pltpu.VMEM((heads, rows, size), bf16),
            pltpu.SemaphoreType.DMA((5 + heads,)),
        ],
        compiler_params=PARAMS,
        cost_estimate=cost(6.3),
        name="attend",
    )(page, *pin(*row_parts, *chunk, *more, ids_row))


def attend_back_kernel(heads, half, page_ref, *refs):
    da_refs, saved, idr_ref, refs = refs[:4], refs[4:10], refs[10], refs[11:]
    if half == 0:
        other_ref, dproj_ref, dtable_ref, keep_ref, send_ref, refs = refs[0], refs[1], refs[2], refs[3], refs[4], refs[5:]
    else:
        dproj_ref, dtable_ref, part_ref, refs = refs[0], refs[1], refs[2], refs[3:]
    left_ref, right_ref, value_ref, prob_ref, w_ref, wo_ref, refs = refs[0], refs[1], refs[2], refs[3], refs[4], refs[5], refs[6:]
    da_ref, hot_ref, grad_ref, dleft_ref, dright_ref, dvalue_ref, sems = refs
    early = [
        pltpu.make_async_copy(source, target, sems.at[at])
        for at, (source, target) in enumerate(
            ((saved[5], wo_ref), (saved[2], value_ref), (saved[1], right_ref), (saved[0], left_ref))
        )
    ]
    late = pltpu.make_async_copy(saved[4], w_ref, sems.at[4])

    def fetch_prob(head):
        return pltpu.make_async_copy(saved[3].at[head], prob_ref.at[head], sems.at[5 + head])

    early[0].start()
    early[1].start()
    fetch_prob(0).start()
    early[2].start()
    early[3].start()
    for head in range(1, heads):
        fetch_prob(head).start()
    late.start()
    load_rows(da_refs, da_ref)
    rows = da_ref.shape[0]
    width = w_ref.shape[1] // 6
    size = width // heads
    buckets = 2 * width // 3
    small, wide = buckets // GROUPS, buckets // 2
    columns = turned(idr_ref)
    for which in range(3):
        hot_ref[:, which * buckets : (which + 1) * buckets] = hot_columns(columns, which, buckets)
    bucket = lax.broadcasted_iota(jnp.int32, (buckets, rows), 0)
    early[0].wait()
    grad_heads = dot(da_ref[...], wo_ref[:, half * width : (half + 1) * width], AB).astype(bf16)
    for head in range(heads):
        grad_ref[head] = grad_heads[:, head * size : (head + 1) * size]
    for copy in early[1:]:
        copy.wait()

    def body(head, carry):
        fetch_prob(head).wait()
        prob = prob_ref[head]
        grad_out = grad_ref[head]
        grad_prob = dot(grad_out, value_ref[head], ABT)
        weighted = prob.astype(f32) * grad_prob
        row_dot = jnp.sum(weighted, axis=1, keepdims=True)
        grad_score = (weighted - prob.astype(f32) * row_dot).astype(bf16)
        dvalue_ref[head] = dot(prob, grad_out, ATB).astype(bf16)
        right = jnp.concatenate([right_ref[head], hot_ref[...]], axis=1)
        spread = dot(grad_score, right, AB)
        dleft_ref[head] = (spread[:, : 2 * size] * 0.125).astype(bf16)
        dright_ref[head] = dot(grad_score, left_ref[head], ATB).astype(bf16)
        pieces = []
        for which in range(3):
            start = 2 * size + which * buckets
            hot_t = jnp.where(idr_ref[which : which + 1, :] == bucket, 1.0, 0.0).astype(bf16)
            pieces.append(dot(hot_t, spread[:, start : start + buckets].astype(bf16), AB))
        for side, start in enumerate(table_rows(head, heads, small)):
            block = jnp.concatenate([piece[:, side * wide : (side + 1) * wide] for piece in pieces], axis=1)
            for group in range(GROUPS):
                dtable_ref[group, pl.ds(start, small), :] = block[group * small : (group + 1) * small]
        return carry

    lax.fori_loop(0, heads, body, 0)
    every = range(heads)
    dproj_ref[:, :width] = jnp.concatenate([dleft_ref[head][:, :size] for head in every], axis=1)
    dproj_ref[:, width : 2 * width] = jnp.concatenate([dright_ref[head][:, :size] for head in every], axis=1)
    dproj_ref[:, 2 * width : 3 * width] = jnp.concatenate([dleft_ref[head][:, size:] for head in every], axis=1)
    dproj_ref[:, 3 * width : 4 * width] = jnp.concatenate([dright_ref[head][:, size:] for head in every], axis=1)
    dproj_ref[:, 4 * width :] = jnp.concatenate([dvalue_ref[head] for head in every], axis=1)
    late.wait()
    part = dot(dproj_ref[:, : 2 * width], w_ref[:, : 2 * width], ABT)
    part = part + dot(dproj_ref[:, 4 * width :], w_ref[:, 4 * width : 5 * width], ABT)
    if half == 0:
        part = part + other_ref[...]
        keep_ref[...] = part[: rows // 2]
        send_ref[...] = part[rows // 2 :].astype(bf16)
    else:
        part_ref[...] = part


def attend_back(heads, half, page, da_parts, saved, ids_row, other=None):
    rows = ids_row.shape[1]
    features = da_parts[0].shape[-1]
    width = saved[4].shape[1] // 6
    size = width // heads
    outs = (struct((rows, 5 * width), bf16), struct((GROUPS, features // GROUPS, width), f32))
    if half == 0:
        outs += (struct((rows // 2, features), f32), struct((rows // 2, features), bf16))
    else:
        outs += (struct((rows, features), f32),)
    return pl.pallas_call(
        functools.partial(attend_back_kernel, heads, half),
        in_specs=[SMEM] + [VM] * 4 + [HBM] * 6 + [VM] * (2 if half == 0 else 1),
        out_shape=outs,
        scratch_shapes=[pltpu.VMEM(ref.shape, ref.dtype) for ref in saved]
        + [
            pltpu.VMEM((rows, features), bf16),
            pltpu.VMEM((rows, 2 * width), bf16),
            pltpu.VMEM((heads, rows, size), bf16),
            pltpu.VMEM((heads, rows, 2 * size), bf16),
            pltpu.VMEM((heads, rows, 2 * size), bf16),
            pltpu.VMEM((heads, rows, size), bf16),
            pltpu.SemaphoreType.DMA((5 + heads,)),
        ],
        compiler_params=PARAMS,
        cost_estimate=cost(6),
        name="attend_back",
    )(page, *pin(*da_parts), *[pltpu.with_memory_space_constraint(ref, pltpu.HBM) for ref in saved], *pin(ids_row, *([other] if half == 0 else [])))


def put_blocks(page, masks, full_ref, columns, keep_ref, send_ref):
    half = GROUPS // 2

    def body(place, carry):
        keep_ref[place] = full_ref[page_of(place, page, masks), :, columns]
        send_ref[place] = full_ref[page_of(place + half, page, masks), :, columns].astype(bf16)
        return carry

    lax.fori_loop(0, half, body, 0)


def attn_weights_kernel(batches, split, page_ref, *refs):
    rows_refs, dproj_refs, dtable_refs = refs[:4], refs[4 : 4 + batches], refs[4 + batches : 4 + 2 * batches]
    out_refs, (x_ref, d_ref, full_ref) = refs[4 + 2 * batches : -3], refs[-3:]
    page = page_ref[0]
    rows = x_ref.shape[1] // batches
    for batch in range(batches):
        at = pl.ds(batch * rows, rows)
        for which in range(2):
            load_rows(rows_refs, x_ref.at[which, at], which, batch)
        d_ref[at] = dproj_refs[batch][...]
    width = d_ref.shape[1] // 5

    def blocks(value):
        return value.reshape(GROUPS, value.shape[0] // GROUPS, value.shape[1])

    x_t = x_ref[0].T
    full_ref[:, :, : 2 * width] = blocks(dot(x_t, d_ref[:, : 2 * width], AB))
    full_ref[:, :, 2 * width : 4 * width] = blocks(dot(x_ref[1].T, d_ref[:, 2 * width : 4 * width], AB))
    full_ref[:, :, 4 * width : 5 * width] = blocks(dot(x_t, d_ref[:, 4 * width :], AB))
    total = dtable_refs[0][...]
    for ref in dtable_refs[1:]:
        total = total + ref[...]
    full_ref[:, :, 5 * width :] = total
    if split:
        put_blocks(page, FAR_Z, full_ref, slice(0, split), *out_refs[:2])
    put_blocks(page, FAR_X, full_ref, slice(split, 6 * width), *out_refs[-2:])


def attn_weights(page, row_parts, dprojs, dtables, split):
    batches = len(dprojs)
    rows, columns = dprojs[0].shape
    columns = 6 * (columns // 5)
    features = row_parts[0].shape[-1]
    inner = features // GROUPS
    outs = ()
    for count in (split, columns - split) if split else (columns,):
        outs += (struct((GROUPS // 2, inner, count), f32), struct((GROUPS // 2, inner, count), bf16))
    return pl.pallas_call(
        functools.partial(attn_weights_kernel, batches, split),
        in_specs=[SMEM] + [VM] * (4 + batches) + [VM] * batches,
        out_shape=outs,
        scratch_shapes=[
            pltpu.VMEM((2, batches * rows, features), bf16),
            pltpu.VMEM((batches * rows, dprojs[0].shape[1]), bf16),
            pltpu.VMEM((GROUPS, inner, columns), f32),
        ],
        compiler_params=PARAMS,
        cost_estimate=cost(3.12),
        name="attn_weights",
    )(page, *pin(*row_parts, *dprojs, *dtables))


def out_weights_kernel(batches, page_ref, *refs):
    da_refs, head_refs, refs = refs[: 4 * batches], refs[4 * batches : 6 * batches], refs[6 * batches :]
    sums_refs, refs = refs[: 2 * batches], refs[2 * batches :]
    keep_ref, send_ref, da_ref, head_ref, full_ref = refs
    page = page_ref[0]
    rows = da_ref.shape[0] // batches
    width = head_ref.shape[2]
    for batch in range(batches):
        at = pl.ds(batch * rows, rows)
        load_rows(da_refs[4 * batch : 4 * batch + 4], da_ref.at[at])
        for half in range(2):
            head_ref[half, at] = head_refs[2 * batch + half][...]
    share = da_ref.shape[1] // GROUPS
    full_ref[:, share:, :] = jnp.zeros((GROUPS, EXTRA, 2 * width), f32)
    for layer in range(2):
        total = sums_refs[layer][...]
        for batch in range(1, batches):
            total = total + sums_refs[2 * batch + layer][...]
        for which in range(2):
            for group in range(GROUPS):
                start = (2 * which + layer) * share
                full_ref[group, share : share + 1, start : start + share] = total[
                    which : which + 1, group * share : (group + 1) * share
                ]
    da_t = da_ref[...].T
    for half in range(2):
        full_ref[:, :share, half * width : (half + 1) * width] = dot(da_t, head_ref[half], AB).reshape(
            GROUPS, share, width
        )
    put_blocks(page, FAR_X, full_ref, slice(0, 2 * width), keep_ref, send_ref)


def out_weights(page, da_parts, head_rows, sums):
    batches = len(da_parts)
    rows, width = head_rows[0].shape
    features = da_parts[0][0].shape[-1]
    chunk = (GROUPS // 2, features // GROUPS + EXTRA, 2 * width)
    return pl.pallas_call(
        functools.partial(out_weights_kernel, batches),
        in_specs=[SMEM] + [VM] * (6 * batches) + [VM] * (2 * batches),
        out_shape=(struct(chunk, f32), struct(chunk, bf16)),
        scratch_shapes=[
            pltpu.VMEM((batches * rows, features), bf16),
            pltpu.VMEM((2, batches * rows, width), bf16),
            pltpu.VMEM((GROUPS,) + chunk[1:], f32),
        ],
        compiler_params=PARAMS,
        cost_estimate=cost(2.7),
        name="out_weights",
    )(page, *pin(*[ref for parts in da_parts for ref in parts], *head_rows, *sums))


def hidden_weights(refs):
    return jnp.concatenate([ref[...].reshape(-1, ref.shape[2]) for ref in refs])


def forward_kernel(own_ref, side_ref, *refs):
    f_refs, (act_ref, slope_ref, keep_ref, send_ref) = refs[:4], refs[4:]
    own, features = own_ref.shape
    rows = jnp.concatenate([own_ref[...], side_ref[...]])
    weight = hidden_weights(f_refs)
    pre = dot(rows, weight[:, :features], ABT)
    normal = 0.5 + 0.5 * lax.erf(pre * 0.7071067811865476)
    act = (pre * normal).astype(bf16)
    act_ref[...] = act
    slope_ref[...] = (normal + pre * jnp.exp(-0.5 * pre * pre) * 0.3989422804014327).astype(bf16)
    part = dot(act, weight[:, features:], AB)
    keep_ref[...] = part[:own]
    send_ref[...] = part[own:].astype(bf16)


def backward_kernel(own_ref, side_ref, *refs):
    f_refs, (act_ref, slope_ref, pre_ref, keep_ref, send_ref) = refs[:4], refs[4:]
    own, features = own_ref.shape
    rows = jnp.concatenate([own_ref[...], side_ref[...]])
    weight = hidden_weights(f_refs)
    grad_act = dot(rows, weight[:, features:], ABT)
    grad_pre = (grad_act * slope_ref[...].astype(f32)).astype(bf16)
    pre_ref[...] = grad_pre
    part = dot(grad_pre, weight[:, :features], AB)
    keep_ref[...] = part[:own]
    send_ref[...] = part[own:].astype(bf16)


def ff_call(kernel, name, parts, weights, saved):
    own, features = parts[0].shape
    hidden = sum(ref.shape[0] * ref.shape[1] for ref in weights)
    outs = (struct((2 * own, hidden), bf16),) * (1 if saved else 2)
    return pl.pallas_call(
        kernel,
        in_specs=[VM] * (6 + len(saved)),
        out_shape=outs + (struct((own, features), f32), struct((own, features), bf16)),
        compiler_params=PARAMS,
        cost_estimate=cost(1.8),
        name=name,
    )(*pin(*parts, *weights, *saved))


def ff_weights_kernel(batches, *refs):
    h_refs, g_refs = refs[: 2 * batches], refs[2 * batches : 4 * batches]
    pre_refs, act_refs = refs[4 * batches : 5 * batches], refs[5 * batches : 6 * batches]
    ours_ref, theirs_ref = refs[6 * batches :]
    features = ours_ref.shape[2]
    features = features // 2
    half = GROUPS * ours_ref.shape[1]
    shape = ours_ref.shape[:2] + (features,)
    for left_refs, right_refs, at in ((pre_refs, h_refs, 0), (act_refs, g_refs, features)):
        left = jnp.concatenate([ref[...] for ref in left_refs])
        right = jnp.concatenate([ref[...] for ref in right_refs])
        total = dot(left, right, ATB).astype(bf16)
        ours_ref[:, :, at : at + features] = total[:half].reshape(shape)
        theirs_ref[:, :, at : at + features] = total[half:].reshape(shape)


def ff_weights(h_parts, g_parts, grad_pres, acts):
    batches = len(acts)
    hidden = acts[0].shape[1]
    features = h_parts[0][0].shape[1]
    chunk = (GROUPS, hidden // (2 * GROUPS), 2 * features)
    return pl.pallas_call(
        functools.partial(ff_weights_kernel, batches),
        in_specs=[VM] * (6 * batches),
        out_shape=(struct(chunk, bf16), struct(chunk, bf16)),
        compiler_params=PARAMS,
        cost_estimate=cost(3.36),
        name="ff_weights",
    )(*pin(*[ref for parts in h_parts + g_parts for ref in parts], *grad_pres, *acts))


def normalize(value):
    centred = value - jnp.mean(value, axis=1, keepdims=True)
    scale = lax.rsqrt(jnp.mean(centred * centred, axis=1, keepdims=True) + EPS)
    return centred * scale, scale


def normalize_back(grad, normal, scale, gain):
    inner = grad * gain
    inner = inner - jnp.mean(inner, axis=1, keepdims=True) - normal * jnp.mean(inner * normal, axis=1, keepdims=True)
    return inner * scale


def norm_sums(grad, normal):
    gain = jnp.sum(grad * normal, axis=0, keepdims=True)
    shift = jnp.sum(grad, axis=0, keepdims=True)
    return jnp.concatenate([gain, shift], axis=0)


def norm_one_kernel(keep_ref, near_ref, far_ref, first_ref, second_ref, norms_ref, normal_ref, scale_ref, low_ref):
    value = first_ref[...].astype(f32) + second_ref[...].astype(f32)
    value = value + (keep_ref[...] + near_ref[...].astype(f32) + far_ref[...].astype(f32))
    normal, scale = normalize(value)
    normal_ref[...] = normal
    scale_ref[...] = scale
    low_ref[...] = (normal * norms_ref[0:1] + norms_ref[2:3]).astype(bf16)


def norm_two_kernel(keep_ref, far_ref, normal_ref, grad_ref, norms_ref, out_ref, dc_ref, dz_ref, sums_ref):
    value = normal_ref[...] * norms_ref[0:1] + norms_ref[2:3]
    value = value + (keep_ref[...] + far_ref[...].astype(f32))
    normal, scale = normalize(value)
    out_ref[...] = (normal * norms_ref[1:2] + norms_ref[3:4]).astype(bf16)
    grad = grad_ref[...].astype(f32)
    dc = normalize_back(grad, normal, scale, norms_ref[1:2])
    dc_ref[...] = dc
    dz_ref[...] = dc.astype(bf16)
    sums_ref[...] = norm_sums(grad, normal)


def norm_back_kernel(keep_ref, far_ref, dc_ref, normal_ref, scale_ref, norms_ref, da_ref, low_ref, sums_ref):
    grad = dc_ref[...] + (keep_ref[...] + far_ref[...].astype(f32))
    normal = normal_ref[...]
    da = normalize_back(grad, normal, scale_ref[...], norms_ref[0:1])
    da_ref[...] = da
    low_ref[...] = da.astype(bf16)
    sums_ref[...] = norm_sums(grad, normal)


def norm_call(kernel, name, outs, *args):
    return pl.pallas_call(kernel, in_specs=[VM] * len(args), out_shape=outs, compiler_params=PARAMS, cost_estimate=cost(0.6), name=name)(*pin(*args))


def local(
    tokens,
    spatial,
    box_coords,
    reading_order,
    page_len,
    w_attn,
    tables,
    w_out,
    ln_gain,
    ln_shift,
    w_up,
    w_down,
    grad_out,
):
    batches, own, features = tokens.shape[1:]
    rows = box_coords.shape[3]
    buckets = tables.shape[4]
    own_heads = tables.shape[2]
    heads = 2 * own_heads
    half = w_attn.shape[3]
    width = 2 * half
    share = w_attn.shape[2]
    step = tables.shape[3]
    coarse = COORD // buckets
    head_index = lax.axis_index("head")
    modality = head_index // 2
    pages = lax.axis_size("page")
    page_index = lax.axis_index("page")
    page = (page_index if direct() else page_index * 0).astype(jnp.int32).reshape(1)

    def mine(value):
        return lax.dynamic_index_in_dim(value, modality, 0, keepdims=False)

    def other(value):
        return lax.dynamic_index_in_dim(value, 1 - modality, 0, keepdims=False)

    def split_table(value):
        pieces = value.reshape(3, own_heads, step, 2, buckets // 2).transpose(3, 1, 2, 0, 4)
        return pieces.reshape(share, half)

    split = 5 * features // 6
    turns = jnp.array([0, 2, 1, 3], jnp.int32)
    blocks = turns ^ head_index
    slots = jnp.take(turns, jnp.arange(4, dtype=jnp.int32) ^ head_index)
    sequence = (0, 1, 3, 4, 2)
    attn_own = mine(w_attn)
    chunk_a = jnp.concatenate([attn_own[which] for which in sequence], axis=1)
    one_a = Gather(chunk_a[:, :split], FAR_Z)
    if direct():
        one_a.start()
    first = one_a.part
    attn_send = other(after(w_attn, first))
    attn_got = swap(attn_send, "head", 2)
    table_own = split_table(mine(after(tables, attn_send)))
    two_a = Gather(jnp.concatenate([chunk_a[:, split:], table_own], axis=1), FAR_X)
    if direct():
        two_a.start()
    table_got = swap(other(after(tables, two_a.part)), "head", 2)
    out_got = swap(other(after(w_out, two_a.part)), "head", 2)
    norms_own = after(jnp.stack([ln_gain, ln_shift]), two_a.part)
    norms_four = gather_rows(norms_own)
    if direct():
        one_a.step(two_a.part)
        out_got, norms_four = after((out_got, norms_four), one_a.part)
    else:
        chunk_a = jnp.concatenate([chunk_a, table_own], axis=1)
    norms_head = jnp.take(jnp.stack(norms_four), slots, axis=0)
    chunk_o = jnp.concatenate([mine(w_out), out_got]).T
    gate, rows_gate = (norms_head,), norms_head
    if direct():
        norms_row = norms_head.transpose(1, 2, 0, 3).reshape(1, -1)
        chunk_o = jnp.concatenate([chunk_o, jnp.pad(norms_row, ((0, EXTRA - 1), (0, 0)))])
        part_o = Gather(chunk_o, X_FIRST)
        two_a.step(one_a.part)
        part_o.start(two_a.part)
        gate = (part_o.part,)
    tokens_late, spatial_late = after((tokens, spatial), first)
    rows_own = jnp.stack([mine(tokens_late), mine(spatial_late)])
    rows_side = swap(after(jnp.stack([other(tokens_late), other(spatial_late)]), *gate), "head", 2)
    rows_near = swap(after(rows_own, *gate), "head", 1)
    attn_got, table_got = after((attn_got, table_got), *gate)
    chunk_b = jnp.concatenate([attn_got[which] for which in sequence] + [split_table(table_got)], axis=1)
    chunk_f = jnp.concatenate([w_up.T, w_down], axis=1)
    part_b = Gather(chunk_b, FAR_X)
    if direct():
        part_f = Gather(chunk_f, FAR_X)
        part_b.start()
        one_a.step(part_b.part)
        two_a.step(one_a.part)
        part_b.step(two_a.part)
        part_o.step(part_b.part)
        rows_gate = part_b.part
        part_f.start(part_b.part, one_a.got, two_a.got)
        half_a = one_a.result() + two_a.result()
    else:
        half_a = generic_gather(chunk_a, 5 * half, 2 * own_heads)
        half_a = tuple(ref[..., :split] for ref in half_a) + tuple(ref[..., split:] for ref in half_a)
        half_b = generic_gather(chunk_b, 5 * half, 2 * own_heads)
        norms_full = by_page(gather_pages(norms_head)).transpose(2, 3, 0, 1, 4).reshape(4, GROUPS, 1, -1)
        norms_full = norms_full.transpose(1, 2, 0, 3).reshape(GROUPS, 1, -1)
        norms_full = jnp.pad(norms_full, ((0, 0), (0, EXTRA - 1), (0, 0)))
        pair_o = generic_gather(chunk_o)
        pair_o = tuple(
            jnp.concatenate([ref, extra], axis=1)
            for ref, extra in zip(pair_o, (norms_full[: GROUPS // 2], norms_full[GROUPS // 2 :]))
        )
        pair_f = generic_gather(chunk_f)
    row_parts = rows_own, rows_side, rows_near, swap(after(rows_side, rows_gate), "head", 1)

    ids = jnp.concatenate(
        [
            mine(reading_order)[None],
            mine(box_coords) // coarse,
            jnp.arange(rows, dtype=jnp.int32)[None, None] // page_len.reshape(1, batches, 1),
        ]
    )
    ids = jnp.take(ids.reshape(4, batches, 4, own), blocks, axis=2).reshape(4, batches, rows)

    state = [dict() for _ in range(batches)]
    gate_b = gate_f = gate_last = page
    if direct():
        gate_b = part_f.part
    for batch, here in enumerate(state):
        here["ids"] = (ids[:, batch],)
        *here["saved_a"], here["head_a"] = attend(
            batch, own_heads, after(page, gate_b), row_parts, half_a, *here["ids"]
        )
        gate_b = here["head_a"]
        if direct() and batch == 0:
            part_b.step(gate_b)
            part_o.step(part_b.part)
            part_f.step(part_o.part)
            gate_b = part_b.part
        elif direct():
            part_f.step(gate_b)
            gate_last = part_f.part
    if direct():
        half_b, pair_o, pair_f = part_b.result(), part_o.result(), part_f.result()
    for batch, here in enumerate(state):
        *here["saved_b"], here["head_b"], here["out_t"], here["keep"], here["send"], norms = attend(
            batch, own_heads, after(page, gate_b, gate_last), row_parts, half_b, *here["ids"],
            final=(pair_o, here["head_a"]),
        )
        gate_b = here["head_b"]
    ff_parts = pair_f + tuple(swap(ref, "head", 1) for ref in pair_f)

    wide = struct((own, features), f32)
    low = struct((own, features), bf16)
    sums = struct((2, features), f32)
    for batch, here in enumerate(state):
        keep, near, far = scatter_rows(here["keep"], here["send"])
        here["normal"], here["scale"], hidden_low = norm_call(
            norm_one_kernel, "norm_one", (wide, struct((own, 1), f32), low),
            keep[:own], near[:own], far, tokens[0, batch], tokens[1, batch], norms,
        )
        here["h"] = hidden_low, swap(hidden_low, "head", 2)
        here["act"], here["slope"], keep, send = ff_call(forward_kernel, "forward", here["h"], ff_parts, ())
        here["out"], here["dc"], dz, here["sums_two"] = norm_call(
            norm_two_kernel, "norm_two", (low, wide, low, sums),
            keep, swap(send, "head", 2), here["normal"], grad_out[batch], norms,
        )
        here["g"] = dz, swap(dz, "head", 2)
        here["grad_pre"], keep, send = ff_call(
            backward_kernel, "backward", here["g"], ff_parts, (here["act"], here["slope"])
        )
        here["da"], da_low, here["sums_one"] = norm_call(
            norm_back_kernel, "norm_back", (wide, low, sums),
            keep, swap(send, "head", 2), here["dc"], here["normal"], here["scale"], norms,
        )
        here["a"] = gather_rows(da_low)

    def every(name):
        return [here[name] for here in state]

    ours, theirs = ff_weights(every("h"), every("g"), every("grad_pre"), every("act"))
    keep_f, send_f = fold(ours, swap(theirs, "head", 1))
    part_f = Scatter(keep_f, send_f, FAR_X)
    if direct():
        part_f.start()

    def saved_of(here, name):
        return [*here[name][:4], state[0][name][4], state[0]["out_t"]]

    def back_b(here, *gate):
        here["dproj_b"], here["dtable_b"], here["part"] = attend_back(
            own_heads, 1, after(page, *gate), here["a"], saved_of(here, "saved_b"), *here["ids"]
        )
        return here["dproj_b"]

    def back_a(here, *gate):
        here["dproj_a"], here["dtable_a"], here["keep"], here["send"] = attend_back(
            own_heads, 0, after(page, *gate), here["a"], saved_of(here, "saved_a"), *here["ids"],
            here["part"],
        )
        here["near"] = swap(here["send"], "head", 1)
        return here["dproj_a"]

    gate = back_b(state[0], part_f.send, *[here["a"][0] for here in state])
    keep_o, send_o = out_weights(
        after(page, gate),
        every("a"),
        [here[name] for here in state for name in ("head_a", "head_b")],
        [here[name] for here in state for name in ("sums_one", "sums_two")],
    )
    part_o = Scatter(keep_o, send_o, FAR_X)
    gate = (send_o,)
    if direct():
        part_o.start(part_f.send)
        part_f.step(part_o.send)
        gate += (part_f.send,)
    for here in state[1:]:
        gate = (back_b(here, *gate),)
    weights_b = attn_weights(after(page, *gate), row_parts, every("dproj_b"), every("dtable_b"), split)
    one_b, two_b = Scatter(*weights_b[:2], FAR_Z), Scatter(*weights_b[2:], FAR_X)
    gate = (weights_b[1],)
    if direct():
        two_b.start(part_f.send)
        one_b.start(two_b.send)
        part_o.step(one_b.send)
        gate = (part_o.send,)
    gate = (back_a(state[0], *gate),)
    if direct():
        part_f.step(part_o.send)
        gate += (part_f.send,)
    for here in state[1:]:
        gate = (back_a(here, *gate),)
    if direct():
        two_b.step(part_f.send)
        part_o.step(two_b.send)
        gate += (two_b.send, part_o.send)
    weights_a = attn_weights(after(page, *gate), row_parts, every("dproj_a"), every("dtable_a"), split)
    one_a, two_a = Scatter(*weights_a[:2], FAR_Z), Scatter(*weights_a[2:], FAR_X)
    if direct():
        two_a.start(two_b.send)
        one_a.start(two_a.send)
        one_b.step(one_a.send)
        two_b.step(one_b.send)
        two_a.step(two_b.send)
        one_b.step(two_a.send)
        one_a.step(one_b.send)
        two_a.step(one_a.send)
        grad_b = jnp.concatenate([one_b.result(one_a.send), two_b.result(one_a.send)], axis=1)
        dff, dout = part_f.result(one_a.send), part_o.result(one_a.send)
        one_a.step(two_a.send)
        grad_a = jnp.concatenate([one_a.result(), two_a.result()], axis=1)
        dnorms = dout[share].reshape(4, 4, -1).transpose(1, 0, 2)
        dout = dout[:share]
    else:
        inner = features // GROUPS
        dff = generic_scatter(keep_f, send_f)
        dout = generic_scatter(keep_o[:, :inner], send_o[:, :inner])
        flat = jnp.concatenate([keep_o[:, inner], send_o[:, inner].astype(f32)]).reshape(GROUPS, 4, -1)
        flat = flat.transpose(1, 0, 2).reshape(4, pages, 4, -1).transpose(1, 2, 0, 3)
        dnorms = scatter_pages(by_page(flat))
        grads = []
        for weights in (weights_a, weights_b):
            keep = jnp.concatenate(weights[::2], axis=2)
            send = jnp.concatenate(weights[1::2], axis=2)
            grads.append(generic_scatter(keep, send, 5 * half, 2 * own_heads))
        grad_a, grad_b = grads

    dnorms = jnp.take(dnorms, blocks, axis=0)
    pair = dnorms[:2] + swap(dnorms[2:], "head", 1)
    dnorms = (pair[0] + swap(pair[1], "head", 2)).reshape(2, 2, -1)

    def both_modalities(ours, theirs):
        got = swap(theirs.astype(bf16), "head", 2).astype(f32)
        return jnp.where(modality == 0, jnp.stack([ours, got]), jnp.stack([got, ours]))

    token_grads = []
    for here in state:
        total = here["keep"] + after(here["near"], weights_a[1]).astype(f32)
        token_grads.append(both_modalities(total[:own], total[own:]) + here["da"][None])

    got_b = swap(grad_b.astype(bf16), "head", 2).astype(f32)
    chunks = jnp.where(modality == 0, jnp.stack([grad_a, got_b]), jnp.stack([got_b, grad_a]))
    dattn = jnp.stack([chunks[:, :, which * half : (which + 1) * half] for which in (0, 1, 4, 2, 3)], axis=1)
    dtable = chunks[:, :, 5 * half :].reshape(2, 2, own_heads, step, 3, buckets // 2)
    dtable = dtable.transpose(0, 4, 2, 3, 1, 5).reshape(2, 3, own_heads, step, buckets)
    dout = dout.reshape(share, 2, half).transpose(1, 2, 0)
    return (
        jnp.stack([here["out"] for here in state]),
        jnp.stack(token_grads, axis=1).astype(bf16),
        dattn,
        dtable,
        both_modalities(dout[0], dout[1]),
        dnorms[0],
        dnorms[1],
        dff[:, :features].T,
        dff[:, features:],
    )


def solution(mesh):
    return jax.shard_map(
        local,
        mesh=mesh,
        in_specs=(
            P(None, None, ("page", "head"), None),
            P(None, None, ("page", "head"), None),
            P(None, None, None, "page"),
            P(None, None, "page"),
            P(None, "page"),
            P(None, None, "page", "head"),
            P(None, None, "head", "page", None),
            P(None, "head", "page"),
            P(None, ("page", "head")),
            P(None, ("page", "head")),
            P(None, ("page", "head")),
            P(("page", "head"), None),
            P(None, ("page", "head"), None),
        ),
        out_specs=(
            P(None, ("page", "head"), None),
            P(None, None, ("page", "head"), None),
            P(None, None, "page", "head"),
            P(None, None, "head", "page", None),
            P(None, "head", "page"),
            P(None, ("page", "head")),
            P(None, ("page", "head")),
            P(None, ("page", "head")),
            P(("page", "head"), None),
        ),
        check_vma=False,
    )
```

```python
import functools

import jax
import jax.numpy as jnp
from jax import lax
from jax.experimental import pallas as pl
from jax.experimental.pallas import tpu as pltpu
from jax.sharding import PartitionSpec as P

COORD = 1024
EPS = 1e-05
GROUPS = 8
SCALE = 7e+08
EXTRA = 16
f32 = jnp.float32
bf16 = jnp.bfloat16
AB = ((1,), (0,))
ABT = ((1,), (1,))
ATB = ((0,), (0,))
SMEM = pl.BlockSpec(memory_space=pltpu.SMEM)
VM = pl.BlockSpec(memory_space=pltpu.VMEM)
HBM = pl.BlockSpec(memory_space=pltpu.HBM)
PARAMS = pltpu.CompilerParams(vmem_limit_bytes=14 * 1024 * 1024)
FAR_X = (4, 2, 1)
FAR_Z = (4, 1, 2)
X_FIRST = (1, 4, 2)


def cost(microseconds):
    return pl.CostEstimate(
        flops=int(microseconds * SCALE), bytes_accessed=int(microseconds * 3e5), transcendentals=0
    )


def struct(shape, kind):
    return pltpu.VMEM(tuple(shape), kind)


def pin(*values):
    return [pltpu.with_memory_space_constraint(value, pltpu.VMEM) for value in values]


def dot(left, right, dims):
    return lax.dot_general(left, right, (dims, ((), ())), preferred_element_type=f32)


def swap(value, axis, mask):
    count = lax.axis_size(axis)
    return lax.ppermute(value, axis, [(place, place ^ mask) for place in range(count)])


def after(value, *earlier):
    return lax.optimization_barrier((value, earlier))[0]


def gather_rows(own):
    side = swap(own, "head", 2)
    return own, side, swap(own, "head", 1), swap(side, "head", 1)


def scatter_rows(keep, send):
    own = keep.shape[0] // 2
    near = swap(send, "head", 1)
    far = swap((keep[own:] + near[own:].astype(f32)).astype(bf16), "head", 2)
    return keep, near, far


def page_bits():
    count = lax.axis_size("page")
    return [1 << bit for bit in reversed(range(count.bit_length() - 1))]


def gather_pages(own):
    full = own
    for depth, mask in enumerate(page_bits()):
        full = jnp.stack([full, swap(full, "page", mask)], axis=depth)
    return full.reshape((lax.axis_size("page"),) + own.shape)


def scatter_pages(blocks):
    masks = page_bits()
    part = blocks.reshape((2,) * len(masks) + blocks.shape[1:])
    for depth in reversed(range(len(masks))):
        keep = lax.index_in_dim(part, 0, depth, keepdims=False)
        send = lax.index_in_dim(part, 1, depth, keepdims=False)
        part = keep.astype(f32) + swap(send.astype(bf16), "page", masks[depth]).astype(f32)
    return part


def by_page(blocks):
    count = blocks.shape[0]
    order = jnp.arange(count, dtype=jnp.int32) ^ lax.axis_index("page")
    return jnp.take(blocks, order, axis=0)


def regroup(full, heads):
    pages, share, columns = full.shape
    if heads == 1:
        return full.reshape(GROUPS, -1, columns)
    parts = full.reshape(GROUPS, pages // GROUPS, heads, share // heads, columns)
    return parts.transpose(0, 2, 1, 3, 4).reshape(GROUPS, -1, columns)


def ungroup(full, pages, heads):
    columns = full.shape[2]
    if heads == 1:
        return full.reshape(pages, -1, columns)
    parts = full.reshape(GROUPS, heads, pages // GROUPS, -1, columns)
    return parts.transpose(0, 2, 1, 3, 4).reshape(pages, -1, columns)


def direct():
    return lax.axis_size("page") == GROUPS


def join_kernel(first_ref, second_ref, out_ref):
    half = first_ref.shape[0]
    out_ref[:half] = first_ref[...]
    out_ref[half:] = second_ref[...]


def join(first, second):
    return pl.pallas_call(
        join_kernel,
        in_specs=[VM] * 2,
        out_shape=struct((2 * first.shape[0],) + first.shape[1:], first.dtype),
        compiler_params=PARAMS,
        cost_estimate=cost(0.4),
        name="join",
    )(*pin(first, second))


def fold_kernel(first_ref, second_ref, keep_ref, send_ref):
    half = keep_ref.shape[0]
    keep_ref[...] = first_ref[:half].astype(f32) + second_ref[:half].astype(f32)
    send_ref[...] = (first_ref[half:].astype(f32) + second_ref[half:].astype(f32)).astype(bf16)


def fold(first, second):
    half = (first.shape[0] // 2,) + first.shape[1:]
    return pl.pallas_call(
        fold_kernel,
        in_specs=[VM] * 2,
        out_shape=(struct(half, f32), struct(half, bf16)),
        compiler_params=PARAMS,
        cost_estimate=cost(0.432),
        name="fold",
    )(*pin(first, second))


class Gather:
    def __init__(self, share, masks):
        self.part, self.masks = share[None], list(masks)

    def start(self, *earlier):
        self.part = after(self.part, *earlier)
        self.got = swap(self.part, "page", self.masks.pop(0))

    def step(self, *earlier):
        self.part = join(self.part, after(self.got, *earlier))
        self.start(*earlier)

    def result(self):
        return self.part, self.got


def generic_gather(share, columns=None, heads=1):
    full = by_page(gather_pages(share))
    if heads == 1:
        full = regroup(full, 1)
    else:
        full = jnp.concatenate([regroup(full[..., :columns], 1), regroup(full[..., columns:], heads)], axis=2)
    return full[: GROUPS // 2], full[GROUPS // 2 :]


class Scatter:
    def __init__(self, keep, send, masks):
        self.keep, self.send, self.masks = keep, send, list(masks)

    def start(self, *earlier):
        self.send = after(self.send, *earlier)
        self.got = swap(self.send, "page", self.masks.pop())

    def step(self, *earlier):
        self.keep, self.send = fold(self.keep, after(self.got, *earlier))
        self.start(*earlier)

    def result(self, *earlier):
        return self.keep[0] + after(self.got, *earlier)[0].astype(f32)


def generic_scatter(keep, send, columns=None, heads=1):
    pages = lax.axis_size("page")
    full = jnp.concatenate([keep.astype(bf16), send])
    if heads == 1:
        full = ungroup(full, pages, 1)
    else:
        full = jnp.concatenate(
            [ungroup(full[..., :columns], pages, 1), ungroup(full[..., columns:], pages, heads)], axis=2
        )
    return scatter_pages(by_page(full))


def places(masks):
    if not direct():
        masks = (1, 2, 4)
    return [
        sum(mask for bit, mask in enumerate(masks) if (place >> bit) & 1) for place in range(GROUPS)
    ]


def page_of(place, page, masks):
    if not direct():
        masks = (1, 2, 4)
    for bit, mask in enumerate(masks):
        page = jnp.bitwise_xor(page, jnp.bitwise_and(lax.shift_right_logical(place, bit), 1) * mask)
    return page


def load_chunk(page, refs, masks, target, start=0):
    share = target.shape[0] // GROUPS
    stop = start + refs[0].shape[2]
    for half, ref in enumerate(refs):

        def body(place, carry):
            row = page_of(place + half * (GROUPS // 2), page, masks) * share
            target[pl.ds(pl.multiple_of(row, share), share), start:stop] = ref[place, :share]
            return carry

        lax.fori_loop(0, GROUPS // 2, body, 0)


def load_rows(refs, target, *pick):
    count = refs[0].shape[-2]
    for place, ref in enumerate(refs):
        target[place * count : (place + 1) * count] = ref[pick] if pick else ref[...]


def load_extra(page, refs, masks, target):
    share = refs[0].shape[1] - EXTRA
    for place, number in enumerate(places(masks)):
        target[jnp.bitwise_xor(page, number)] = refs[place // (GROUPS // 2)][place % (GROUPS // 2), share:]


def load_split(page, refs, target):
    if len(refs) == 2:
        load_chunk(page, refs, FAR_X, target)
    else:
        load_chunk(page, refs[:2], FAR_Z, target)
        load_chunk(page, refs[2:], FAR_X, target, refs[0].shape[2])


def turned(ids_ref):
    ids = ids_ref[...].astype(f32)
    return jnp.concatenate([ids, ids]).T


def hot_columns(ids, which, buckets):
    lane = lax.broadcasted_iota(jnp.int32, (ids.shape[0], buckets), 1).astype(f32)
    return jnp.where(ids[:, which : which + 1] == lane, 1.0, 0.0).astype(bf16)


def table_rows(head, heads, small):
    return [pl.multiple_of((side * heads + head) * small, small) for side in range(2)]


def attend_kernel(batch, heads, last, page_ref, *refs):
    parts = 2 if last else 4
    rows_refs, w_refs, refs = refs[:4], refs[4 : 4 + parts], refs[4 + parts :]
    if last:
        o_refs, other_ref, refs = refs[:2], refs[2], refs[3:]
    idr_ref, saved, head_ref, refs = refs[0], refs[1:6], refs[6], refs[7:]
    if last:
        saved += refs[:1]
        keep_ref, send_ref, norms_ref, refs = refs[1], refs[2], refs[3], refs[4:]
        wo_ref, extra_ref, refs = refs[0], refs[1], refs[2:]
    left_ref, right_ref, value_ref, prob_ref, w_ref, x_ref, s_ref, hot_ref, head_part_ref, sems = refs
    page = page_ref[0]
    load_rows(rows_refs, x_ref, 0, batch)
    load_rows(rows_refs, s_ref, 1, batch)
    load_split(page, w_refs, w_ref)
    copies = [pltpu.make_async_copy(w_ref, saved[4], sems.at[0])]
    if last:
        load_chunk(page, o_refs, X_FIRST, wo_ref)
        load_extra(page, o_refs, X_FIRST, extra_ref)
        copies.append(pltpu.make_async_copy(wo_ref, saved[5], sems.at[1]))
    rows = x_ref.shape[0]
    width = w_ref.shape[1] // 6
    share = w_ref.shape[0] // GROUPS
    size = width // heads
    buckets = 2 * width // 3
    small, wide = buckets // GROUPS, buckets // 2
    columns = turned(idr_ref)
    for which in range(3):
        hot_ref[:, which * buckets : (which + 1) * buckets] = hot_columns(columns, which, buckets)
    same = columns[:, 3:4] == idr_ref[3:4, :].astype(f32)
    first = dot(x_ref[...], w_ref[:, : 2 * width], AB).astype(bf16)
    second = dot(s_ref[...], w_ref[:, 2 * width : 4 * width], AB).astype(bf16)
    third = dot(x_ref[...], w_ref[:, 4 * width : 5 * width], AB).astype(bf16)
    for head in range(heads):
        low, high = slice(head * size, (head + 1) * size), slice(width + head * size, width + (head + 1) * size)
        left_ref[head] = jnp.concatenate([first[:, low], second[:, low]], axis=1) * bf16(0.125)
        right_ref[head] = jnp.concatenate([first[:, high], second[:, high]], axis=1)
        value_ref[head] = third[:, low]
    for at, ref in enumerate((left_ref, right_ref, value_ref)):
        copies.append(pltpu.make_async_copy(ref, saved[at], sems.at[2 + at]))
    for copy in copies:
        copy.start()

    def save_prob(head):
        return pltpu.make_async_copy(prob_ref.at[head], saved[3].at[head], sems.at[5 + head])

    def body(head, carry):
        sides = []
        for start in table_rows(head, heads, small):
            pieces = [w_ref[pl.ds(group * share + start, small), 5 * width :] for group in range(GROUPS)]
            sides.append(jnp.concatenate(pieces))
        parts = [left_ref[head]]
        for which in range(3):
            table = jnp.concatenate([side[:, which * wide : (which + 1) * wide] for side in sides], axis=1)
            parts.append(dot(hot_ref[:, which * buckets : (which + 1) * buckets], table, AB).astype(bf16))
        left = jnp.concatenate(parts, axis=1)
        right = jnp.concatenate([right_ref[head], hot_ref[...]], axis=1)
        score = jnp.where(same, dot(left, right, ABT), -1e30)
        weight = jnp.exp(score - jnp.max(score, axis=1, keepdims=True))
        prob = (weight * (1.0 / jnp.sum(weight, axis=1, keepdims=True))).astype(bf16)
        prob_ref[head] = prob
        save_prob(head).start()
        head_part_ref[head] = dot(prob, value_ref[head], AB).astype(bf16)
        return carry

    lax.fori_loop(0, heads, body, 0)
    head_ref[...] = jnp.concatenate([head_part_ref[head] for head in range(heads)], axis=1)
    if last:
        part = dot(other_ref[...], wo_ref[:, :width], ABT) + dot(head_ref[...], wo_ref[:, width:], ABT)
        keep_ref[...] = part[: rows // 2]
        send_ref[...] = part[rows // 2 :].astype(bf16)
        inner = norms_ref.shape[1] // GROUPS
        for group in range(GROUPS):
            for which in range(norms_ref.shape[0]):
                norms_ref[which : which + 1, group * inner : (group + 1) * inner] = extra_ref[
                    group, 0:1, which * inner : (which + 1) * inner
                ].astype(f32)
    for copy in copies:
        copy.wait()
    for head in range(heads):
        save_prob(head).wait()


def attend(batch, heads, page, row_parts, chunk, ids_row, final=None):
    rows = ids_row.shape[1]
    features = row_parts[0].shape[-1]
    columns = sum(ref.shape[2] for ref in chunk[::2])
    width = columns // 6
    size = width // heads
    saved = [
        ((heads, rows, 2 * size), bf16),
        ((heads, rows, 2 * size), bf16),
        ((heads, rows, size), bf16),
        ((heads, rows, rows), bf16),
        ((features, columns), bf16),
    ]
    scratch = [pltpu.VMEM(shape, kind) for shape, kind in saved]
    more = ()
    extra_outs, first_scratch = (), []
    if final is not None:
        pair_o, other = final
        more = (*pair_o, other)
        extra_outs = (
            pltpu.HBM((features, 2 * width), bf16),
            struct((rows // 2, features), f32), struct((rows // 2, features), bf16), struct((4, features), f32),
        )
        first_scratch = [pltpu.VMEM((features, 2 * width), bf16), pltpu.VMEM((GROUPS, EXTRA, 2 * width), bf16)]
    outs = tuple(pltpu.HBM(shape, kind) for shape, kind in saved) + (struct((rows, width), bf16),)
    return pl.pallas_call(
        functools.partial(attend_kernel, batch, heads, final is not None),
        in_specs=[SMEM] + [VM] * (4 + len(chunk) + len(more) + 1),
        out_specs=[HBM] * 5 + [VM] + ([] if final is None else [HBM, VM, VM, VM]),
        out_shape=outs + extra_outs,
        scratch_shapes=first_scratch + scratch + [
            pltpu.VMEM((rows, features), bf16),
            pltpu.VMEM((rows, features), bf16),
            pltpu.VMEM((rows, 2 * width), bf16),
            pltpu.VMEM((heads, rows, size), bf16),
            pltpu.SemaphoreType.DMA((5 + heads,)),
        ],
        compiler_params=PARAMS,
        cost_estimate=cost(6.3),
        name="attend",
    )(page, *pin(*row_parts, *chunk, *more, ids_row))


def attend_back_kernel(heads, half, page_ref, *refs):
    da_refs, saved, idr_ref, refs = refs[:4], refs[4:10], refs[10], refs[11:]
    if half == 0:
        other_ref, dproj_ref, dtable_ref, keep_ref, send_ref, refs = refs[0], refs[1], refs[2], refs[3], refs[4], refs[5:]
    else:
        dproj_ref, dtable_ref, part_ref, refs = refs[0], refs[1], refs[2], refs[3:]
    left_ref, right_ref, value_ref, prob_ref, w_ref, wo_ref, refs = refs[0], refs[1], refs[2], refs[3], refs[4], refs[5], refs[6:]
    da_ref, hot_ref, grad_ref, dleft_ref, dright_ref, dvalue_ref, sems = refs
    early = [
        pltpu.make_async_copy(source, target, sems.at[at])
        for at, (source, target) in enumerate(
            ((saved[5], wo_ref), (saved[2], value_ref), (saved[1], right_ref), (saved[0], left_ref))
        )
    ]
    late = pltpu.make_async_copy(saved[4], w_ref, sems.at[4])

    def fetch_prob(head):
        return pltpu.make_async_copy(saved[3].at[head], prob_ref.at[head], sems.at[5 + head])

    early[0].start()
    early[1].start()
    fetch_prob(0).start()
    early[2].start()
    early[3].start()
    for head in range(1, heads):
        fetch_prob(head).start()
    late.start()
    load_rows(da_refs, da_ref)
    rows = da_ref.shape[0]
    width = w_ref.shape[1] // 6
    size = width // heads
    buckets = 2 * width // 3
    small, wide = buckets // GROUPS, buckets // 2
    columns = turned(idr_ref)
    for which in range(3):
        hot_ref[:, which * buckets : (which + 1) * buckets] = hot_columns(columns, which, buckets)
    bucket = lax.broadcasted_iota(jnp.int32, (buckets, rows), 0)
    early[0].wait()
    grad_heads = dot(da_ref[...], wo_ref[:, half * width : (half + 1) * width], AB).astype(bf16)
    for head in range(heads):
        grad_ref[head] = grad_heads[:, head * size : (head + 1) * size]
    for copy in early[1:]:
        copy.wait()

    def body(head, carry):
        fetch_prob(head).wait()
        prob = prob_ref[head]
        grad_out = grad_ref[head]
        grad_prob = dot(grad_out, value_ref[head], ABT)
        weighted = prob.astype(f32) * grad_prob
        row_dot = jnp.sum(weighted, axis=1, keepdims=True)
        grad_score = (weighted - prob.astype(f32) * row_dot).astype(bf16)
        dvalue_ref[head] = dot(prob, grad_out, ATB).astype(bf16)
        right = jnp.concatenate([right_ref[head], hot_ref[...]], axis=1)
        spread = dot(grad_score, right, AB)
        dleft_ref[head] = (spread[:, : 2 * size] * 0.125).astype(bf16)
        dright_ref[head] = dot(grad_score, left_ref[head], ATB).astype(bf16)
        pieces = []
        for which in range(3):
            start = 2 * size + which * buckets
            hot_t = jnp.where(idr_ref[which : which + 1, :] == bucket, 1.0, 0.0).astype(bf16)
            pieces.append(dot(hot_t, spread[:, start : start + buckets].astype(bf16), AB))
        for side, start in enumerate(table_rows(head, heads, small)):
            block = jnp.concatenate([piece[:, side * wide : (side + 1) * wide] for piece in pieces], axis=1)
            for group in range(GROUPS):
                dtable_ref[group, pl.ds(start, small), :] = block[group * small : (group + 1) * small]
        return carry

    lax.fori_loop(0, heads, body, 0)
    every = range(heads)
    dproj_ref[:, :width] = jnp.concatenate([dleft_ref[head][:, :size] for head in every], axis=1)
    dproj_ref[:, width : 2 * width] = jnp.concatenate([dright_ref[head][:, :size] for head in every], axis=1)
    dproj_ref[:, 2 * width : 3 * width] = jnp.concatenate([dleft_ref[head][:, size:] for head in every], axis=1)
    dproj_ref[:, 3 * width : 4 * width] = jnp.concatenate([dright_ref[head][:, size:] for head in every], axis=1)
    dproj_ref[:, 4 * width :] = jnp.concatenate([dvalue_ref[head] for head in every], axis=1)
    late.wait()
    part = dot(dproj_ref[:, : 2 * width], w_ref[:, : 2 * width], ABT)
    part = part + dot(dproj_ref[:, 4 * width :], w_ref[:, 4 * width : 5 * width], ABT)
    if half == 0:
        part = part + other_ref[...]
        keep_ref[...] = part[: rows // 2]
        send_ref[...] = part[rows // 2 :].astype(bf16)
    else:
        part_ref[...] = part


def attend_back(heads, half, page, da_parts, saved, ids_row, other=None):
    rows = ids_row.shape[1]
    features = da_parts[0].shape[-1]
    width = saved[4].shape[1] // 6
    size = width // heads
    outs = (struct((rows, 5 * width), bf16), struct((GROUPS, features // GROUPS, width), f32))
    if half == 0:
        outs += (struct((rows // 2, features), f32), struct((rows // 2, features), bf16))
    else:
        outs += (struct((rows, features), f32),)
    return pl.pallas_call(
        functools.partial(attend_back_kernel, heads, half),
        in_specs=[SMEM] + [VM] * 4 + [HBM] * 6 + [VM] * (2 if half == 0 else 1),
        out_shape=outs,
        scratch_shapes=[pltpu.VMEM(ref.shape, ref.dtype) for ref in saved]
        + [
            pltpu.VMEM((rows, features), bf16),
            pltpu.VMEM((rows, 2 * width), bf16),
            pltpu.VMEM((heads, rows, size), bf16),
            pltpu.VMEM((heads, rows, 2 * size), bf16),
            pltpu.VMEM((heads, rows, 2 * size), bf16),
            pltpu.VMEM((heads, rows, size), bf16),
            pltpu.SemaphoreType.DMA((5 + heads,)),
        ],
        compiler_params=PARAMS,
        cost_estimate=cost(6),
        name="attend_back",
    )(page, *pin(*da_parts), *[pltpu.with_memory_space_constraint(ref, pltpu.HBM) for ref in saved], *pin(ids_row, *([other] if half == 0 else [])))


def put_blocks(page, masks, full_ref, columns, keep_ref, send_ref):
    half = GROUPS // 2

    def body(place, carry):
        keep_ref[place] = full_ref[page_of(place, page, masks), :, columns]
        send_ref[place] = full_ref[page_of(place + half, page, masks), :, columns].astype(bf16)
        return carry

    lax.fori_loop(0, half, body, 0)


def attn_weights_kernel(batches, split, page_ref, *refs):
    rows_refs, dproj_refs, dtable_refs = refs[:4], refs[4 : 4 + batches], refs[4 + batches : 4 + 2 * batches]
    out_refs, (x_ref, d_ref, full_ref) = refs[4 + 2 * batches : -3], refs[-3:]
    page = page_ref[0]
    rows = x_ref.shape[1] // batches
    for batch in range(batches):
        at = pl.ds(batch * rows, rows)
        for which in range(2):
            load_rows(rows_refs, x_ref.at[which, at], which, batch)
        d_ref[at] = dproj_refs[batch][...]
    width = d_ref.shape[1] // 5

    def blocks(value):
        return value.reshape(GROUPS, value.shape[0] // GROUPS, value.shape[1])

    x_t = x_ref[0].T
    full_ref[:, :, : 2 * width] = blocks(dot(x_t, d_ref[:, : 2 * width], AB))
    full_ref[:, :, 2 * width : 4 * width] = blocks(dot(x_ref[1].T, d_ref[:, 2 * width : 4 * width], AB))
    full_ref[:, :, 4 * width : 5 * width] = blocks(dot(x_t, d_ref[:, 4 * width :], AB))
    total = dtable_refs[0][...]
    for ref in dtable_refs[1:]:
        total = total + ref[...]
    full_ref[:, :, 5 * width :] = total
    if split:
        put_blocks(page, FAR_Z, full_ref, slice(0, split), *out_refs[:2])
    put_blocks(page, FAR_X, full_ref, slice(split, 6 * width), *out_refs[-2:])


def attn_weights(page, row_parts, dprojs, dtables, split):
    batches = len(dprojs)
    rows, columns = dprojs[0].shape
    columns = 6 * (columns // 5)
    features = row_parts[0].shape[-1]
    inner = features // GROUPS
    outs = ()
    for count in (split, columns - split) if split else (columns,):
        outs += (struct((GROUPS // 2, inner, count), f32), struct((GROUPS // 2, inner, count), bf16))
    return pl.pallas_call(
        functools.partial(attn_weights_kernel, batches, split),
        in_specs=[SMEM] + [VM] * (4 + batches) + [VM] * batches,
        out_shape=outs,
        scratch_shapes=[
            pltpu.VMEM((2, batches * rows, features), bf16),
            pltpu.VMEM((batches * rows, dprojs[0].shape[1]), bf16),
            pltpu.VMEM((GROUPS, inner, columns), f32),
        ],
        compiler_params=PARAMS,
        cost_estimate=cost(3.12),
        name="attn_weights",
    )(page, *pin(*row_parts, *dprojs, *dtables))


def out_weights_kernel(batches, page_ref, *refs):
    da_refs, head_refs, refs = refs[: 4 * batches], refs[4 * batches : 6 * batches], refs[6 * batches :]
    sums_refs, refs = refs[: 2 * batches], refs[2 * batches :]
    keep_ref, send_ref, da_ref, head_ref, full_ref = refs
    page = page_ref[0]
    rows = da_ref.shape[0] // batches
    width = head_ref.shape[2]
    for batch in range(batches):
        at = pl.ds(batch * rows, rows)
        load_rows(da_refs[4 * batch : 4 * batch + 4], da_ref.at[at])
        for half in range(2):
            head_ref[half, at] = head_refs[2 * batch + half][...]
    share = da_ref.shape[1] // GROUPS
    full_ref[:, share:, :] = jnp.zeros((GROUPS, EXTRA, 2 * width), f32)
    for layer in range(2):
        total = sums_refs[layer][...]
        for batch in range(1, batches):
            total = total + sums_refs[2 * batch + layer][...]
        for which in range(2):
            for group in range(GROUPS):
                start = (2 * which + layer) * share
                full_ref[group, share : share + 1, start : start + share] = total[
                    which : which + 1, group * share : (group + 1) * share
                ]
    da_t = da_ref[...].T
    for half in range(2):
        full_ref[:, :share, half * width : (half + 1) * width] = dot(da_t, head_ref[half], AB).reshape(
            GROUPS, share, width
        )
    put_blocks(page, FAR_X, full_ref, slice(0, 2 * width), keep_ref, send_ref)


def out_weights(page, da_parts, head_rows, sums):
    batches = len(da_parts)
    rows, width = head_rows[0].shape
    features = da_parts[0][0].shape[-1]
    chunk = (GROUPS // 2, features // GROUPS + EXTRA, 2 * width)
    return pl.pallas_call(
        functools.partial(out_weights_kernel, batches),
        in_specs=[SMEM] + [VM] * (6 * batches) + [VM] * (2 * batches),
        out_shape=(struct(chunk, f32), struct(chunk, bf16)),
        scratch_shapes=[
            pltpu.VMEM((batches * rows, features), bf16),
            pltpu.VMEM((2, batches * rows, width), bf16),
            pltpu.VMEM((GROUPS,) + chunk[1:], f32),
        ],
        compiler_params=PARAMS,
        cost_estimate=cost(2.7),
        name="out_weights",
    )(page, *pin(*[ref for parts in da_parts for ref in parts], *head_rows, *sums))


def hidden_weights(refs):
    return jnp.concatenate([ref[...].reshape(-1, ref.shape[2]) for ref in refs])


def forward_kernel(own_ref, side_ref, *refs):
    f_refs, (act_ref, slope_ref, keep_ref, send_ref) = refs[:4], refs[4:]
    own, features = own_ref.shape
    rows = jnp.concatenate([own_ref[...], side_ref[...]])
    weight = hidden_weights(f_refs)
    pre = dot(rows, weight[:, :features], ABT)
    normal = 0.5 + 0.5 * lax.erf(pre * 0.7071067811865476)
    act = (pre * normal).astype(bf16)
    act_ref[...] = act
    slope_ref[...] = (normal + pre * jnp.exp(-0.5 * pre * pre) * 0.3989422804014327).astype(bf16)
    part = dot(act, weight[:, features:], AB)
    keep_ref[...] = part[:own]
    send_ref[...] = part[own:].astype(bf16)


def backward_kernel(own_ref, side_ref, *refs):
    f_refs, (act_ref, slope_ref, pre_ref, keep_ref, send_ref) = refs[:4], refs[4:]
    own, features = own_ref.shape
    rows = jnp.concatenate([own_ref[...], side_ref[...]])
    weight = hidden_weights(f_refs)
    grad_act = dot(rows, weight[:, features:], ABT)
    grad_pre = (grad_act * slope_ref[...].astype(f32)).astype(bf16)
    pre_ref[...] = grad_pre
    part = dot(grad_pre, weight[:, :features], AB)
    keep_ref[...] = part[:own]
    send_ref[...] = part[own:].astype(bf16)


def ff_call(kernel, name, parts, weights, saved):
    own, features = parts[0].shape
    hidden = sum(ref.shape[0] * ref.shape[1] for ref in weights)
    outs = (struct((2 * own, hidden), bf16),) * (1 if saved else 2)
    return pl.pallas_call(
        kernel,
        in_specs=[VM] * (6 + len(saved)),
        out_shape=outs + (struct((own, features), f32), struct((own, features), bf16)),
        compiler_params=PARAMS,
        cost_estimate=cost(1.17),
        name=name,
    )(*pin(*parts, *weights, *saved))


def ff_weights_kernel(batches, *refs):
    h_refs, g_refs = refs[: 2 * batches], refs[2 * batches : 4 * batches]
    pre_refs, act_refs = refs[4 * batches : 5 * batches], refs[5 * batches : 6 * batches]
    ours_ref, theirs_ref = refs[6 * batches :]
    features = ours_ref.shape[2]
    features = features // 2
    half = GROUPS * ours_ref.shape[1]
    shape = ours_ref.shape[:2] + (features,)
    for left_refs, right_refs, at in ((pre_refs, h_refs, 0), (act_refs, g_refs, features)):
        left = jnp.concatenate([ref[...] for ref in left_refs])
        right = jnp.concatenate([ref[...] for ref in right_refs])
        total = dot(left, right, ATB).astype(bf16)
        ours_ref[:, :, at : at + features] = total[:half].reshape(shape)
        theirs_ref[:, :, at : at + features] = total[half:].reshape(shape)


def ff_weights(h_parts, g_parts, grad_pres, acts):
    batches = len(acts)
    hidden = acts[0].shape[1]
    features = h_parts[0][0].shape[1]
    chunk = (GROUPS, hidden // (2 * GROUPS), 2 * features)
    return pl.pallas_call(
        functools.partial(ff_weights_kernel, batches),
        in_specs=[VM] * (6 * batches),
        out_shape=(struct(chunk, bf16), struct(chunk, bf16)),
        compiler_params=PARAMS,
        cost_estimate=cost(3.36),
        name="ff_weights",
    )(*pin(*[ref for parts in h_parts + g_parts for ref in parts], *grad_pres, *acts))


def normalize(value):
    centred = value - jnp.mean(value, axis=1, keepdims=True)
    scale = lax.rsqrt(jnp.mean(centred * centred, axis=1, keepdims=True) + EPS)
    return centred * scale, scale


def normalize_back(grad, normal, scale, gain):
    inner = grad * gain
    inner = inner - jnp.mean(inner, axis=1, keepdims=True) - normal * jnp.mean(inner * normal, axis=1, keepdims=True)
    return inner * scale


def norm_sums(grad, normal):
    gain = jnp.sum(grad * normal, axis=0, keepdims=True)
    shift = jnp.sum(grad, axis=0, keepdims=True)
    return jnp.concatenate([gain, shift], axis=0)


def norm_one_kernel(keep_ref, near_ref, far_ref, first_ref, second_ref, norms_ref, normal_ref, scale_ref, low_ref):
    value = first_ref[...].astype(f32) + second_ref[...].astype(f32)
    value = value + (keep_ref[...] + near_ref[...].astype(f32) + far_ref[...].astype(f32))
    normal, scale = normalize(value)
    normal_ref[...] = normal
    scale_ref[...] = scale
    low_ref[...] = (normal * norms_ref[0:1] + norms_ref[2:3]).astype(bf16)


def norm_two_kernel(keep_ref, far_ref, normal_ref, grad_ref, norms_ref, out_ref, dc_ref, dz_ref, sums_ref):
    value = normal_ref[...] * norms_ref[0:1] + norms_ref[2:3]
    value = value + (keep_ref[...] + far_ref[...].astype(f32))
    normal, scale = normalize(value)
    out_ref[...] = (normal * norms_ref[1:2] + norms_ref[3:4]).astype(bf16)
    grad = grad_ref[...].astype(f32)
    dc = normalize_back(grad, normal, scale, norms_ref[1:2])
    dc_ref[...] = dc
    dz_ref[...] = dc.astype(bf16)
    sums_ref[...] = norm_sums(grad, normal)


def norm_back_kernel(keep_ref, far_ref, dc_ref, normal_ref, scale_ref, norms_ref, da_ref, low_ref, sums_ref):
    grad = dc_ref[...] + (keep_ref[...] + far_ref[...].astype(f32))
    normal = normal_ref[...]
    da = normalize_back(grad, normal, scale_ref[...], norms_ref[0:1])
    da_ref[...] = da
    low_ref[...] = da.astype(bf16)
    sums_ref[...] = norm_sums(grad, normal)


def norm_call(kernel, name, outs, *args):
    return pl.pallas_call(kernel, in_specs=[VM] * len(args), out_shape=outs, compiler_params=PARAMS, cost_estimate=cost(0.75), name=name)(*pin(*args))


def local(
    tokens,
    spatial,
    box_coords,
    reading_order,
    page_len,
    w_attn,
    tables,
    w_out,
    ln_gain,
    ln_shift,
    w_up,
    w_down,
    grad_out,
):
    batches, own, features = tokens.shape[1:]
    rows = box_coords.shape[3]
    buckets = tables.shape[4]
    own_heads = tables.shape[2]
    heads = 2 * own_heads
    half = w_attn.shape[3]
    width = 2 * half
    share = w_attn.shape[2]
    step = tables.shape[3]
    coarse = COORD // buckets
    head_index = lax.axis_index("head")
    modality = head_index // 2
    pages = lax.axis_size("page")
    page_index = lax.axis_index("page")
    page = (page_index if direct() else page_index * 0).astype(jnp.int32).reshape(1)

    def mine(value):
        return lax.dynamic_index_in_dim(value, modality, 0, keepdims=False)

    def other(value):
        return lax.dynamic_index_in_dim(value, 1 - modality, 0, keepdims=False)

    def split_table(value):
        pieces = value.reshape(3, own_heads, step, 2, buckets // 2).transpose(3, 1, 2, 0, 4)
        return pieces.reshape(share, half)

    split = 5 * features // 6
    turns = jnp.array([0, 2, 1, 3], jnp.int32)
    blocks = turns ^ head_index
    slots = jnp.take(turns, jnp.arange(4, dtype=jnp.int32) ^ head_index)
    sequence = (0, 1, 3, 4, 2)
    attn_own = mine(w_attn)
    chunk_a = jnp.concatenate([attn_own[which] for which in sequence], axis=1)
    one_a = Gather(chunk_a[:, :split], FAR_Z)
    if direct():
        one_a.start()
    first = one_a.part
    attn_send = other(after(w_attn, first))
    attn_got = swap(attn_send, "head", 2)
    table_own = split_table(mine(after(tables, attn_send)))
    two_a = Gather(jnp.concatenate([chunk_a[:, split:], table_own], axis=1), FAR_X)
    if direct():
        two_a.start()
    table_got = swap(other(after(tables, two_a.part)), "head", 2)
    out_got = swap(other(after(w_out, two_a.part)), "head", 2)
    norms_own = after(jnp.stack([ln_gain, ln_shift]), two_a.part)
    norms_four = gather_rows(norms_own)
    if direct():
        one_a.step(two_a.part)
        out_got, norms_four = after((out_got, norms_four), one_a.part)
    else:
        chunk_a = jnp.concatenate([chunk_a, table_own], axis=1)
    norms_head = jnp.take(jnp.stack(norms_four), slots, axis=0)
    chunk_o = jnp.concatenate([mine(w_out), out_got]).T
    gate, rows_gate = (norms_head,), norms_head
    if direct():
        norms_row = norms_head.transpose(1, 2, 0, 3).reshape(1, -1)
        chunk_o = jnp.concatenate([chunk_o, jnp.pad(norms_row, ((0, EXTRA - 1), (0, 0)))])
        part_o = Gather(chunk_o, X_FIRST)
        two_a.step(one_a.part)
        part_o.start(two_a.part)
        gate = (part_o.part,)
    tokens_late, spatial_late = after((tokens, spatial), first)
    rows_own = jnp.stack([mine(tokens_late), mine(spatial_late)])
    rows_side = swap(after(jnp.stack([other(tokens_late), other(spatial_late)]), *gate), "head", 2)
    rows_near = swap(after(rows_own, *gate), "head", 1)
    attn_got, table_got = after((attn_got, table_got), *gate)
    chunk_b = jnp.concatenate([attn_got[which] for which in sequence] + [split_table(table_got)], axis=1)
    chunk_f = jnp.concatenate([w_up.T, w_down], axis=1)
    part_b = Gather(chunk_b, FAR_X)
    if direct():
        part_f = Gather(chunk_f, FAR_X)
        part_b.start()
        one_a.step(part_b.part)
        two_a.step(one_a.part)
        part_b.step(two_a.part)
        part_o.step(part_b.part)
        rows_gate = part_b.part
        part_f.start(part_b.part, one_a.got, two_a.got)
        half_a = one_a.result() + two_a.result()
    else:
        half_a = generic_gather(chunk_a, 5 * half, 2 * own_heads)
        half_a = tuple(ref[..., :split] for ref in half_a) + tuple(ref[..., split:] for ref in half_a)
        half_b = generic_gather(chunk_b, 5 * half, 2 * own_heads)
        norms_full = by_page(gather_pages(norms_head)).transpose(2, 3, 0, 1, 4).reshape(4, GROUPS, 1, -1)
        norms_full = norms_full.transpose(1, 2, 0, 3).reshape(GROUPS, 1, -1)
        norms_full = jnp.pad(norms_full, ((0, 0), (0, EXTRA - 1), (0, 0)))
        pair_o = generic_gather(chunk_o)
        pair_o = tuple(
            jnp.concatenate([ref, extra], axis=1)
            for ref, extra in zip(pair_o, (norms_full[: GROUPS // 2], norms_full[GROUPS // 2 :]))
        )
        pair_f = generic_gather(chunk_f)
    row_parts = rows_own, rows_side, rows_near, swap(after(rows_side, rows_gate), "head", 1)

    ids = jnp.concatenate(
        [
            mine(reading_order)[None],
            mine(box_coords) // coarse,
            jnp.arange(rows, dtype=jnp.int32)[None, None] // page_len.reshape(1, batches, 1),
        ]
    )
    ids = jnp.take(ids.reshape(4, batches, 4, own), blocks, axis=2).reshape(4, batches, rows)

    state = [dict() for _ in range(batches)]
    gate_b = gate_f = gate_last = page
    if direct():
        gate_b = part_f.part
    for batch, here in enumerate(state):
        here["ids"] = (ids[:, batch],)
        *here["saved_a"], here["head_a"] = attend(
            batch, own_heads, after(page, gate_b), row_parts, half_a, *here["ids"]
        )
        gate_b = here["head_a"]
        if direct() and batch == 0:
            part_b.step(gate_b)
            part_o.step(part_b.part)
            part_f.step(part_o.part)
            gate_b = part_b.part
        elif direct():
            part_f.step(gate_b)
            gate_last = part_f.part
    if direct():
        half_b, pair_o, pair_f = part_b.result(), part_o.result(), part_f.result()
    for batch, here in enumerate(state):
        *here["saved_b"], here["head_b"], here["out_t"], here["keep"], here["send"], norms = attend(
            batch, own_heads, after(page, gate_b, gate_last), row_parts, half_b, *here["ids"],
            final=(pair_o, here["head_a"]),
        )
        gate_b = here["head_b"]
    ff_parts = pair_f + tuple(swap(ref, "head", 1) for ref in pair_f)

    wide = struct((own, features), f32)
    low = struct((own, features), bf16)
    sums = struct((2, features), f32)
    for batch, here in enumerate(state):
        keep, near, far = scatter_rows(here["keep"], here["send"])
        here["normal"], here["scale"], hidden_low = norm_call(
            norm_one_kernel, "norm_one", (wide, struct((own, 1), f32), low),
            keep[:own], near[:own], far, tokens[0, batch], tokens[1, batch], norms,
        )
        here["h"] = hidden_low, swap(hidden_low, "head", 2)
        here["act"], here["slope"], keep, send = ff_call(forward_kernel, "forward", here["h"], ff_parts, ())
        here["out"], here["dc"], dz, here["sums_two"] = norm_call(
            norm_two_kernel, "norm_two", (low, wide, low, sums),
            keep, swap(send, "head", 2), here["normal"], grad_out[batch], norms,
        )
        here["g"] = dz, swap(dz, "head", 2)
        here["grad_pre"], keep, send = ff_call(
            backward_kernel, "backward", here["g"], ff_parts, (here["act"], here["slope"])
        )
        here["da"], da_low, here["sums_one"] = norm_call(
            norm_back_kernel, "norm_back", (wide, low, sums),
            keep, swap(send, "head", 2), here["dc"], here["normal"], here["scale"], norms,
        )
        here["a"] = gather_rows(da_low)

    def every(name):
        return [here[name] for here in state]

    ours, theirs = ff_weights(every("h"), every("g"), every("grad_pre"), every("act"))
    keep_f, send_f = fold(ours, swap(theirs, "head", 1))
    part_f = Scatter(keep_f, send_f, FAR_X)
    if direct():
        part_f.start()

    def saved_of(here, name):
        return [*here[name][:4], state[0][name][4], state[0]["out_t"]]

    def back_b(here, *gate):
        here["dproj_b"], here["dtable_b"], here["part"] = attend_back(
            own_heads, 1, after(page, *gate), here["a"], saved_of(here, "saved_b"), *here["ids"]
        )
        return here["dproj_b"]

    def back_a(here, *gate):
        here["dproj_a"], here["dtable_a"], here["keep"], here["send"] = attend_back(
            own_heads, 0, after(page, *gate), here["a"], saved_of(here, "saved_a"), *here["ids"],
            here["part"],
        )
        here["near"] = swap(here["send"], "head", 1)
        return here["dproj_a"]

    gate = back_b(state[0], part_f.send, *[here["a"][0] for here in state])
    keep_o, send_o = out_weights(
        after(page, gate),
        every("a"),
        [here[name] for here in state for name in ("head_a", "head_b")],
        [here[name] for here in state for name in ("sums_one", "sums_two")],
    )
    part_o = Scatter(keep_o, send_o, FAR_X)
    gate = (send_o,)
    if direct():
        part_o.start(part_f.send)
        part_f.step(part_o.send)
        gate += (part_f.send,)
    for here in state[1:]:
        gate = (back_b(here, *gate),)
    weights_b = attn_weights(after(page, *gate), row_parts, every("dproj_b"), every("dtable_b"), split)
    one_b, two_b = Scatter(*weights_b[:2], FAR_Z), Scatter(*weights_b[2:], FAR_X)
    gate = (weights_b[1],)
    if direct():
        two_b.start(part_f.send)
        one_b.start(two_b.send)
        part_o.step(one_b.send)
        gate = (part_o.send,)
    gate = (back_a(state[0], *gate),)
    if direct():
        part_f.step(part_o.send)
        gate += (part_f.send,)
    for here in state[1:]:
        gate = (back_a(here, *gate),)
    if direct():
        two_b.step(part_f.send)
        part_o.step(two_b.send)
        gate += (two_b.send, part_o.send)
    weights_a = attn_weights(after(page, *gate), row_parts, every("dproj_a"), every("dtable_a"), split)
    one_a, two_a = Scatter(*weights_a[:2], FAR_Z), Scatter(*weights_a[2:], FAR_X)
    if direct():
        two_a.start(two_b.send)
        one_a.start(two_a.send)
        one_b.step(one_a.send)
        two_b.step(one_b.send)
        two_a.step(two_b.send)
        one_b.step(two_a.send)
        one_a.step(one_b.send)
        two_a.step(one_a.send)
        grad_b = jnp.concatenate([one_b.result(one_a.send), two_b.result(one_a.send)], axis=1)
        dff, dout = part_f.result(one_a.send), part_o.result(one_a.send)
        one_a.step(two_a.send)
        grad_a = jnp.concatenate([one_a.result(), two_a.result()], axis=1)
        dnorms = dout[share].reshape(4, 4, -1).transpose(1, 0, 2)
        dout = dout[:share]
    else:
        inner = features // GROUPS
        dff = generic_scatter(keep_f, send_f)
        dout = generic_scatter(keep_o[:, :inner], send_o[:, :inner])
        flat = jnp.concatenate([keep_o[:, inner], send_o[:, inner].astype(f32)]).reshape(GROUPS, 4, -1)
        flat = flat.transpose(1, 0, 2).reshape(4, pages, 4, -1).transpose(1, 2, 0, 3)
        dnorms = scatter_pages(by_page(flat))
        grads = []
        for weights in (weights_a, weights_b):
            keep = jnp.concatenate(weights[::2], axis=2)
            send = jnp.concatenate(weights[1::2], axis=2)
            grads.append(generic_scatter(keep, send, 5 * half, 2 * own_heads))
        grad_a, grad_b = grads

    dnorms = jnp.take(dnorms, blocks, axis=0)
    pair = dnorms[:2] + swap(dnorms[2:], "head", 1)
    dnorms = (pair[0] + swap(pair[1], "head", 2)).reshape(2, 2, -1)

    def both_modalities(ours, theirs):
        got = swap(theirs.astype(bf16), "head", 2).astype(f32)
        return jnp.where(modality == 0, jnp.stack([ours, got]), jnp.stack([got, ours]))

    token_grads = []
    for here in state:
        total = here["keep"] + after(here["near"], weights_a[1]).astype(f32)
        token_grads.append(both_modalities(total[:own], total[own:]) + here["da"][None])

    got_b = swap(grad_b.astype(bf16), "head", 2).astype(f32)
    chunks = jnp.where(modality == 0, jnp.stack([grad_a, got_b]), jnp.stack([got_b, grad_a]))
    dattn = jnp.stack([chunks[:, :, which * half : (which + 1) * half] for which in (0, 1, 4, 2, 3)], axis=1)
    dtable = chunks[:, :, 5 * half :].reshape(2, 2, own_heads, step, 3, buckets // 2)
    dtable = dtable.transpose(0, 4, 2, 3, 1, 5).reshape(2, 3, own_heads, step, buckets)
    dout = dout.reshape(share, 2, half).transpose(1, 2, 0)
    return (
        jnp.stack([here["out"] for here in state]),
        jnp.stack(token_grads, axis=1).astype(bf16),
        dattn,
        dtable,
        both_modalities(dout[0], dout[1]),
        dnorms[0],
        dnorms[1],
        dff[:, :features].T,
        dff[:, features:],
    )


def solution(mesh):
    return jax.shard_map(
        local,
        mesh=mesh,
        in_specs=(
            P(None, None, ("page", "head"), None),
            P(None, None, ("page", "head"), None),
            P(None, None, None, "page"),
            P(None, None, "page"),
            P(None, "page"),
            P(None, None, "page", "head"),
            P(None, None, "head", "page", None),
            P(None, "head", "page"),
            P(None, ("page", "head")),
            P(None, ("page", "head")),
            P(None, ("page", "head")),
            P(("page", "head"), None),
            P(None, ("page", "head"), None),
        ),
        out_specs=(
            P(None, ("page", "head"), None),
            P(None, None, ("page", "head"), None),
            P(None, None, "page", "head"),
            P(None, None, "head", "page", None),
            P(None, "head", "page"),
            P(None, ("page", "head")),
            P(None, ("page", "head")),
            P(None, ("page", "head")),
            P(("page", "head"), None),
        ),
        check_vma=False,
    )
```
